32 devices in a mesh: blk: 2 (over y), tm: 4 (over z), fsdp: 4 (over x, core).
Axes of the slice: x: 2, y: 2, z: 4, core: 2. Of those that a mesh axis runs over, the one named last changes fastest.
Arguments:
- features: bfloat16 [4, 4, 320, 512], P('fsdp', 'tm', 'blk'), may hold values from -6 to 6
- neighbours: int32 [320, 8], P('blk'), may hold values from 0 to 319, as said below
- conv_taps: float32 [9, 512], replicated, may hold values from -3 to 3
- norm_gain: float32 [512], replicated, may hold values from 0.25 to 1.75
- qkv_weight: bfloat16 [512, 1536], P('fsdp'), as said below
- out_weight: bfloat16 [512, 512], P('fsdp'), may hold values from -0.25 to 0.25
- cotangent: bfloat16 [4, 4, 320, 512], P('fsdp', 'tm', 'blk'), may hold values from -0.083496094 to 0.083496094
Outputs:
- weight_grads: float32 [1048576], P(('blk', 'tm', 'fsdp'))
The draws below stay inside these ranges and needn't reach their ends.
Inputs may be any that keep to these rules, and one draw needn't show every extreme that they name: `neighbours`: row p holds p - 1, p + 1, three neighbouring pixels near p - 128 and three near p + 128, clipped to the window; every entry lies within 130 of p, and one lies exactly 130 away. `qkv_weight`: projection weights of order 512 ** -0.5 per entry.
All inputs are finite; a program needn't handle non-finite values.
Results may differ from the reference program's by a relative error of at most 0.0086.
Values may be sent and summed in bfloat16 or wider, within the bound.
No kernel may reach another device: no remote copies, remote signals or barrier semaphores. Data moves between devices by JAX's collectives and lax.ppermute only.
A program may use at most 64 MiB of HBM per device.

```python
import jax
import jax.numpy as jnp
from jax import lax

C = 512
HEADS = 8
CYCLE = 128
PIX = 320
FRAMES = 4
SAMPLES = 4
ROWS = 5120


def draw_neighbours(key, part):
    jitter = jax.random.randint(key, (PIX, 2), -1, 2).astype(jnp.int32)
    jitter = jitter.at[0, 1].set(1)
    pixel_ids = jnp.arange(PIX, dtype=jnp.int32)[:, None]
    offsets = jnp.array([-1, 1, -CYCLE - 1, -CYCLE, -CYCLE + 1, CYCLE - 1, CYCLE, CYCLE + 1], dtype=jnp.int32)[None, :]
    extra = jnp.concatenate([jnp.zeros((PIX, 2), jnp.int32), jnp.repeat(jitter[:, 0:1], 3, axis=1), jnp.repeat(jitter[:, 1:2], 3, axis=1)], axis=1)
    return jnp.clip(pixel_ids + offsets + extra, 0, PIX - 1).astype(jnp.int32)


def draw_qkv_weight(key, part):
    base = jax.random.normal(key, (C, 3 * C), jnp.float32) * C ** (-0.5)
    return base.astype(jnp.bfloat16)


def levels(own_key, dims, shards, smallest, top_value):
    factor_of = 1.0
    for dim, shards_of in shards:
        draws = jax.random.uniform(jax.random.fold_in(jax.random.fold_in(own_key, 6), dim), (shards_of,), jnp.float32, smallest / len(shards), top_value / len(shards))
        factor_of = factor_of * jnp.repeat(jnp.exp(draws), dims[dim] // shards_of).reshape((-1,) + (1,) * (len(dims) - 1 - dim))
    return factor_of


def normal_values(stream_key, extent, scale, most, cuts=(), held_as=jnp.bfloat16):
    factor_of = levels(stream_key, extent, cuts, -0.22, 0.18) if cuts else 1.0
    values = jax.random.normal(stream_key, extent, jnp.float32) * scale * factor_of
    return jnp.minimum(jnp.maximum(values, -most), most).astype(held_as)


def setup_inputs(seed: int = 0) -> dict:
    key_of = jax.random.split(jax.random.key(seed), 8)
    features = normal_values(key_of[0], (SAMPLES, FRAMES, PIX, C), 1.0, 6.0, ((0, 4), (1, 4), (2, 2)))
    neighbours = draw_neighbours(jax.random.fold_in(key_of[7], 71), 0)
    conv_taps = normal_values(key_of[2], (9, C), 0.35, 3.0, (), jnp.float32)
    norm_gain = jnp.clip(1.0 + 0.15 * jax.random.normal(key_of[3], (C,), jnp.float32), 0.25, 1.75)
    qkv_weight = draw_qkv_weight(jax.random.fold_in(key_of[7], 71), 0)
    out_weight = normal_values(key_of[5], (C, C), C ** -0.5, 0.25, ((0, 4),))
    cotangent = normal_values(key_of[6], (SAMPLES, FRAMES, PIX, C), (1.0 / ROWS ** 0.5), 0.083496094, ((0, 4), (1, 4), (2, 2)))
    return dict(features=features, neighbours=neighbours, conv_taps=conv_taps, norm_gain=norm_gain, qkv_weight=qkv_weight, out_weight=out_weight, cotangent=cotangent)


def rounded(values):
    return lax.optimization_barrier(values.astype(jnp.bfloat16)).astype(jnp.float32)

def attend_rows(qkv_rows, grad_rows):
    frames, pixels, width = qkv_rows.shape
    channels = width // 3

    def split_heads(block):
        return block.reshape(frames, pixels, HEADS, channels // HEADS).astype(jnp.float32)
    queries = split_heads(qkv_rows[:, :, :channels])
    keys_all = split_heads(qkv_rows[:, :, channels:2 * channels])
    values = split_heads(qkv_rows[:, :, 2 * channels:])
    grads = split_heads(grad_rows)
    scores = jnp.einsum('tpeh,upeh->petu', queries, keys_all) * 0.125
    causal = jnp.arange(frames)[:, None] >= jnp.arange(frames)[None, :]
    masked = jnp.where(causal, scores, -1e+30)
    largest = lax.optimization_barrier(jnp.max(masked, axis=-1, keepdims=True))
    totals = lax.optimization_barrier(jnp.sum(jnp.exp(masked - largest), axis=-1, keepdims=True))
    log_total = largest + jnp.log(totals)
    weights = rounded(jnp.exp(masked - log_total))
    attended = jnp.einsum('petu,upeh->tpeh', weights, values)
    dprob = jnp.einsum('tpeh,upeh->petu', grads, values)
    delta = lax.optimization_barrier(jnp.sum(weights * dprob, axis=-1, keepdims=True))
    dscore = rounded(weights * (dprob - delta) * 0.125)
    grad_query = jnp.einsum('petu,upeh->tpeh', dscore, keys_all)
    grad_key = jnp.einsum('petu,tpeh->upeh', dscore, queries)
    grad_value = jnp.einsum('petu,tpeh->upeh', weights, grads)
    joined = jnp.concatenate([part.reshape(frames, pixels, channels) for part in (grad_query, grad_key, grad_value)], axis=-1)
    return (attended.reshape(frames, pixels, channels).astype(jnp.bfloat16), joined.astype(jnp.bfloat16))

def sample_pass(pair):
    return attend_rows(pair[0], pair[1])

def reference(features, neighbours, conv_taps, norm_gain, qkv_weight, out_weight, cotangent):
    channels = features.shape[-1]
    inputs = features.astype(jnp.float32)
    spatial = conv_taps[0] * inputs
    for column in range(8):
        spatial = spatial + conv_taps[column + 1] * jnp.take(inputs, neighbours[:, column], axis=2)
    hidden_f = rounded(inputs + spatial)
    inverse = lax.rsqrt(lax.optimization_barrier(jnp.mean(hidden_f * hidden_f, axis=-1, keepdims=True)) + 1e-05)
    normed = (hidden_f * inverse * norm_gain).astype(jnp.bfloat16)
    flat_normed = normed.reshape(-1, channels)
    projected = jnp.dot(flat_normed, qkv_weight, preferred_element_type=jnp.float32).astype(jnp.bfloat16)
    projected = projected.reshape(features.shape[:3] + (3 * channels,))
    flat_cot = cotangent.reshape(-1, channels)
    att_grads = jnp.dot(flat_cot, out_weight.T, preferred_element_type=jnp.float32).astype(jnp.bfloat16)
    att_grads = att_grads.reshape(features.shape)
    attended, dqkv = lax.map(sample_pass, (projected, att_grads))
    grad_in = jnp.dot(flat_normed.T, dqkv.reshape(-1, 3 * channels), preferred_element_type=jnp.float32)
    grad_out = jnp.dot(attended.reshape(-1, channels).T, flat_cot, preferred_element_type=jnp.float32)
    return jnp.concatenate([grad_in.reshape(-1), grad_out.reshape(-1)])
```

```python
import jax
import jax.numpy as jnp
from jax import lax
from jax.sharding import PartitionSpec as P

HEADS = 8
HALO = 130


def with_halo(cells, sides, width):
    for axis, dim in sides:
        count = lax.axis_size(axis)
        ends = count - 1
        head = lax.slice_in_dim(cells, 0, width, axis=dim)
        tail = lax.slice_in_dim(cells, cells.shape[dim] - width, cells.shape[dim], axis=dim)
        cells = jnp.concatenate(
            [
                lax.ppermute(tail, axis, [(i, (i + 1) % count) for i in range(ends)]),
                cells,
                lax.ppermute(head, axis, [((i + 1) % count, i) for i in range(ends)]),
            ],
            axis=dim,
        )
    return cells


def halved(partial, axis, bit):
    count = lax.axis_size(axis)
    mine = (lax.axis_index(axis) >> bit) & 1
    keep = lax.dynamic_index_in_dim(partial, mine, 0, keepdims=False)
    send = lax.dynamic_index_in_dim(partial, 1 - mine, 0, keepdims=False)
    got = lax.ppermute(send.astype(jnp.bfloat16), axis, [(i, i ^ (1 << bit)) for i in range(count)])
    return keep + got.astype(jnp.float32)


def scattered_sum(summands):
    counts = [lax.axis_size(axis) for axis in ("blk", "tm", "fsdp")]
    bits = [count.bit_length() - 1 for count in counts]
    order = [("fsdp", bit) for bit in range(bits[2])]
    order += [("blk", bit) for bit in range(bits[0])]
    order += [("tm", bit) for bit in range(bits[1])]
    labels = [(axis, bit) for axis, many in zip(("blk", "tm", "fsdp"), bits) for bit in reversed(range(many))]
    partial = summands.reshape((2,) * len(labels) + (-1, 128))
    for axis, bit in order:
        place = labels.index((axis, bit))
        labels.pop(place)
        partial = halved(jnp.moveaxis(partial, place, 0), axis, bit)
    return partial.reshape(-1)


def rounded(values):
    return lax.optimization_barrier(values.astype(jnp.bfloat16)).astype(jnp.float32)


def attend_all(qkv_rows, grad_rows):
    frames, pixels, width = qkv_rows.shape
    channels = width // 3

    def split_heads(block):
        return block.reshape(frames, pixels, HEADS, channels // HEADS).astype(jnp.float32)

    queries = split_heads(qkv_rows[:, :, :channels])
    keys_all = split_heads(qkv_rows[:, :, channels : 2 * channels])
    values = split_heads(qkv_rows[:, :, 2 * channels :])
    grads = split_heads(grad_rows)
    scores = jnp.einsum("tpeh,upeh->petu", queries, keys_all) * 0.125
    causal = jnp.arange(frames)[:, None] >= jnp.arange(frames)[None, :]
    masked = jnp.where(causal, scores, -1e30)
    largest = jnp.max(masked, axis=-1, keepdims=True)
    totals = jnp.sum(jnp.exp(masked - largest), axis=-1, keepdims=True)
    log_total = largest + jnp.log(totals)
    weights = rounded(jnp.exp(masked - log_total))
    attended = jnp.einsum("petu,upeh->tpeh", weights, values)
    dprob = jnp.einsum("tpeh,upeh->petu", grads, values)
    delta = jnp.sum(weights * dprob, axis=-1, keepdims=True)
    dscore = rounded(weights * (dprob - delta) * 0.125)
    grad_query = jnp.einsum("petu,upeh->tpeh", dscore, keys_all)
    grad_key = jnp.einsum("petu,tpeh->upeh", dscore, queries)
    grad_value = jnp.einsum("petu,tpeh->upeh", weights, grads)
    joined = jnp.concatenate(
        [part.reshape(frames, pixels, channels) for part in (grad_query, grad_key, grad_value)],
        axis=-1,
    )
    return (
        attended.reshape(frames, pixels, channels).astype(jnp.bfloat16),
        joined.astype(jnp.bfloat16),
    )


def per_device(features, neighbours, conv_taps, norm_gain, qkv_weight, out_weight, cotangent):
    inputs = features[0, 0]
    upstream = cotangent[0, 0]
    pixels, channels = inputs.shape
    padded = with_halo(inputs, (("blk", 0),), HALO)
    first_pixel = lax.axis_index("blk") * pixels
    local_rows = neighbours - first_pixel + HALO
    inputs_f = inputs.astype(jnp.float32)
    spatial = conv_taps[0] * inputs_f
    for column in range(8):
        spatial = spatial + conv_taps[column + 1] * jnp.take(
            padded, local_rows[:, column], axis=0
        ).astype(jnp.float32)
    hidden_f = rounded(inputs_f + spatial)
    inverse = lax.rsqrt(jnp.mean(hidden_f * hidden_f, axis=-1, keepdims=True) + 1e-05)
    normed = (hidden_f * inverse * norm_gain).astype(jnp.bfloat16)
    full_qkv, full_out = (
        lax.all_gather(qkv_weight, "fsdp", axis=0, tiled=True),
        lax.all_gather(out_weight, "fsdp", axis=0, tiled=True),
    )
    att_grads = jnp.dot(upstream, full_out.T, preferred_element_type=jnp.float32).astype(
        jnp.bfloat16
    )
    swap_normed, swap_grads, swap_upstream = (
        lax.all_to_all(normed[None], "tm", split_axis=1, concat_axis=0, tiled=True),
        lax.all_to_all(att_grads[None], "tm", split_axis=1, concat_axis=0, tiled=True),
        lax.all_to_all(upstream[None], "tm", split_axis=1, concat_axis=0, tiled=True),
    )
    frames = swap_normed.shape[0]
    few_pixels = swap_normed.shape[1]
    flat_normed = swap_normed.reshape(-1, channels)
    qkv_rows = jnp.dot(flat_normed, full_qkv, preferred_element_type=jnp.float32).astype(
        jnp.bfloat16
    )
    qkv_rows = qkv_rows.reshape(frames, few_pixels, 3 * channels)
    attended_x, dqkv_x = attend_all(qkv_rows, swap_grads)
    grad_in = jnp.einsum(
        "pc,pd->cd",
        flat_normed,
        dqkv_x.reshape(-1, 3 * channels),
        preferred_element_type=jnp.float32,
    )
    grad_out = jnp.einsum(
        "pc,pd->cd",
        attended_x.reshape(-1, channels),
        swap_upstream.reshape(-1, channels),
        preferred_element_type=jnp.float32,
    )
    summands = jnp.concatenate([grad_in.reshape(-1), grad_out.reshape(-1)])
    return scattered_sum(summands)


def solution(mesh):
    return jax.shard_map(
        per_device,
        mesh=mesh,
        in_specs=(
            P("fsdp", "tm", "blk", None),
            P("blk", None),
            P(),
            P(),
            P("fsdp", None),
            P("fsdp", None),
            P("fsdp", "tm", "blk", None),
        ),
        out_specs=P(("blk", "tm", "fsdp")),
        check_vma=False,
    )
```

```python
import jax
import jax.numpy as jnp
from jax import lax
from jax.experimental import pallas as pl
from jax.experimental.pallas import tpu as pltpu
from jax.sharding import PartitionSpec as P

HEADS = 8
HALO = 130
VMEM = pltpu.MemorySpace.VMEM
SMEM = pltpu.MemorySpace.SMEM


def swap(values, axis, mask):
    return lax.ppermute(values, axis, [(i, i ^ mask) for i in range(lax.axis_size(axis))])


def pick(values, index, dim=0):
    return lax.dynamic_index_in_dim(values, index, dim, keepdims=False)


def conv_kernel(where_ref, near_ref, own_ref, halo_ref, taps_ref, gain_ref, out_ref):
    pixels, channels = own_ref.shape
    first, halo_first, zp = where_ref[0], where_ref[1], where_ref[2]
    half = pixels // 2
    near = near_ref[...]
    local = near - first
    outside = (local < 0) | (local >= pixels)
    local = jnp.where(outside, near - halo_first + pixels, local)
    table = jnp.concatenate([own_ref[...], halo_ref[...]], axis=0)
    slots = lax.broadcasted_iota(jnp.int32, (pixels, table.shape[0]), 1)
    chosen = jnp.concatenate(
        [
            jnp.where(local[:, k : k + 1] == slots, 1.0, 0.0).astype(jnp.bfloat16)
            for k in range(near.shape[1])
        ],
        axis=0,
    )
    gathered = jnp.dot(chosen, table, preferred_element_type=jnp.float32)
    own = own_ref[...].astype(jnp.float32)
    spatial = taps_ref[0:1, :] * own
    for k in range(near.shape[1]):
        spatial = spatial + taps_ref[k + 1 : k + 2, :] * gathered[k * pixels : (k + 1) * pixels]
    hidden = (own + spatial).astype(jnp.bfloat16).astype(jnp.float32)
    inverse = lax.rsqrt(jnp.mean(hidden * hidden, axis=-1, keepdims=True) + 1e-05)
    normed = (hidden * inverse * gain_ref[...]).astype(jnp.bfloat16)
    for h in range(2):
        out_ref[h ^ zp] = normed[h * half : (h + 1) * half]


def block_kernel(
    where_ref,
    *refs,
):
    frames = 4
    normed_refs, up_refs = refs[:frames], refs[frames : 2 * frames]
    qkv_ref, out_w_ref, keep_ref, send_ref, n_ref, u_ref, sums_ref, out_sums_ref = refs[2 * frames :]
    t, core = where_ref[0], where_ref[1]
    pixels, channels = normed_refs[0].shape
    width = out_w_ref.shape[0]
    depth = channels // HEADS
    for k in range(frames):
        n_ref[t ^ k] = normed_refs[k][...]
        u_ref[t ^ k] = up_refs[k][...]
    normed = n_ref[...].reshape(frames * pixels, channels)
    upstream = u_ref[...].reshape(frames * pixels, channels)
    qkv = jnp.dot(normed, qkv_ref[...], preferred_element_type=jnp.float32).astype(jnp.bfloat16)
    grads = lax.dot_general(
        upstream, out_w_ref[...], (((1,), (1,)), ((), ())), preferred_element_type=jnp.float32
    ).astype(jnp.bfloat16)

    def part(values, frame, third=0):
        rows = values[frame * pixels : (frame + 1) * pixels]
        return rows[:, third * width : (third + 1) * width].astype(jnp.float32)

    q = [part(qkv, i, 0) for i in range(frames)]
    k = [part(qkv, i, 1) for i in range(frames)]
    v = [part(qkv, i, 2) for i in range(frames)]
    g = [part(grads, i) for i in range(frames)]
    row_head = lax.broadcasted_iota(jnp.int32, (width, width), 0) // depth
    col_head = lax.broadcasted_iota(jnp.int32, (width, width), 1) // depth
    same = jnp.where(row_head == col_head, 1.0, 0.0).astype(jnp.bfloat16)

    def head_sums(products):
        stacked = jnp.concatenate(products, axis=0)
        high = stacked.astype(jnp.bfloat16)
        low = (stacked - high.astype(jnp.float32)).astype(jnp.bfloat16)
        total = jnp.dot(high, same, preferred_element_type=jnp.float32)
        total = total + jnp.dot(low, same, preferred_element_type=jnp.float32)
        return [total[i * pixels : (i + 1) * pixels] for i in range(len(products))]

    def rounded(values):
        return values.astype(jnp.bfloat16).astype(jnp.float32)

    attended, dq = [], []
    dk, dv = [None] * frames, [None] * frames

    def plus(total, term):
        return term if total is None else total + term

    for i in range(frames):
        scores = head_sums([q[i] * k[u] for u in range(i + 1)])
        scores = [s * 0.125 for s in scores]
        largest = scores[0]
        for s in scores[1:]:
            largest = jnp.maximum(largest, s)
        powers = [jnp.exp(s - largest) for s in scores]
        total = powers[0]
        for p in powers[1:]:
            total = total + p
        scale = 1.0 / total
        weights = [rounded(p * scale) for p in powers]
        dprob = head_sums([g[i] * v[u] for u in range(i + 1)])
        delta = weights[0] * dprob[0]
        for u in range(1, i + 1):
            delta = delta + weights[u] * dprob[u]
        seen, grad_q = None, None
        for u in range(i + 1):
            ds = rounded(weights[u] * (dprob[u] - delta) * 0.125)
            seen = plus(seen, weights[u] * v[u])
            grad_q = plus(grad_q, ds * k[u])
            dk[u] = plus(dk[u], ds * q[i])
            dv[u] = plus(dv[u], weights[u] * g[i])
        attended.append(seen.astype(jnp.bfloat16))
        dq.append(grad_q.astype(jnp.bfloat16))
    thirds = (dq, [d.astype(jnp.bfloat16) for d in dk], [d.astype(jnp.bfloat16) for d in dv])

    def over_rows(lhs, rhs):
        return lax.dot_general(
            lhs, rhs, (((0,), (0,)), ((), ())), preferred_element_type=jnp.float32
        )

    for m, pieces in enumerate(thirds):
        grad = over_rows(normed, jnp.concatenate(pieces, axis=0))
        for lane in range(0, width, 128):
            sums_ref[lane // 128, pl.ds(m, channels, stride=3), :] = grad[:, lane : lane + 128]
    out_sums_ref[...] = over_rows(jnp.concatenate(attended, axis=0), upstream)

    block = 64
    for x in range(2):
        for y in range(2):
            for zp in range(2):
                slot = (x * 2 + y) * 2 + zp
                for side, ref in ((core, keep_ref), (1 - core, send_ref)):
                    if y == 1 and zp == 1:
                        start = pl.multiple_of((2 * x + side) * block, block)
                        rows = out_sums_ref[pl.ds(start, block), :]
                        pieces = (rows[:, :width], rows[:, width:])
                    else:
                        pieces = []
                        for low in range(2):
                            index = y * 16 + (2 * zp + low) * 4 + 2 * x + side
                            start = pl.multiple_of(index * block, block)
                            pieces.append(
                                jnp.concatenate(
                                    [
                                        sums_ref[lane, pl.ds(start, block), :]
                                        for lane in range(width // 128)
                                    ],
                                    axis=1,
                                )
                            )
                    for low in range(2):
                        ref[slot, low * block : (low + 1) * block, :] = pieces[low].astype(ref.dtype)


def split_form(features, neighbours, conv_taps, norm_gain, qkv_weight, out_weight, cotangent):
    own = features[0, 0]
    upstream = cotangent[0, 0]
    pixels, channels = own.shape
    half = pixels // 2
    y = lax.axis_index("blk")
    t = lax.axis_index("tm")
    f = lax.axis_index("fsdp")
    zp, zh = t // 2, t % 2
    x, core = f // 2, f % 2
    width = channels // 2

    edge = lax.dynamic_slice(own, ((1 - y) * (pixels - HALO), 0), (HALO, channels))
    halo = swap(edge, "blk", 1)

    halves = upstream.reshape(2, half, channels)
    up_mine, up_other = pick(halves, zp), pick(halves, 1 - zp)
    ups = [up_mine, swap(up_mine, "tm", 1), swap(up_other, "tm", 2), swap(up_other, "tm", 3)]

    thirds = qkv_weight.reshape(-1, 3, 2, width)
    columns = pick(thirds, zh, 2).reshape(-1, 3 * width)
    from_x = swap(columns, "fsdp", 2)
    out_from_x = swap(out_weight, "fsdp", 2)
    out_rows = jnp.where(x == zh, out_weight, out_from_x)
    pair = jnp.stack([columns, from_x])
    pair_other = swap(pair, "fsdp", 1)
    out_other = swap(out_rows, "fsdp", 1)
    depth = qkv_weight.shape[0]
    by_core = jnp.where(
        core == 0, jnp.stack([pair, pair_other]), jnp.stack([pair_other, pair])
    )
    by_x = jnp.where(x == 0, by_core, by_core[:, ::-1])
    full_qkv = by_x.transpose(1, 0, 2, 3).reshape(4 * depth, 3 * width)
    full_out = jnp.where(
        core == 0, jnp.concatenate([out_rows, out_other]), jnp.concatenate([out_other, out_rows])
    )

    where = jnp.stack([y * pixels, jnp.where(y == 0, pixels, pixels - HALO), zp]).astype(jnp.int32)
    normed = pl.pallas_call(
        conv_kernel,
        out_shape=jax.ShapeDtypeStruct((2, half, channels), jnp.bfloat16),
        in_specs=[pl.BlockSpec(memory_space=SMEM)] + [pl.BlockSpec(memory_space=VMEM)] * 5,
        out_specs=pl.BlockSpec(memory_space=VMEM),
        name="conv",
    )(where, neighbours, own, halo, conv_taps, norm_gain.reshape(1, channels))
    n_mine, n_other = normed[0], normed[1]
    rows = [n_mine, swap(n_mine, "tm", 1), swap(n_other, "tm", 2), swap(n_other, "tm", 3)]

    block = 64
    keep, send = pl.pallas_call(
        block_kernel,
        out_shape=(
            jax.ShapeDtypeStruct((8, 2 * block, width), jnp.float32),
            jax.ShapeDtypeStruct((8, 2 * block, width), jnp.bfloat16),
        ),
        in_specs=[pl.BlockSpec(memory_space=SMEM)] + [pl.BlockSpec(memory_space=VMEM)] * 10,
        out_specs=(pl.BlockSpec(memory_space=VMEM), pl.BlockSpec(memory_space=VMEM)),
        scratch_shapes=[
            pltpu.VMEM((4, half, channels), jnp.bfloat16),
            pltpu.VMEM((4, half, channels), jnp.bfloat16),
            pltpu.VMEM((width // 128, 3 * channels, 128), jnp.float32),
            pltpu.VMEM((width, channels), jnp.float32),
        ],
        name="attend",
    )(jnp.stack([t, core]).astype(jnp.int32), *rows, *ups, full_qkv, full_out)

    def narrow(values):
        return values.astype(jnp.bfloat16)

    total = keep + swap(send, "fsdp", 1).astype(jnp.float32)
    total = total.reshape(2, 2, 2, 2 * block, width)
    first, second = total[..., : width // 2], total[..., width // 2 :]
    got_first = swap(narrow(pick(first, 1 - x, 0)), "fsdp", 2)
    got_second = swap(narrow(pick(second, 1 - y, 1)), "blk", 1)
    first = pick(first, x, 0) + got_first.astype(jnp.float32)
    second = pick(second, y, 1) + got_second.astype(jnp.float32)
    got_first = swap(narrow(pick(first, 1 - y, 0)), "blk", 1)
    got_second = swap(narrow(pick(second, 1 - x, 0)), "fsdp", 2)
    first = pick(first, y, 0) + got_first.astype(jnp.float32)
    second = pick(second, x, 0) + got_second.astype(jnp.float32)
    total = jnp.concatenate([first, second], axis=-1)
    total = pick(total, zp) + swap(narrow(pick(total, 1 - zp)), "tm", 2).astype(jnp.float32)
    total = total.reshape(2, block, width)
    mine = pick(total, zh)
    got = swap(pick(total, 1 - zh), "tm", 1)
    is_out = (y == 1) & (zp == 1)
    left = jnp.where(is_out, total[0], jnp.where(zh == 0, mine, got))
    right = jnp.where(is_out, total[1], jnp.where(zh == 0, got, mine))
    return jnp.concatenate([left, right], axis=1).reshape(-1)


def with_halo(cells, sides, width):
    for axis, dim in sides:
        count = lax.axis_size(axis)
        ends = count - 1
        head = lax.slice_in_dim(cells, 0, width, axis=dim)
        tail = lax.slice_in_dim(cells, cells.shape[dim] - width, cells.shape[dim], axis=dim)
        cells = jnp.concatenate(
            [
                lax.ppermute(tail, axis, [(i, (i + 1) % count) for i in range(ends)]),
                cells,
                lax.ppermute(head, axis, [((i + 1) % count, i) for i in range(ends)]),
            ],
            axis=dim,
        )
    return cells


def halved(partial, axis, bit):
    count = lax.axis_size(axis)
    mine = (lax.axis_index(axis) >> bit) & 1
    keep = lax.dynamic_index_in_dim(partial, mine, 0, keepdims=False)
    send = lax.dynamic_index_in_dim(partial, 1 - mine, 0, keepdims=False)
    got = lax.ppermute(send.astype(jnp.bfloat16), axis, [(i, i ^ (1 << bit)) for i in range(count)])
    return keep + got.astype(jnp.float32)


def scattered_sum(summands):
    counts = [lax.axis_size(axis) for axis in ("blk", "tm", "fsdp")]
    bits = [count.bit_length() - 1 for count in counts]
    order = [("fsdp", bit) for bit in range(bits[2])]
    order += [("blk", bit) for bit in range(bits[0])]
    order += [("tm", bit) for bit in range(bits[1])]
    labels = [(axis, bit) for axis, many in zip(("blk", "tm", "fsdp"), bits) for bit in reversed(range(many))]
    partial = summands.reshape((2,) * len(labels) + (-1, 128))
    for axis, bit in order:
        place = labels.index((axis, bit))
        labels.pop(place)
        partial = halved(jnp.moveaxis(partial, place, 0), axis, bit)
    return partial.reshape(-1)


def rounded(values):
    return lax.optimization_barrier(values.astype(jnp.bfloat16)).astype(jnp.float32)


def attend_all(qkv_rows, grad_rows):
    frames, pixels, width = qkv_rows.shape
    channels = width // 3

    def split_heads(block):
        return block.reshape(frames, pixels, HEADS, channels // HEADS).astype(jnp.float32)

    queries = split_heads(qkv_rows[:, :, :channels])
    keys_all = split_heads(qkv_rows[:, :, channels : 2 * channels])
    values = split_heads(qkv_rows[:, :, 2 * channels :])
    grads = split_heads(grad_rows)
    scores = jnp.einsum("tpeh,upeh->petu", queries, keys_all) * 0.125
    causal = jnp.arange(frames)[:, None] >= jnp.arange(frames)[None, :]
    masked = jnp.where(causal, scores, -1e30)
    largest = jnp.max(masked, axis=-1, keepdims=True)
    totals = jnp.sum(jnp.exp(masked - largest), axis=-1, keepdims=True)
    log_total = largest + jnp.log(totals)
    weights = rounded(jnp.exp(masked - log_total))
    attended = jnp.einsum("petu,upeh->tpeh", weights, values)
    dprob = jnp.einsum("tpeh,upeh->petu", grads, values)
    delta = jnp.sum(weights * dprob, axis=-1, keepdims=True)
    dscore = rounded(weights * (dprob - delta) * 0.125)
    grad_query = jnp.einsum("petu,upeh->tpeh", dscore, keys_all)
    grad_key = jnp.einsum("petu,tpeh->upeh", dscore, queries)
    grad_value = jnp.einsum("petu,tpeh->upeh", weights, grads)
    joined = jnp.concatenate(
        [part.reshape(frames, pixels, channels) for part in (grad_query, grad_key, grad_value)],
        axis=-1,
    )
    return (
        attended.reshape(frames, pixels, channels).astype(jnp.bfloat16),
        joined.astype(jnp.bfloat16),
    )


def general_form(features, neighbours, conv_taps, norm_gain, qkv_weight, out_weight, cotangent):
    inputs = features[0, 0]
    upstream = cotangent[0, 0]
    pixels, channels = inputs.shape
    padded = with_halo(inputs, (("blk", 0),), HALO)
    first_pixel = lax.axis_index("blk") * pixels
    local_rows = neighbours - first_pixel + HALO
    inputs_f = inputs.astype(jnp.float32)
    spatial = conv_taps[0] * inputs_f
    for column in range(8):
        spatial = spatial + conv_taps[column + 1] * jnp.take(
            padded, local_rows[:, column], axis=0
        ).astype(jnp.float32)
    hidden_f = rounded(inputs_f + spatial)
    inverse = lax.rsqrt(jnp.mean(hidden_f * hidden_f, axis=-1, keepdims=True) + 1e-05)
    normed = (hidden_f * inverse * norm_gain).astype(jnp.bfloat16)
    full_qkv, full_out = (
        lax.all_gather(qkv_weight, "fsdp", axis=0, tiled=True),
        lax.all_gather(out_weight, "fsdp", axis=0, tiled=True),
    )
    att_grads = jnp.dot(upstream, full_out.T, preferred_element_type=jnp.float32).astype(
        jnp.bfloat16
    )
    swap_normed, swap_grads, swap_upstream = (
        lax.all_to_all(normed[None], "tm", split_axis=1, concat_axis=0, tiled=True),
        lax.all_to_all(att_grads[None], "tm", split_axis=1, concat_axis=0, tiled=True),
        lax.all_to_all(upstream[None], "tm", split_axis=1, concat_axis=0, tiled=True),
    )
    frames = swap_normed.shape[0]
    few_pixels = swap_normed.shape[1]
    flat_normed = swap_normed.reshape(-1, channels)
    qkv_rows = jnp.dot(flat_normed, full_qkv, preferred_element_type=jnp.float32).astype(
        jnp.bfloat16
    )
    qkv_rows = qkv_rows.reshape(frames, few_pixels, 3 * channels)
    attended_x, dqkv_x = attend_all(qkv_rows, swap_grads)
    grad_in = jnp.einsum(
        "pc,pd->cd",
        flat_normed,
        dqkv_x.reshape(-1, 3 * channels),
        preferred_element_type=jnp.float32,
    )
    grad_out = jnp.einsum(
        "pc,pd->cd",
        attended_x.reshape(-1, channels),
        swap_upstream.reshape(-1, channels),
        preferred_element_type=jnp.float32,
    )
    summands = jnp.concatenate([grad_in.reshape(-1), grad_out.reshape(-1)])
    return scattered_sum(summands)


def solution(mesh):
    sizes = mesh.shape

    def per_device(*arrays):
        pixels, channels = arrays[0].shape[-2:]
        devices = sizes["blk"] * sizes["tm"] * sizes["fsdp"]
        fits = (
            sizes["blk"] == 2
            and sizes["tm"] == sizes["fsdp"] == arrays[0].shape[0] * 4
            and devices == 4 * HEADS
            and pixels >= HALO
            and pixels % 32 == 0
            and channels == 64 * HEADS
        )
        return (split_form if fits else general_form)(*arrays)

    return jax.shard_map(
        per_device,
        mesh=mesh,
        in_specs=(
            P("fsdp", "tm", "blk", None),
            P("blk", None),
            P(),
            P(),
            P("fsdp", None),
            P("fsdp", None),
            P("fsdp", "tm", "blk", None),
        ),
        out_specs=P(("blk", "tm", "fsdp")),
        check_vma=False,
    )
```

```python
import jax
import jax.numpy as jnp
from jax import lax
from jax.experimental import pallas as pl
from jax.experimental.pallas import tpu as pltpu
from jax.sharding import PartitionSpec as P


HEADS = 8
HALO = 130
VMEM = pltpu.MemorySpace.VMEM


def swap(values, axis, mask):
    return lax.ppermute(values, axis, [(i, i ^ mask) for i in range(lax.axis_size(axis))])


def pick(values, index, dim=0):
    return lax.dynamic_index_in_dim(values, index, dim, keepdims=False)


def place():
    t, f = lax.axis_index("tm"), lax.axis_index("fsdp")
    return lax.axis_index("blk"), t, t >> 1, t & 1, f >> 1, f & 1


def start_all(copies):
    for copy in copies:
        copy.start()


def prep_kernel(up_ref, qkv_ref, out_w_ref, mine_ref, other_ref, cut_ref, sems):
    _, _, zp, zh, _, _ = place()
    half = mine_ref.shape[0]
    width = out_w_ref.shape[1] // 2
    rows = lambda h: up_ref.at[pl.ds(pl.multiple_of(h * half, 16), half)]
    copies = [
        pltpu.make_async_copy(rows(zp), mine_ref, sems.at[0]),
        pltpu.make_async_copy(rows(1 - zp), other_ref, sems.at[1]),
        pltpu.make_async_copy(out_w_ref, cut_ref.at[:, pl.ds(3 * width, 2 * width)], sems.at[2]),
    ]
    for m in range(3):
        start = pl.multiple_of((2 * m + zh) * width, 128)
        copies.append(
            pltpu.make_async_copy(
                qkv_ref.at[:, pl.ds(start, width)],
                cut_ref.at[:, pl.ds(m * width, width)],
                sems.at[3 + m],
            )
        )
    start_all(copies)
    for copy in copies:
        copy.wait()


def conv_kernel(
    near_hbm, own_hbm, band_hbm, taps_hbm, gain_hbm, mine_ref, other_ref,
    near_ref, table_ref, taps_ref, gain_ref, sems,
):
    y, _, zp, _, _, _ = place()
    pixels, _ = own_hbm.shape
    half = pixels // 2
    pairs = [
        (near_hbm, near_ref),
        (taps_hbm, taps_ref),
        (gain_hbm, gain_ref),
        (own_hbm, table_ref.at[pl.ds(0, pixels)]),
        (band_hbm, table_ref.at[pl.ds(pixels, pixels)]),
    ]
    copies = [pltpu.make_async_copy(a, b, sems.at[i]) for i, (a, b) in enumerate(pairs)]
    start_all(copies)
    copies[0].wait()
    near = near_ref[...].T
    neighbours = near.shape[1]
    local = near - y * pixels
    local = jnp.where(local < 0, local + 2 * pixels, local)
    slots = lax.broadcasted_iota(jnp.int32, (pixels, 2 * pixels), 1)
    chosen = jnp.concatenate(
        [
            jnp.where(local[:, k : k + 1] == slots, 1.0, 0.0).astype(jnp.bfloat16)
            for k in range(neighbours)
        ],
        axis=0,
    )
    for copy in copies[1:]:
        copy.wait()
    gathered = jnp.dot(chosen, table_ref[...], preferred_element_type=jnp.float32)
    own = table_ref[:pixels, :].astype(jnp.float32)
    spatial = taps_ref[0:1, :] * own
    for k in range(neighbours):
        spatial = spatial + taps_ref[k + 1 : k + 2, :] * gathered[k * pixels : (k + 1) * pixels]
    hidden = (own + spatial).astype(jnp.bfloat16).astype(jnp.float32)
    inverse = lax.rsqrt(jnp.mean(hidden * hidden, axis=-1, keepdims=True) + 1e-05)
    normed = (hidden * inverse * gain_ref[...]).astype(jnp.bfloat16)
    low, high = normed[:half], normed[half:]

    @pl.when(zp == 0)
    def _():
        mine_ref[...] = low
        other_ref[...] = high

    @pl.when(zp == 1)
    def _():
        mine_ref[...] = high
        other_ref[...] = low


def block_kernel(*refs):
    frames = 4
    sources, refs = refs[: 3 * frames], refs[3 * frames :]
    keep_ref, send_ref, n_ref, u_ref, qkv_ref, out_w_ref, sums_ref, out_sums_ref, sems = refs
    _, t, _, zh, x, core = place()
    pixels, channels = sources[0].shape
    width, depth = out_w_ref.shape[0], channels // HEADS
    rows = sources[-1].shape[0]
    up_copies, row_copies, qkv_copies = [], [], []
    for k in range(frames):
        row_copies.append(pltpu.make_async_copy(sources[k], n_ref.at[t ^ k], sems.at[k]))
        up_copies.append(
            pltpu.make_async_copy(sources[frames + k], u_ref.at[t ^ k], sems.at[frames + k])
        )
    shards = sources[2 * frames :]
    for k, shard in enumerate(shards):
        f = (2 * x + core) ^ (2 * (k & 1) + (k >> 1))
        qkv_copies.append(
            pltpu.make_async_copy(
                shard.at[:, pl.ds(0, 3 * width)],
                qkv_ref.at[pl.ds(pl.multiple_of(f * rows, 128), rows)],
                sems.at[2 * frames + k],
            )
        )

    def out_copy(shard, k):
        start = pl.multiple_of((core ^ k) * rows, 128)
        return pltpu.make_async_copy(
            shard.at[:, pl.ds(3 * width, channels)],
            out_w_ref.at[pl.ds(start, rows)],
            sems.at[3 * frames + k],
        )

    start_all(row_copies + qkv_copies + up_copies)
    for k in range(2):

        @pl.when(x == zh)
        def _(k=k):
            out_copy(shards[2 * k], k).start()

        @pl.when(x != zh)
        def _(k=k):
            out_copy(shards[2 * k + 1], k).start()

    for copy in row_copies + qkv_copies:
        copy.wait()
    normed = n_ref[...].reshape(frames * pixels, channels)
    qkv = jnp.dot(normed, qkv_ref[...], preferred_element_type=jnp.float32).astype(jnp.bfloat16)
    for copy in up_copies + [out_copy(shards[2 * k], k) for k in range(2)]:
        copy.wait()
    upstream = u_ref[...].reshape(frames * pixels, channels)
    grads = lax.dot_general(
        upstream, out_w_ref[...], (((1,), (1,)), ((), ())), preferred_element_type=jnp.float32
    ).astype(jnp.bfloat16)

    def part(values, frame, third=0):
        rows = values[frame * pixels : (frame + 1) * pixels]
        return rows[:, third * width : (third + 1) * width].astype(jnp.float32)

    q = [part(qkv, i, 0) for i in range(frames)]
    k = [part(qkv, i, 1) for i in range(frames)]
    v = [part(qkv, i, 2) for i in range(frames)]
    g = [part(grads, i) for i in range(frames)]
    row_head = lax.broadcasted_iota(jnp.int32, (width, width), 0) // depth
    col_head = lax.broadcasted_iota(jnp.int32, (width, width), 1) // depth
    same = jnp.where(row_head == col_head, 1.0, 0.0).astype(jnp.bfloat16)

    def head_sums(products):
        stacked = jnp.concatenate(products, axis=0)
        high = stacked.astype(jnp.bfloat16)
        low = (stacked - high.astype(jnp.float32)).astype(jnp.bfloat16)
        total = jnp.dot(high, same, preferred_element_type=jnp.float32)
        total = total + jnp.dot(low, same, preferred_element_type=jnp.float32)
        return [total[i * pixels : (i + 1) * pixels] for i in range(len(products))]

    def rounded(values):
        return values.astype(jnp.bfloat16).astype(jnp.float32)

    attended, dq = [], []
    dk, dv = [None] * frames, [None] * frames

    def plus(total, term):
        return term if total is None else total + term

    for i in range(frames):
        scores = head_sums([q[i] * k[u] for u in range(i + 1)])
        scores = [s * 0.125 for s in scores]
        largest = scores[0]
        for s in scores[1:]:
            largest = jnp.maximum(largest, s)
        powers = [jnp.exp(s - largest) for s in scores]
        total = powers[0]
        for p in powers[1:]:
            total = total + p
        scale = 1.0 / total
        weights = [rounded(p * scale) for p in powers]
        dprob = head_sums([g[i] * v[u] for u in range(i + 1)])
        delta = weights[0] * dprob[0]
        for u in range(1, i + 1):
            delta = delta + weights[u] * dprob[u]
        seen, grad_q = None, None
        for u in range(i + 1):
            ds = rounded(weights[u] * (dprob[u] - delta) * 0.125)
            seen = plus(seen, weights[u] * v[u])
            grad_q = plus(grad_q, ds * k[u])
            dk[u] = plus(dk[u], ds * q[i])
            dv[u] = plus(dv[u], weights[u] * g[i])
        attended.append(seen.astype(jnp.bfloat16))
        dq.append(grad_q.astype(jnp.bfloat16))
    thirds = (dq, [d.astype(jnp.bfloat16) for d in dk], [d.astype(jnp.bfloat16) for d in dv])

    def over_rows(lhs, rhs):
        return lax.dot_general(
            lhs, rhs, (((0,), (0,)), ((), ())), preferred_element_type=jnp.float32
        )

    for m, pieces in enumerate(thirds):
        grad = over_rows(normed, jnp.concatenate(pieces, axis=0))
        for lane in range(0, width, 128):
            sums_ref[lane // 128, pl.ds(m, channels, stride=3), :] = grad[:, lane : lane + 128]
    out_sums_ref[...] = over_rows(jnp.concatenate(attended, axis=0), upstream)

    block = 64
    for x in range(2):
        for y in range(2):
            for zp in range(2):
                slot = (x * 2 + y) * 2 + zp
                for side, ref in ((core, keep_ref), (1 - core, send_ref)):
                    if y == 1 and zp == 1:
                        start = pl.multiple_of((2 * x + side) * block, block)
                        rows = out_sums_ref[pl.ds(start, block), :]
                        pieces = (rows[:, :width], rows[:, width:])
                    else:
                        pieces = []
                        for low in range(2):
                            index = y * 16 + (2 * zp + low) * 4 + 2 * x + side
                            start = pl.multiple_of(index * block, block)
                            pieces.append(
                                jnp.concatenate(
                                    [
                                        sums_ref[lane, pl.ds(start, block), :]
                                        for lane in range(width // 128)
                                    ],
                                    axis=1,
                                )
                            )
                    for low in range(2):
                        ref[slot, low * block : (low + 1) * block, :] = pieces[low].astype(ref.dtype)


def split_form(features, neighbours, conv_taps, norm_gain, qkv_weight, out_weight, cotangent):
    own = features[0, 0]
    pixels, channels = own.shape
    half, width, block = pixels // 2, channels // 2, channels // HEADS
    y, _, zp, zh, x, _ = place()
    narrow_type = jnp.bfloat16
    anywhere = pl.BlockSpec(memory_space=pl.ANY)
    in_vmem = pl.BlockSpec(memory_space=VMEM)
    piece = jax.ShapeDtypeStruct((half, channels), narrow_type)

    band = swap(own, "blk", 1)
    up_mine, up_other, cut = pl.pallas_call(
        prep_kernel,
        out_shape=(
            piece,
            piece,
            jax.ShapeDtypeStruct((qkv_weight.shape[0], 3 * width + channels), narrow_type),
        ),
        in_specs=[anywhere] * 3,
        out_specs=(in_vmem,) * 3,
        scratch_shapes=[pltpu.SemaphoreType.DMA((6,))],
        compiler_params=pltpu.CompilerParams(vmem_limit_bytes=4 << 20),
        name="prep",
    )(cotangent[0, 0], qkv_weight, out_weight)

    def spread(mine, other):
        far = swap(other, "tm", 3)
        middle = swap(other, "tm", 2)
        near = swap(mine, "tm", 1)
        return [mine, near, middle, far]

    ups = spread(up_mine, up_other)
    cut_x = swap(cut, "fsdp", 2)
    n_mine, n_other = pl.pallas_call(
        conv_kernel,
        out_shape=(piece, piece),
        in_specs=[anywhere] * 5,
        out_specs=(in_vmem,) * 2,
        scratch_shapes=[
            pltpu.VMEM((neighbours.shape[1], pixels), jnp.int32),
            pltpu.VMEM((2 * pixels, channels), narrow_type),
            pltpu.VMEM(conv_taps.shape, jnp.float32),
            pltpu.VMEM((1, channels), jnp.float32),
            pltpu.SemaphoreType.DMA((5,)),
        ],
        compiler_params=pltpu.CompilerParams(vmem_limit_bytes=16 << 20),
        name="conv",
    )(neighbours.T, own, band, conv_taps, norm_gain.reshape(1, channels))
    rows = spread(n_mine, n_other)
    cut_c = swap(cut, "fsdp", 1)
    cut_xc = swap(cut_x, "fsdp", 1)

    keep, send = pl.pallas_call(
        block_kernel,
        out_shape=(
            jax.ShapeDtypeStruct((8, 2 * block, width), jnp.float32),
            jax.ShapeDtypeStruct((8, 2 * block, width), narrow_type),
        ),
        in_specs=[anywhere] * 12,
        out_specs=(in_vmem, in_vmem),
        scratch_shapes=[
            pltpu.VMEM((4, half, channels), narrow_type),
            pltpu.VMEM((4, half, channels), narrow_type),
            pltpu.VMEM((channels, 3 * width), narrow_type),
            pltpu.VMEM((width, channels), narrow_type),
            pltpu.VMEM((width // 128, 3 * channels, 128), jnp.float32),
            pltpu.VMEM((width, channels), jnp.float32),
            pltpu.SemaphoreType.DMA((14,)),
        ],
        compiler_params=pltpu.CompilerParams(vmem_limit_bytes=32 << 20),
        name="attend",
    )(*rows, *ups, cut, cut_x, cut_c, cut_xc)

    def narrow(values):
        return values.astype(jnp.bfloat16)

    total = keep + swap(send, "fsdp", 1).astype(jnp.float32)
    total = total.reshape(2, 2, 2, 2 * block, width)
    first, second = total[..., : width // 2], total[..., width // 2 :]
    got_first = swap(narrow(pick(first, 1 - x, 0)), "fsdp", 2)
    got_second = swap(narrow(pick(second, 1 - y, 1)), "blk", 1)
    first = pick(first, x, 0) + got_first.astype(jnp.float32)
    second = pick(second, y, 1) + got_second.astype(jnp.float32)
    got_first = swap(narrow(pick(first, 1 - y, 0)), "blk", 1)
    got_second = swap(narrow(pick(second, 1 - x, 0)), "fsdp", 2)
    first = pick(first, y, 0) + got_first.astype(jnp.float32)
    second = pick(second, x, 0) + got_second.astype(jnp.float32)
    total = jnp.concatenate([first, second], axis=-1)
    total = pick(total, zp) + swap(narrow(pick(total, 1 - zp)), "tm", 2).astype(jnp.float32)
    total = total.reshape(2, block, width)
    mine = pick(total, zh)
    got = swap(pick(total, 1 - zh), "tm", 1)
    is_out = (y == 1) & (zp == 1)
    left = jnp.where(is_out, total[0], jnp.where(zh == 0, mine, got))
    right = jnp.where(is_out, total[1], jnp.where(zh == 0, got, mine))
    return jnp.concatenate([left, right], axis=1).reshape(-1)


def with_halo(cells, sides, width):
    for axis, dim in sides:
        count = lax.axis_size(axis)
        ends = count - 1
        head = lax.slice_in_dim(cells, 0, width, axis=dim)
        tail = lax.slice_in_dim(cells, cells.shape[dim] - width, cells.shape[dim], axis=dim)
        cells = jnp.concatenate(
            [
                lax.ppermute(tail, axis, [(i, (i + 1) % count) for i in range(ends)]),
                cells,
                lax.ppermute(head, axis, [((i + 1) % count, i) for i in range(ends)]),
            ],
            axis=dim,
        )
    return cells


def halved(partial, axis, bit):
    count = lax.axis_size(axis)
    mine = (lax.axis_index(axis) >> bit) & 1
    keep = lax.dynamic_index_in_dim(partial, mine, 0, keepdims=False)
    send = lax.dynamic_index_in_dim(partial, 1 - mine, 0, keepdims=False)
    got = lax.ppermute(send.astype(jnp.bfloat16), axis, [(i, i ^ (1 << bit)) for i in range(count)])
    return keep + got.astype(jnp.float32)


def scattered_sum(summands):
    counts = [lax.axis_size(axis) for axis in ("blk", "tm", "fsdp")]
    bits = [count.bit_length() - 1 for count in counts]
    order = [("fsdp", bit) for bit in range(bits[2])]
    order += [("blk", bit) for bit in range(bits[0])]
    order += [("tm", bit) for bit in range(bits[1])]
    labels = [(axis, bit) for axis, many in zip(("blk", "tm", "fsdp"), bits) for bit in reversed(range(many))]
    partial = summands.reshape((2,) * len(labels) + (-1, 128))
    for axis, bit in order:
        place = labels.index((axis, bit))
        labels.pop(place)
        partial = halved(jnp.moveaxis(partial, place, 0), axis, bit)
    return partial.reshape(-1)


def rounded(values):
    return lax.optimization_barrier(values.astype(jnp.bfloat16)).astype(jnp.float32)


def attend_all(qkv_rows, grad_rows):
    frames, pixels, width = qkv_rows.shape
    channels = width // 3

    def split_heads(block):
        return block.reshape(frames, pixels, HEADS, channels // HEADS).astype(jnp.float32)

    queries = split_heads(qkv_rows[:, :, :channels])
    keys_all = split_heads(qkv_rows[:, :, channels : 2 * channels])
    values = split_heads(qkv_rows[:, :, 2 * channels :])
    grads = split_heads(grad_rows)
    scores = jnp.einsum("tpeh,upeh->petu", queries, keys_all) * 0.125
    causal = jnp.arange(frames)[:, None] >= jnp.arange(frames)[None, :]
    masked = jnp.where(causal, scores, -1e30)
    largest = jnp.max(masked, axis=-1, keepdims=True)
    totals = jnp.sum(jnp.exp(masked - largest), axis=-1, keepdims=True)
    log_total = largest + jnp.log(totals)
    weights = rounded(jnp.exp(masked - log_total))
    attended = jnp.einsum("petu,upeh->tpeh", weights, values)
    dprob = jnp.einsum("tpeh,upeh->petu", grads, values)
    delta = jnp.sum(weights * dprob, axis=-1, keepdims=True)
    dscore = rounded(weights * (dprob - delta) * 0.125)
    grad_query = jnp.einsum("petu,upeh->tpeh", dscore, keys_all)
    grad_key = jnp.einsum("petu,tpeh->upeh", dscore, queries)
    grad_value = jnp.einsum("petu,tpeh->upeh", weights, grads)
    joined = jnp.concatenate(
        [part.reshape(frames, pixels, channels) for part in (grad_query, grad_key, grad_value)],
        axis=-1,
    )
    return (
        attended.reshape(frames, pixels, channels).astype(jnp.bfloat16),
        joined.astype(jnp.bfloat16),
    )


def general_form(features, neighbours, conv_taps, norm_gain, qkv_weight, out_weight, cotangent):
    inputs = features[0, 0]
    upstream = cotangent[0, 0]
    pixels, channels = inputs.shape
    padded = with_halo(inputs, (("blk", 0),), HALO)
    first_pixel = lax.axis_index("blk") * pixels
    local_rows = neighbours - first_pixel + HALO
    inputs_f = inputs.astype(jnp.float32)
    spatial = conv_taps[0] * inputs_f
    for column in range(8):
        spatial = spatial + conv_taps[column + 1] * jnp.take(
            padded, local_rows[:, column], axis=0
        ).astype(jnp.float32)
    hidden_f = rounded(inputs_f + spatial)
    inverse = lax.rsqrt(jnp.mean(hidden_f * hidden_f, axis=-1, keepdims=True) + 1e-05)
    normed = (hidden_f * inverse * norm_gain).astype(jnp.bfloat16)
    full_qkv, full_out = (
        lax.all_gather(qkv_weight, "fsdp", axis=0, tiled=True),
        lax.all_gather(out_weight, "fsdp", axis=0, tiled=True),
    )
    att_grads = jnp.dot(upstream, full_out.T, preferred_element_type=jnp.float32).astype(
        jnp.bfloat16
    )
    swap_normed, swap_grads, swap_upstream = (
        lax.all_to_all(normed[None], "tm", split_axis=1, concat_axis=0, tiled=True),
        lax.all_to_all(att_grads[None], "tm", split_axis=1, concat_axis=0, tiled=True),
        lax.all_to_all(upstream[None], "tm", split_axis=1, concat_axis=0, tiled=True),
    )
    frames = swap_normed.shape[0]
    few_pixels = swap_normed.shape[1]
    flat_normed = swap_normed.reshape(-1, channels)
    qkv_rows = jnp.dot(flat_normed, full_qkv, preferred_element_type=jnp.float32).astype(
        jnp.bfloat16
    )
    qkv_rows = qkv_rows.reshape(frames, few_pixels, 3 * channels)
    attended_x, dqkv_x = attend_all(qkv_rows, swap_grads)
    grad_in = jnp.einsum(
        "pc,pd->cd",
        flat_normed,
        dqkv_x.reshape(-1, 3 * channels),
        preferred_element_type=jnp.float32,
    )
    grad_out = jnp.einsum(
        "pc,pd->cd",
        attended_x.reshape(-1, channels),
        swap_upstream.reshape(-1, channels),
        preferred_element_type=jnp.float32,
    )
    summands = jnp.concatenate([grad_in.reshape(-1), grad_out.reshape(-1)])
    return scattered_sum(summands)


def solution(mesh):
    sizes = mesh.shape

    def per_device(*arrays):
        pixels, channels = arrays[0].shape[-2:]
        devices = sizes["blk"] * sizes["tm"] * sizes["fsdp"]
        fits = (
            sizes["blk"] == 2
            and sizes["tm"] == sizes["fsdp"] == arrays[0].shape[0] * 4
            and devices == 4 * HEADS
            and pixels >= HALO
            and pixels % 32 == 0
            and channels == 64 * HEADS
        )
        if not fits:
            return general_form(*arrays)
        return split_form(*arrays)

    return jax.shard_map(
        per_device,
        mesh=mesh,
        in_specs=(
            P("fsdp", "tm", "blk", None),
            P("blk", None),
            P(),
            P(),
            P("fsdp", None),
            P("fsdp", None),
            P("fsdp", "tm", "blk", None),
        ),
        out_specs=P(("blk", "tm", "fsdp")),
        check_vma=False,
    )
```

```python
import jax
import jax.numpy as jnp
from jax import lax
from jax.experimental import pallas as pl
from jax.experimental.pallas import tpu as pltpu
from jax.sharding import PartitionSpec as P


HEADS = 8
HALO = 130
VMEM = pltpu.MemorySpace.VMEM


def swap(values, axis, mask):
    return lax.ppermute(values, axis, [(i, i ^ mask) for i in range(lax.axis_size(axis))])


def pick(values, index, dim=0):
    return lax.dynamic_index_in_dim(values, index, dim, keepdims=False)


def place():
    t, f = lax.axis_index("tm"), lax.axis_index("fsdp")
    return lax.axis_index("blk"), t, t >> 1, t & 1, f >> 1, f & 1


def start_all(copies):
    for copy in copies:
        copy.start()


def prep_kernel(up_ref, qkv_ref, out_w_ref, mine_ref, other_ref, cut_ref, sems):
    _, _, zp, zh, _, _ = place()
    half = mine_ref.shape[0]
    width = out_w_ref.shape[1] // 2
    rows = lambda h: up_ref.at[pl.ds(pl.multiple_of(h * half, 16), half)]
    copies = [
        pltpu.make_async_copy(rows(zp), mine_ref, sems.at[0]),
        pltpu.make_async_copy(rows(1 - zp), other_ref, sems.at[1]),
        pltpu.make_async_copy(out_w_ref, cut_ref.at[:, pl.ds(3 * width, 2 * width)], sems.at[2]),
    ]
    for m in range(3):
        start = pl.multiple_of((2 * m + zh) * width, 128)
        copies.append(
            pltpu.make_async_copy(
                qkv_ref.at[:, pl.ds(start, width)],
                cut_ref.at[:, pl.ds(m * width, width)],
                sems.at[3 + m],
            )
        )
    start_all(copies)
    for copy in copies:
        copy.wait()


def conv_kernel(
    near_hbm, own_hbm, band_hbm, taps_hbm, gain_hbm, mine_ref, other_ref,
    near_ref, table_ref, taps_ref, gain_ref, sems,
):
    y, _, zp, _, _, _ = place()
    pixels, _ = own_hbm.shape
    half = pixels // 2
    pairs = [
        (near_hbm, near_ref),
        (taps_hbm, taps_ref),
        (gain_hbm, gain_ref),
        (own_hbm, table_ref.at[pl.ds(0, pixels)]),
        (band_hbm, table_ref.at[pl.ds(pixels, pixels)]),
    ]
    copies = [pltpu.make_async_copy(a, b, sems.at[i]) for i, (a, b) in enumerate(pairs)]
    start_all(copies)
    copies[0].wait()
    near = near_ref[...].T
    neighbours = near.shape[1]
    local = near - y * pixels
    local = jnp.where(local < 0, local + 2 * pixels, local)
    slots = lax.broadcasted_iota(jnp.int32, (pixels, 2 * pixels), 1)
    chosen = jnp.concatenate(
        [
            jnp.where(local[:, k : k + 1] == slots, 1.0, 0.0).astype(jnp.bfloat16)
            for k in range(neighbours)
        ],
        axis=0,
    )
    for copy in copies[1:]:
        copy.wait()
    gathered = jnp.dot(chosen, table_ref[...], preferred_element_type=jnp.float32)
    own = table_ref[:pixels, :].astype(jnp.float32)
    spatial = taps_ref[0:1, :] * own
    for k in range(neighbours):
        spatial = spatial + taps_ref[k + 1 : k + 2, :] * gathered[k * pixels : (k + 1) * pixels]
    hidden = (own + spatial).astype(jnp.bfloat16).astype(jnp.float32)
    inverse = lax.rsqrt(jnp.mean(hidden * hidden, axis=-1, keepdims=True) + 1e-05)
    normed = (hidden * inverse * gain_ref[...]).astype(jnp.bfloat16)
    low, high = normed[:half], normed[half:]

    @pl.when(zp == 0)
    def _():
        mine_ref[...] = low
        other_ref[...] = high

    @pl.when(zp == 1)
    def _():
        mine_ref[...] = high
        other_ref[...] = low


def block_kernel(*refs):
    frames = 4
    sources, refs = refs[: 3 * frames], refs[3 * frames :]
    keep_ref, send_ref, n_ref, u_ref, qkv_ref, out_w_ref, sums_ref, out_sums_ref, sems = refs
    _, t, _, zh, x, core = place()
    pixels, channels = sources[0].shape
    width, depth = out_w_ref.shape[0], channels // HEADS
    rows = sources[-1].shape[0]
    up_copies, row_copies, qkv_copies = [], [], []
    for k in range(frames):
        row_copies.append(pltpu.make_async_copy(sources[k], n_ref.at[t ^ k], sems.at[k]))
        up_copies.append(
            pltpu.make_async_copy(sources[frames + k], u_ref.at[t ^ k], sems.at[frames + k])
        )
    shards = sources[2 * frames :]
    for k, shard in enumerate(shards):
        f = (2 * x + core) ^ (2 * (k & 1) + (k >> 1))
        qkv_copies.append(
            pltpu.make_async_copy(
                shard.at[:, pl.ds(0, 3 * width)],
                qkv_ref.at[pl.ds(pl.multiple_of(f * rows, 128), rows)],
                sems.at[2 * frames + k],
            )
        )

    def out_copy(shard, k):
        start = pl.multiple_of((core ^ k) * rows, 128)
        return pltpu.make_async_copy(
            shard.at[:, pl.ds(3 * width, channels)],
            out_w_ref.at[pl.ds(start, rows)],
            sems.at[3 * frames + k],
        )

    start_all(row_copies + qkv_copies + up_copies)
    for k in range(2):

        @pl.when(x == zh)
        def _(k=k):
            out_copy(shards[2 * k], k).start()

        @pl.when(x != zh)
        def _(k=k):
            out_copy(shards[2 * k + 1], k).start()

    for copy in row_copies + qkv_copies:
        copy.wait()
    normed = n_ref[...].reshape(frames * pixels, channels)
    qkv = jnp.dot(normed, qkv_ref[...], preferred_element_type=jnp.float32).astype(jnp.bfloat16)
    for copy in up_copies + [out_copy(shards[2 * k], k) for k in range(2)]:
        copy.wait()
    upstream = u_ref[...].reshape(frames * pixels, channels)
    grads = lax.dot_general(
        upstream, out_w_ref[...], (((1,), (1,)), ((), ())), preferred_element_type=jnp.float32
    ).astype(jnp.bfloat16)

    def part(values, frame, third=0):
        rows = values[frame * pixels : (frame + 1) * pixels]
        return rows[:, third * width : (third + 1) * width].astype(jnp.float32)

    q = [part(qkv, i, 0) for i in range(frames)]
    k = [part(qkv, i, 1) for i in range(frames)]
    v = [part(qkv, i, 2) for i in range(frames)]
    g = [part(grads, i) for i in range(frames)]
    row_head = lax.broadcasted_iota(jnp.int32, (width, width), 0) // depth
    col_head = lax.broadcasted_iota(jnp.int32, (width, width), 1) // depth
    same = jnp.where(row_head == col_head, 1.0, 0.0).astype(jnp.bfloat16)

    def head_sums(products):
        stacked = jnp.concatenate(products, axis=0)
        high = stacked.astype(jnp.bfloat16)
        low = (stacked - high.astype(jnp.float32)).astype(jnp.bfloat16)
        total = jnp.dot(high, same, preferred_element_type=jnp.float32)
        total = total + jnp.dot(low, same, preferred_element_type=jnp.float32)
        return [total[i * pixels : (i + 1) * pixels] for i in range(len(products))]

    def rounded(values):
        return values.astype(jnp.bfloat16).astype(jnp.float32)

    attended, dq = [], []
    dk, dv = [None] * frames, [None] * frames

    def plus(total, term):
        return term if total is None else total + term

    for i in range(frames):
        scores = head_sums([q[i] * k[u] for u in range(i + 1)])
        scores = [s * 0.125 for s in scores]
        largest = scores[0]
        for s in scores[1:]:
            largest = jnp.maximum(largest, s)
        powers = [jnp.exp(s - largest) for s in scores]
        total = powers[0]
        for p in powers[1:]:
            total = total + p
        scale = 1.0 / total
        weights = [rounded(p * scale) for p in powers]
        dprob = head_sums([g[i] * v[u] for u in range(i + 1)])
        delta = weights[0] * dprob[0]
        for u in range(1, i + 1):
            delta = delta + weights[u] * dprob[u]
        seen, grad_q = None, None
        for u in range(i + 1):
            ds = rounded(weights[u] * (dprob[u] - delta) * 0.125)
            seen = plus(seen, weights[u] * v[u])
            grad_q = plus(grad_q, ds * k[u])
            dk[u] = plus(dk[u], ds * q[i])
            dv[u] = plus(dv[u], weights[u] * g[i])
        attended.append(seen.astype(jnp.bfloat16))
        dq.append(grad_q.astype(jnp.bfloat16))
    thirds = (dq, [d.astype(jnp.bfloat16) for d in dk], [d.astype(jnp.bfloat16) for d in dv])

    def over_rows(lhs, rhs):
        return lax.dot_general(
            lhs, rhs, (((0,), (0,)), ((), ())), preferred_element_type=jnp.float32
        )

    for m, pieces in enumerate(thirds):
        grad = over_rows(normed, jnp.concatenate(pieces, axis=0))
        for lane in range(0, width, 128):
            sums_ref[lane // 128, pl.ds(m, channels, stride=3), :] = grad[:, lane : lane + 128]
    out_sums_ref[...] = over_rows(jnp.concatenate(attended, axis=0), upstream)

    block = 64
    for x in range(2):
        for y in range(2):
            for zp in range(2):
                slot = (x * 2 + y) * 2 + zp
                for side, ref in ((core, keep_ref), (1 - core, send_ref)):
                    if y == 1 and zp == 1:
                        start = pl.multiple_of((2 * x + side) * block, block)
                        rows = out_sums_ref[pl.ds(start, block), :]
                        pieces = (rows[:, :width], rows[:, width:])
                    else:
                        pieces = []
                        for low in range(2):
                            index = y * 16 + (2 * zp + low) * 4 + 2 * x + side
                            start = pl.multiple_of(index * block, block)
                            pieces.append(
                                jnp.concatenate(
                                    [
                                        sums_ref[lane, pl.ds(start, block), :]
                                        for lane in range(width // 128)
                                    ],
                                    axis=1,
                                )
                            )
                    for low in range(2):
                        ref[slot, low * block : (low + 1) * block, :] = pieces[low].astype(ref.dtype)


def join_kernel(total_ref, got_ref, out_ref):
    y, _, zp, zh, _, _ = place()
    lanes = out_ref.shape[1]
    rows, width = got_ref.shape
    is_out = (y == 1) & (zp == 1)
    got = got_ref[...].astype(jnp.float32)
    for side in range(2):
        joined = jnp.where(is_out | (zh == side), total_ref[side], got)
        for lane in range(0, width, lanes):
            first = (side * width + lane) // lanes
            step = 2 * width // lanes
            out_ref[pl.ds(first, rows, stride=step), :] = joined[:, lane : lane + lanes]


def split_form(features, neighbours, conv_taps, norm_gain, qkv_weight, out_weight, cotangent):
    own = features[0, 0]
    pixels, channels = own.shape
    half, width, block = pixels // 2, channels // 2, channels // HEADS
    y, _, zp, zh, x, _ = place()
    narrow_type = jnp.bfloat16
    anywhere = pl.BlockSpec(memory_space=pl.ANY)
    in_vmem = pl.BlockSpec(memory_space=VMEM)
    piece = jax.ShapeDtypeStruct((half, channels), narrow_type)

    band = swap(own, "blk", 1)
    up_mine, up_other, cut = pl.pallas_call(
        prep_kernel,
        out_shape=(
            piece,
            piece,
            jax.ShapeDtypeStruct((qkv_weight.shape[0], 3 * width + channels), narrow_type),
        ),
        in_specs=[anywhere] * 3,
        out_specs=(in_vmem,) * 3,
        scratch_shapes=[pltpu.SemaphoreType.DMA((6,))],
        name="prep",
    )(cotangent[0, 0], qkv_weight, out_weight)

    cut_x = swap(cut, "fsdp", 2)
    up_2 = swap(up_other, "tm", 2)
    up_1 = swap(up_mine, "tm", 1)
    n_mine, n_other = pl.pallas_call(
        conv_kernel,
        out_shape=(piece, piece),
        in_specs=[anywhere] * 5,
        out_specs=(in_vmem,) * 2,
        scratch_shapes=[
            pltpu.VMEM((neighbours.shape[1], pixels), jnp.int32),
            pltpu.VMEM((2 * pixels, channels), narrow_type),
            pltpu.VMEM(conv_taps.shape, jnp.float32),
            pltpu.VMEM((1, channels), jnp.float32),
            pltpu.SemaphoreType.DMA((5,)),
        ],
        compiler_params=pltpu.CompilerParams(vmem_limit_bytes=16 << 20),
        name="conv",
    )(neighbours.T, own, band, conv_taps, norm_gain.reshape(1, channels))
    row_3 = swap(n_other, "tm", 3)
    row_2 = swap(n_other, "tm", 2)
    row_1 = swap(n_mine, "tm", 1)
    up_3 = swap(up_2, "tm", 1)
    cut_c = swap(cut, "fsdp", 1)
    cut_xc = swap(cut_x, "fsdp", 1)

    keep, send = pl.pallas_call(
        block_kernel,
        out_shape=(
            jax.ShapeDtypeStruct((8, 2 * block, width), jnp.float32),
            jax.ShapeDtypeStruct((8, 2 * block, width), narrow_type),
        ),
        in_specs=[anywhere] * 12,
        out_specs=(in_vmem, in_vmem),
        scratch_shapes=[
            pltpu.VMEM((4, half, channels), narrow_type),
            pltpu.VMEM((4, half, channels), narrow_type),
            pltpu.VMEM((channels, 3 * width), narrow_type),
            pltpu.VMEM((width, channels), narrow_type),
            pltpu.VMEM((width // 128, 3 * channels, 128), jnp.float32),
            pltpu.VMEM((width, channels), jnp.float32),
            pltpu.SemaphoreType.DMA((14,)),
        ],
        compiler_params=pltpu.CompilerParams(vmem_limit_bytes=32 << 20),
        name="attend",
    )(
        *(n_mine, row_1, row_2, row_3), *(up_mine, up_1, up_2, up_3), *(cut, cut_x, cut_c, cut_xc)
    )

    def narrow(values):
        return values.astype(jnp.bfloat16)

    total = keep + swap(send, "fsdp", 1).astype(jnp.float32)
    total = total.reshape(2, 2, 2, 2 * block, width)
    first, second = total[..., : width // 2], total[..., width // 2 :]
    got_first = swap(narrow(pick(first, 1 - x, 0)), "fsdp", 2)
    got_second = swap(narrow(pick(second, 1 - y, 1)), "blk", 1)
    first = pick(first, x, 0) + got_first.astype(jnp.float32)
    second = pick(second, y, 1) + got_second.astype(jnp.float32)
    got_first = swap(narrow(pick(first, 1 - y, 0)), "blk", 1)
    got_second = swap(narrow(pick(second, 1 - x, 0)), "fsdp", 2)
    first = pick(first, y, 0) + got_first.astype(jnp.float32)
    second = pick(second, x, 0) + got_second.astype(jnp.float32)
    total = jnp.concatenate([first, second], axis=-1)
    total = pick(total, zp) + swap(narrow(pick(total, 1 - zp)), "tm", 2).astype(jnp.float32)
    total = total.reshape(2, block, width)
    got = swap(narrow(pick(total, 1 - zh)), "tm", 1)
    lanes = 128
    out = pl.pallas_call(
        join_kernel,
        out_shape=jax.ShapeDtypeStruct((block * channels // lanes, lanes), jnp.float32),
        in_specs=[in_vmem] * 2,
        out_specs=in_vmem,
        compiler_params=pltpu.CompilerParams(vmem_limit_bytes=4 << 20),
        name="join",
    )(total, got)
    return out.reshape(-1)


def with_halo(cells, sides, width):
    for axis, dim in sides:
        count = lax.axis_size(axis)
        ends = count - 1
        head = lax.slice_in_dim(cells, 0, width, axis=dim)
        tail = lax.slice_in_dim(cells, cells.shape[dim] - width, cells.shape[dim], axis=dim)
        cells = jnp.concatenate(
            [
                lax.ppermute(tail, axis, [(i, (i + 1) % count) for i in range(ends)]),
                cells,
                lax.ppermute(head, axis, [((i + 1) % count, i) for i in range(ends)]),
            ],
            axis=dim,
        )
    return cells


def halved(partial, axis, bit):
    count = lax.axis_size(axis)
    mine = (lax.axis_index(axis) >> bit) & 1
    keep = lax.dynamic_index_in_dim(partial, mine, 0, keepdims=False)
    send = lax.dynamic_index_in_dim(partial, 1 - mine, 0, keepdims=False)
    got = lax.ppermute(send.astype(jnp.bfloat16), axis, [(i, i ^ (1 << bit)) for i in range(count)])
    return keep + got.astype(jnp.float32)


def scattered_sum(summands):
    counts = [lax.axis_size(axis) for axis in ("blk", "tm", "fsdp")]
    bits = [count.bit_length() - 1 for count in counts]
    order = [("fsdp", bit) for bit in range(bits[2])]
    order += [("blk", bit) for bit in range(bits[0])]
    order += [("tm", bit) for bit in range(bits[1])]
    labels = [(axis, bit) for axis, many in zip(("blk", "tm", "fsdp"), bits) for bit in reversed(range(many))]
    partial = summands.reshape((2,) * len(labels) + (-1, 128))
    for axis, bit in order:
        place = labels.index((axis, bit))
        labels.pop(place)
        partial = halved(jnp.moveaxis(partial, place, 0), axis, bit)
    return partial.reshape(-1)


def rounded(values):
    return lax.optimization_barrier(values.astype(jnp.bfloat16)).astype(jnp.float32)


def attend_all(qkv_rows, grad_rows):
    frames, pixels, width = qkv_rows.shape
    channels = width // 3

    def split_heads(block):
        return block.reshape(frames, pixels, HEADS, channels // HEADS).astype(jnp.float32)

    queries = split_heads(qkv_rows[:, :, :channels])
    keys_all = split_heads(qkv_rows[:, :, channels : 2 * channels])
    values = split_heads(qkv_rows[:, :, 2 * channels :])
    grads = split_heads(grad_rows)
    scores = jnp.einsum("tpeh,upeh->petu", queries, keys_all) * 0.125
    causal = jnp.arange(frames)[:, None] >= jnp.arange(frames)[None, :]
    masked = jnp.where(causal, scores, -1e30)
    largest = jnp.max(masked, axis=-1, keepdims=True)
    totals = jnp.sum(jnp.exp(masked - largest), axis=-1, keepdims=True)
    log_total = largest + jnp.log(totals)
    weights = rounded(jnp.exp(masked - log_total))
    attended = jnp.einsum("petu,upeh->tpeh", weights, values)
    dprob = jnp.einsum("tpeh,upeh->petu", grads, values)
    delta = jnp.sum(weights * dprob, axis=-1, keepdims=True)
    dscore = rounded(weights * (dprob - delta) * 0.125)
    grad_query = jnp.einsum("petu,upeh->tpeh", dscore, keys_all)
    grad_key = jnp.einsum("petu,tpeh->upeh", dscore, queries)
    grad_value = jnp.einsum("petu,tpeh->upeh", weights, grads)
    joined = jnp.concatenate(
        [part.reshape(frames, pixels, channels) for part in (grad_query, grad_key, grad_value)],
        axis=-1,
    )
    return (
        attended.reshape(frames, pixels, channels).astype(jnp.bfloat16),
        joined.astype(jnp.bfloat16),
    )


def general_form(features, neighbours, conv_taps, norm_gain, qkv_weight, out_weight, cotangent):
    inputs = features[0, 0]
    upstream = cotangent[0, 0]
    pixels, channels = inputs.shape
    padded = with_halo(inputs, (("blk", 0),), HALO)
    first_pixel = lax.axis_index("blk") * pixels
    local_rows = neighbours - first_pixel + HALO
    inputs_f = inputs.astype(jnp.float32)
    spatial = conv_taps[0] * inputs_f
    for column in range(8):
        spatial = spatial + conv_taps[column + 1] * jnp.take(
            padded, local_rows[:, column], axis=0
        ).astype(jnp.float32)
    hidden_f = rounded(inputs_f + spatial)
    inverse = lax.rsqrt(jnp.mean(hidden_f * hidden_f, axis=-1, keepdims=True) + 1e-05)
    normed = (hidden_f * inverse * norm_gain).astype(jnp.bfloat16)
    full_qkv, full_out = (
        lax.all_gather(qkv_weight, "fsdp", axis=0, tiled=True),
        lax.all_gather(out_weight, "fsdp", axis=0, tiled=True),
    )
    att_grads = jnp.dot(upstream, full_out.T, preferred_element_type=jnp.float32).astype(
        jnp.bfloat16
    )
    swap_normed, swap_grads, swap_upstream = (
        lax.all_to_all(normed[None], "tm", split_axis=1, concat_axis=0, tiled=True),
        lax.all_to_all(att_grads[None], "tm", split_axis=1, concat_axis=0, tiled=True),
        lax.all_to_all(upstream[None], "tm", split_axis=1, concat_axis=0, tiled=True),
    )
    frames = swap_normed.shape[0]
    few_pixels = swap_normed.shape[1]
    flat_normed = swap_normed.reshape(-1, channels)
    qkv_rows = jnp.dot(flat_normed, full_qkv, preferred_element_type=jnp.float32).astype(
        jnp.bfloat16
    )
    qkv_rows = qkv_rows.reshape(frames, few_pixels, 3 * channels)
    attended_x, dqkv_x = attend_all(qkv_rows, swap_grads)
    grad_in = jnp.einsum(
        "pc,pd->cd",
        flat_normed,
        dqkv_x.reshape(-1, 3 * channels),
        preferred_element_type=jnp.float32,
    )
    grad_out = jnp.einsum(
        "pc,pd->cd",
        attended_x.reshape(-1, channels),
        swap_upstream.reshape(-1, channels),
        preferred_element_type=jnp.float32,
    )
    summands = jnp.concatenate([grad_in.reshape(-1), grad_out.reshape(-1)])
    return scattered_sum(summands)


def solution(mesh):
    sizes = mesh.shape

    def per_device(*arrays):
        pixels, channels = arrays[0].shape[-2:]
        devices = sizes["blk"] * sizes["tm"] * sizes["fsdp"]
        fits = (
            sizes["blk"] == 2
            and sizes["tm"] == sizes["fsdp"] == arrays[0].shape[0] * 4
            and devices == 4 * HEADS
            and pixels >= HALO
            and pixels % 32 == 0
            and channels == 64 * HEADS
        )
        if not fits:
            return general_form(*arrays)
        return split_form(*arrays)

    return jax.shard_map(
        per_device,
        mesh=mesh,
        in_specs=(
            P("fsdp", "tm", "blk", None),
            P("blk", None),
            P(),
            P(),
            P("fsdp", None),
            P("fsdp", None),
            P("fsdp", "tm", "blk", None),
        ),
        out_specs=P(("blk", "tm", "fsdp")),
        check_vma=False,
    )
```

```python
import functools

import jax
import jax.numpy as jnp
from jax import lax
from jax.experimental import pallas as pl
from jax.experimental.pallas import tpu as pltpu
from jax.sharding import PartitionSpec as P


HEADS = 8
HALO = 130
VMEM = pltpu.MemorySpace.VMEM


def swap(values, axis, mask):
    return lax.ppermute(values, axis, [(i, i ^ mask) for i in range(lax.axis_size(axis))])


def pick(values, index, dim=0):
    return lax.dynamic_index_in_dim(values, index, dim, keepdims=False)


def place():
    t, f = lax.axis_index("tm"), lax.axis_index("fsdp")
    return lax.axis_index("blk"), t, t >> 1, t & 1, f >> 1, f & 1


def start_all(copies):
    for copy in copies:
        copy.start()


def prep_kernel(up_ref, qkv_ref, out_w_ref, mine_ref, other_ref, cut_ref, sems):
    _, _, zp, zh, _, _ = place()
    half = mine_ref.shape[0]
    width = out_w_ref.shape[1] // 2
    rows = lambda h: up_ref.at[pl.ds(pl.multiple_of(h * half, 16), half)]
    copies = [
        pltpu.make_async_copy(rows(zp), mine_ref, sems.at[0]),
        pltpu.make_async_copy(rows(1 - zp), other_ref, sems.at[1]),
        pltpu.make_async_copy(out_w_ref, cut_ref.at[:, pl.ds(3 * width, 2 * width)], sems.at[2]),
    ]
    for m in range(3):
        start = pl.multiple_of((2 * m + zh) * width, 128)
        copies.append(
            pltpu.make_async_copy(
                qkv_ref.at[:, pl.ds(start, width)],
                cut_ref.at[:, pl.ds(m * width, width)],
                sems.at[3 + m],
            )
        )
    start_all(copies)
    for copy in copies:
        copy.wait()


def conv_kernel(
    far, near_hbm, own_hbm, band_hbm, taps_hbm, gain_hbm, out_ref,
    near_ref, turned_ref, table_ref, taps_ref, gain_ref, sems,
):
    y, _, zp, _, _, _ = place()
    pixels, _ = own_hbm.shape
    half = pixels // 2
    begin = pl.multiple_of((1 - zp if far else zp) * half, 16)
    pairs = [
        (near_hbm, near_ref),
        (taps_hbm, taps_ref),
        (gain_hbm, gain_ref),
        (own_hbm, table_ref.at[pl.ds(0, pixels)]),
        (band_hbm, table_ref.at[pl.ds(pixels, pixels)]),
    ]
    copies = [pltpu.make_async_copy(a, b, sems.at[i]) for i, (a, b) in enumerate(pairs)]
    start_all(copies)
    copies[0].wait()
    turned_ref[...] = near_ref[...].T
    near = turned_ref[pl.ds(begin, half), :]
    neighbours = near.shape[1]
    local = near - y * pixels
    local = jnp.where(local < 0, local + 2 * pixels, local)
    slots = lax.broadcasted_iota(jnp.int32, (half, 2 * pixels), 1)
    chosen = jnp.concatenate(
        [
            jnp.where(local[:, k : k + 1] == slots, 1.0, 0.0).astype(jnp.bfloat16)
            for k in range(neighbours)
        ],
        axis=0,
    )
    for copy in copies[1:]:
        copy.wait()
    gathered = jnp.dot(chosen, table_ref[...], preferred_element_type=jnp.float32)
    own = table_ref[pl.ds(begin, half), :].astype(jnp.float32)
    spatial = taps_ref[0:1, :] * own
    for k in range(neighbours):
        spatial = spatial + taps_ref[k + 1 : k + 2, :] * gathered[k * half : (k + 1) * half]
    hidden = (own + spatial).astype(jnp.bfloat16).astype(jnp.float32)
    inverse = lax.rsqrt(jnp.mean(hidden * hidden, axis=-1, keepdims=True) + 1e-05)
    out_ref[...] = (hidden * inverse * gain_ref[...]).astype(jnp.bfloat16)


def block_kernel(*refs):
    frames = 4
    row_refs, pair_refs, shards, refs = refs[:4], refs[4:6], refs[6:10], refs[10:]
    keep_ref, send_ref, n_ref, u_ref, qkv_ref, out_w_ref, sums_ref, out_sums_ref, sems = refs
    _, t, _, zh, x, core = place()
    pixels, channels = row_refs[0].shape
    width, depth = out_w_ref.shape[0], channels // HEADS
    rows = shards[0].shape[0]
    up_copies, row_copies, qkv_copies = [], [], []
    for k in range(frames):
        row_copies.append(pltpu.make_async_copy(row_refs[k], n_ref.at[t ^ k], sems.at[k]))
        up_copies.append(
            pltpu.make_async_copy(
                pair_refs[k & 1].at[k >> 1], u_ref.at[t ^ k], sems.at[frames + k]
            )
        )
    for k, shard in enumerate(shards):
        f = (2 * x + core) ^ (2 * (k & 1) + (k >> 1))
        qkv_copies.append(
            pltpu.make_async_copy(
                shard.at[:, pl.ds(0, 3 * width)],
                qkv_ref.at[pl.ds(pl.multiple_of(f * rows, 128), rows)],
                sems.at[2 * frames + k],
            )
        )

    def out_copy(shard, k):
        start = pl.multiple_of((core ^ k) * rows, 128)
        return pltpu.make_async_copy(
            shard.at[:, pl.ds(3 * width, channels)],
            out_w_ref.at[pl.ds(start, rows)],
            sems.at[3 * frames + k],
        )

    start_all(row_copies + qkv_copies + up_copies)
    for k in range(2):

        @pl.when(x == zh)
        def _(k=k):
            out_copy(shards[2 * k], k).start()

        @pl.when(x != zh)
        def _(k=k):
            out_copy(shards[2 * k + 1], k).start()

    for copy in row_copies + qkv_copies:
        copy.wait()
    normed = n_ref[...].reshape(frames * pixels, channels)
    qkv = jnp.dot(normed, qkv_ref[...], preferred_element_type=jnp.float32).astype(jnp.bfloat16)
    for copy in up_copies + [out_copy(shards[2 * k], k) for k in range(2)]:
        copy.wait()
    upstream = u_ref[...].reshape(frames * pixels, channels)
    grads = lax.dot_general(
        upstream, out_w_ref[...], (((1,), (1,)), ((), ())), preferred_element_type=jnp.float32
    ).astype(jnp.bfloat16)

    def part(values, frame, third=0):
        rows = values[frame * pixels : (frame + 1) * pixels]
        return rows[:, third * width : (third + 1) * width].astype(jnp.float32)

    q = [part(qkv, i, 0) for i in range(frames)]
    k = [part(qkv, i, 1) for i in range(frames)]
    v = [part(qkv, i, 2) for i in range(frames)]
    g = [part(grads, i) for i in range(frames)]
    row_head = lax.broadcasted_iota(jnp.int32, (width, width), 0) // depth
    col_head = lax.broadcasted_iota(jnp.int32, (width, width), 1) // depth
    same = jnp.where(row_head == col_head, 1.0, 0.0).astype(jnp.bfloat16)

    def head_sums(products):
        stacked = jnp.concatenate(products, axis=0)
        high = stacked.astype(jnp.bfloat16)
        low = (stacked - high.astype(jnp.float32)).astype(jnp.bfloat16)
        total = jnp.dot(high, same, preferred_element_type=jnp.float32)
        total = total + jnp.dot(low, same, preferred_element_type=jnp.float32)
        return [total[i * pixels : (i + 1) * pixels] for i in range(len(products))]

    def rounded(values):
        return values.astype(jnp.bfloat16).astype(jnp.float32)

    attended, dq = [], []
    dk, dv = [None] * frames, [None] * frames

    def plus(total, term):
        return term if total is None else total + term

    for i in range(frames):
        scores = head_sums([q[i] * k[u] for u in range(i + 1)])
        scores = [s * 0.125 for s in scores]
        largest = scores[0]
        for s in scores[1:]:
            largest = jnp.maximum(largest, s)
        powers = [jnp.exp(s - largest) for s in scores]
        total = powers[0]
        for p in powers[1:]:
            total = total + p
        scale = 1.0 / total
        weights = [rounded(p * scale) for p in powers]
        dprob = head_sums([g[i] * v[u] for u in range(i + 1)])
        delta = weights[0] * dprob[0]
        for u in range(1, i + 1):
            delta = delta + weights[u] * dprob[u]
        seen, grad_q = None, None
        for u in range(i + 1):
            ds = rounded(weights[u] * (dprob[u] - delta) * 0.125)
            seen = plus(seen, weights[u] * v[u])
            grad_q = plus(grad_q, ds * k[u])
            dk[u] = plus(dk[u], ds * q[i])
            dv[u] = plus(dv[u], weights[u] * g[i])
        attended.append(seen.astype(jnp.bfloat16))
        dq.append(grad_q.astype(jnp.bfloat16))
    thirds = (dq, [d.astype(jnp.bfloat16) for d in dk], [d.astype(jnp.bfloat16) for d in dv])

    def over_rows(lhs, rhs):
        return lax.dot_general(
            lhs, rhs, (((0,), (0,)), ((), ())), preferred_element_type=jnp.float32
        )

    for m, pieces in enumerate(thirds):
        grad = over_rows(normed, jnp.concatenate(pieces, axis=0))
        for lane in range(0, width, 128):
            sums_ref[lane // 128, pl.ds(m, channels, stride=3), :] = grad[:, lane : lane + 128]
    out_sums_ref[...] = over_rows(jnp.concatenate(attended, axis=0), upstream)

    block = 64
    for x in range(2):
        for y in range(2):
            for zp in range(2):
                slot = (x * 2 + y) * 2 + zp
                for side, ref in ((core, keep_ref), (1 - core, send_ref)):
                    if y == 1 and zp == 1:
                        start = pl.multiple_of((2 * x + side) * block, block)
                        rows = out_sums_ref[pl.ds(start, block), :]
                        pieces = (rows[:, :width], rows[:, width:])
                    else:
                        pieces = []
                        for low in range(2):
                            index = y * 16 + (2 * zp + low) * 4 + 2 * x + side
                            start = pl.multiple_of(index * block, block)
                            pieces.append(
                                jnp.concatenate(
                                    [
                                        sums_ref[lane, pl.ds(start, block), :]
                                        for lane in range(width // 128)
                                    ],
                                    axis=1,
                                )
                            )
                    for low in range(2):
                        ref[slot, low * block : (low + 1) * block, :] = pieces[low].astype(ref.dtype)


def join_kernel(total_ref, got_ref, out_ref):
    y, _, zp, zh, _, _ = place()
    lanes = out_ref.shape[1]
    rows, width = got_ref.shape
    is_out = (y == 1) & (zp == 1)
    got = got_ref[...].astype(jnp.float32)
    for side in range(2):
        joined = jnp.where(is_out | (zh == side), total_ref[side], got)
        for lane in range(0, width, lanes):
            first = (side * width + lane) // lanes
            step = 2 * width // lanes
            out_ref[pl.ds(first, rows, stride=step), :] = joined[:, lane : lane + lanes]


def split_form(features, neighbours, conv_taps, norm_gain, qkv_weight, out_weight, cotangent):
    own = features[0, 0]
    pixels, channels = own.shape
    half, width, block = pixels // 2, channels // 2, channels // HEADS
    y, _, zp, zh, x, _ = place()
    narrow_type = jnp.bfloat16
    anywhere = pl.BlockSpec(memory_space=pl.ANY)
    in_vmem = pl.BlockSpec(memory_space=VMEM)
    piece = jax.ShapeDtypeStruct((half, channels), narrow_type)

    band = swap(own, "blk", 1)
    up_mine, up_other, cut = pl.pallas_call(
        prep_kernel,
        out_shape=(
            piece,
            piece,
            jax.ShapeDtypeStruct((qkv_weight.shape[0], 3 * width + channels), narrow_type),
        ),
        in_specs=[anywhere] * 3,
        out_specs=(in_vmem,) * 3,
        scratch_shapes=[pltpu.SemaphoreType.DMA((6,))],
        name="prep",
    )(cotangent[0, 0], qkv_weight, out_weight)

    cut_x = swap(cut, "fsdp", 2)
    up_2 = swap(up_other, "tm", 2)

    def conv(far):
        return pl.pallas_call(
            functools.partial(conv_kernel, far),
            out_shape=piece,
            in_specs=[anywhere] * 5,
            out_specs=in_vmem,
            scratch_shapes=[
                pltpu.VMEM((neighbours.shape[1], pixels), jnp.int32),
                pltpu.VMEM((pixels, neighbours.shape[1]), jnp.int32),
                pltpu.VMEM((2 * pixels, channels), narrow_type),
                pltpu.VMEM(conv_taps.shape, jnp.float32),
                pltpu.VMEM((1, channels), jnp.float32),
                pltpu.SemaphoreType.DMA((5,)),
            ],
            compiler_params=pltpu.CompilerParams(vmem_limit_bytes=16 << 20),
            name="conv_far" if far else "conv_near",
        )(neighbours.T, own, band, conv_taps, norm_gain.reshape(1, channels))

    n_other = conv(True)
    row_3 = swap(n_other, "tm", 3)
    row_2 = swap(n_other, "tm", 2)
    n_mine = conv(False)
    row_1 = swap(n_mine, "tm", 1)
    up_own = jnp.stack([up_mine, up_2])
    up_got = swap(up_own, "tm", 1)
    cut_c = swap(cut, "fsdp", 1)
    cut_xc = swap(cut_x, "fsdp", 1)

    keep, send = pl.pallas_call(
        block_kernel,
        out_shape=(
            jax.ShapeDtypeStruct((8, 2 * block, width), jnp.float32),
            jax.ShapeDtypeStruct((8, 2 * block, width), narrow_type),
        ),
        in_specs=[anywhere] * 10,
        out_specs=(in_vmem, in_vmem),
        scratch_shapes=[
            pltpu.VMEM((4, half, channels), narrow_type),
            pltpu.VMEM((4, half, channels), narrow_type),
            pltpu.VMEM((channels, 3 * width), narrow_type),
            pltpu.VMEM((width, channels), narrow_type),
            pltpu.VMEM((width // 128, 3 * channels, 128), jnp.float32),
            pltpu.VMEM((width, channels), jnp.float32),
            pltpu.SemaphoreType.DMA((14,)),
        ],
        compiler_params=pltpu.CompilerParams(vmem_limit_bytes=32 << 20),
        name="attend",
    )(
        n_mine, row_1, row_2, row_3, up_own, up_got, cut, cut_x, cut_c, cut_xc
    )

    def narrow(values):
        return values.astype(jnp.bfloat16)

    total = keep + swap(send, "fsdp", 1).astype(jnp.float32)
    total = total.reshape(2, 2, 2, 2 * block, width)
    first, second = total[..., : width // 2], total[..., width // 2 :]
    got_first = swap(narrow(pick(first, 1 - x, 0)), "fsdp", 2)
    got_second = swap(narrow(pick(second, 1 - y, 1)), "blk", 1)
    first = pick(first, x, 0) + got_first.astype(jnp.float32)
    second = pick(second, y, 1) + got_second.astype(jnp.float32)
    got_first = swap(narrow(pick(first, 1 - y, 0)), "blk", 1)
    got_second = swap(narrow(pick(second, 1 - x, 0)), "fsdp", 2)
    first = pick(first, y, 0) + got_first.astype(jnp.float32)
    second = pick(second, x, 0) + got_second.astype(jnp.float32)
    total = jnp.concatenate([first, second], axis=-1)
    total = pick(total, zp) + swap(narrow(pick(total, 1 - zp)), "tm", 2).astype(jnp.float32)
    total = total.reshape(2, block, width)
    got = swap(narrow(pick(total, 1 - zh)), "tm", 1)
    lanes = 128
    out = pl.pallas_call(
        join_kernel,
        out_shape=jax.ShapeDtypeStruct((block * channels // lanes, lanes), jnp.float32),
        in_specs=[in_vmem] * 2,
        out_specs=in_vmem,
        compiler_params=pltpu.CompilerParams(vmem_limit_bytes=4 << 20),
        name="join",
    )(total, got)
    return out.reshape(-1)


def with_halo(cells, sides, width):
    for axis, dim in sides:
        count = lax.axis_size(axis)
        ends = count - 1
        head = lax.slice_in_dim(cells, 0, width, axis=dim)
        tail = lax.slice_in_dim(cells, cells.shape[dim] - width, cells.shape[dim], axis=dim)
        cells = jnp.concatenate(
            [
                lax.ppermute(tail, axis, [(i, (i + 1) % count) for i in range(ends)]),
                cells,
                lax.ppermute(head, axis, [((i + 1) % count, i) for i in range(ends)]),
            ],
            axis=dim,
        )
    return cells


def halved(partial, axis, bit):
    count = lax.axis_size(axis)
    mine = (lax.axis_index(axis) >> bit) & 1
    keep = lax.dynamic_index_in_dim(partial, mine, 0, keepdims=False)
    send = lax.dynamic_index_in_dim(partial, 1 - mine, 0, keepdims=False)
    got = lax.ppermute(send.astype(jnp.bfloat16), axis, [(i, i ^ (1 << bit)) for i in range(count)])
    return keep + got.astype(jnp.float32)


def scattered_sum(summands):
    counts = [lax.axis_size(axis) for axis in ("blk", "tm", "fsdp")]
    bits = [count.bit_length() - 1 for count in counts]
    order = [("fsdp", bit) for bit in range(bits[2])]
    order += [("blk", bit) for bit in range(bits[0])]
    order += [("tm", bit) for bit in range(bits[1])]
    labels = [(axis, bit) for axis, many in zip(("blk", "tm", "fsdp"), bits) for bit in reversed(range(many))]
    partial = summands.reshape((2,) * len(labels) + (-1, 128))
    for axis, bit in order:
        place = labels.index((axis, bit))
        labels.pop(place)
        partial = halved(jnp.moveaxis(partial, place, 0), axis, bit)
    return partial.reshape(-1)


def rounded(values):
    return lax.optimization_barrier(values.astype(jnp.bfloat16)).astype(jnp.float32)


def attend_all(qkv_rows, grad_rows):
    frames, pixels, width = qkv_rows.shape
    channels = width // 3

    def split_heads(block):
        return block.reshape(frames, pixels, HEADS, channels // HEADS).astype(jnp.float32)

    queries = split_heads(qkv_rows[:, :, :channels])
    keys_all = split_heads(qkv_rows[:, :, channels : 2 * channels])
    values = split_heads(qkv_rows[:, :, 2 * channels :])
    grads = split_heads(grad_rows)
    scores = jnp.einsum("tpeh,upeh->petu", queries, keys_all) * 0.125
    causal = jnp.arange(frames)[:, None] >= jnp.arange(frames)[None, :]
    masked = jnp.where(causal, scores, -1e30)
    largest = jnp.max(masked, axis=-1, keepdims=True)
    totals = jnp.sum(jnp.exp(masked - largest), axis=-1, keepdims=True)
    log_total = largest + jnp.log(totals)
    weights = rounded(jnp.exp(masked - log_total))
    attended = jnp.einsum("petu,upeh->tpeh", weights, values)
    dprob = jnp.einsum("tpeh,upeh->petu", grads, values)
    delta = jnp.sum(weights * dprob, axis=-1, keepdims=True)
    dscore = rounded(weights * (dprob - delta) * 0.125)
    grad_query = jnp.einsum("petu,upeh->tpeh", dscore, keys_all)
    grad_key = jnp.einsum("petu,tpeh->upeh", dscore, queries)
    grad_value = jnp.einsum("petu,tpeh->upeh", weights, grads)
    joined = jnp.concatenate(
        [part.reshape(frames, pixels, channels) for part in (grad_query, grad_key, grad_value)],
        axis=-1,
    )
    return (
        attended.reshape(frames, pixels, channels).astype(jnp.bfloat16),
        joined.astype(jnp.bfloat16),
    )


def general_form(features, neighbours, conv_taps, norm_gain, qkv_weight, out_weight, cotangent):
    inputs = features[0, 0]
    upstream = cotangent[0, 0]
    pixels, channels = inputs.shape
    padded = with_halo(inputs, (("blk", 0),), HALO)
    first_pixel = lax.axis_index("blk") * pixels
    local_rows = neighbours - first_pixel + HALO
    inputs_f = inputs.astype(jnp.float32)
    spatial = conv_taps[0] * inputs_f
    for column in range(8):
        spatial = spatial + conv_taps[column + 1] * jnp.take(
            padded, local_rows[:, column], axis=0
        ).astype(jnp.float32)
    hidden_f = rounded(inputs_f + spatial)
    inverse = lax.rsqrt(jnp.mean(hidden_f * hidden_f, axis=-1, keepdims=True) + 1e-05)
    normed = (hidden_f * inverse * norm_gain).astype(jnp.bfloat16)
    full_qkv, full_out = (
        lax.all_gather(qkv_weight, "fsdp", axis=0, tiled=True),
        lax.all_gather(out_weight, "fsdp", axis=0, tiled=True),
    )
    att_grads = jnp.dot(upstream, full_out.T, preferred_element_type=jnp.float32).astype(
        jnp.bfloat16
    )
    swap_normed, swap_grads, swap_upstream = (
        lax.all_to_all(normed[None], "tm", split_axis=1, concat_axis=0, tiled=True),
        lax.all_to_all(att_grads[None], "tm", split_axis=1, concat_axis=0, tiled=True),
        lax.all_to_all(upstream[None], "tm", split_axis=1, concat_axis=0, tiled=True),
    )
    frames = swap_normed.shape[0]
    few_pixels = swap_normed.shape[1]
    flat_normed = swap_normed.reshape(-1, channels)
    qkv_rows = jnp.dot(flat_normed, full_qkv, preferred_element_type=jnp.float32).astype(
        jnp.bfloat16
    )
    qkv_rows = qkv_rows.reshape(frames, few_pixels, 3 * channels)
    attended_x, dqkv_x = attend_all(qkv_rows, swap_grads)
    grad_in = jnp.einsum(
        "pc,pd->cd",
        flat_normed,
        dqkv_x.reshape(-1, 3 * channels),
        preferred_element_type=jnp.float32,
    )
    grad_out = jnp.einsum(
        "pc,pd->cd",
        attended_x.reshape(-1, channels),
        swap_upstream.reshape(-1, channels),
        preferred_element_type=jnp.float32,
    )
    summands = jnp.concatenate([grad_in.reshape(-1), grad_out.reshape(-1)])
    return scattered_sum(summands)


def solution(mesh):
    sizes = mesh.shape

    def per_device(*arrays):
        pixels, channels = arrays[0].shape[-2:]
        devices = sizes["blk"] * sizes["tm"] * sizes["fsdp"]
        fits = (
            sizes["blk"] == 2
            and sizes["tm"] == sizes["fsdp"] == arrays[0].shape[0] * 4
            and devices == 4 * HEADS
            and pixels >= HALO
            and pixels % 32 == 0
            and channels == 64 * HEADS
        )
        if not fits:
            return general_form(*arrays)
        return split_form(*arrays)

    return jax.shard_map(
        per_device,
        mesh=mesh,
        in_specs=(
            P("fsdp", "tm", "blk", None),
            P("blk", None),
            P(),
            P(),
            P("fsdp", None),
            P("fsdp", None),
            P("fsdp", "tm", "blk", None),
        ),
        out_specs=P(("blk", "tm", "fsdp")),
        check_vma=False,
    )
```

```python
import functools

import jax
import jax.numpy as jnp
from jax import lax
from jax.experimental import pallas as pl
from jax.experimental.pallas import tpu as pltpu
from jax.sharding import PartitionSpec as P


HEADS = 8
HALO = 130
VMEM = pltpu.MemorySpace.VMEM


def swap(values, axis, mask):
    return lax.ppermute(values, axis, [(i, i ^ mask) for i in range(lax.axis_size(axis))])


def pick(values, index, dim=0):
    return lax.dynamic_index_in_dim(values, index, dim, keepdims=False)


def place():
    t, f = lax.axis_index("tm"), lax.axis_index("fsdp")
    return lax.axis_index("blk"), t, t >> 1, t & 1, f >> 1, f & 1


def start_all(copies):
    for copy in copies:
        copy.start()


def prep_kernel(up_ref, qkv_ref, out_w_ref, mine_ref, other_ref, cut_ref, sems):
    _, _, zp, zh, _, _ = place()
    half = mine_ref.shape[0]
    width = out_w_ref.shape[1] // 2
    rows = lambda h: up_ref.at[pl.ds(pl.multiple_of(h * half, 16), half)]
    copies = [
        pltpu.make_async_copy(rows(zp), mine_ref, sems.at[0]),
        pltpu.make_async_copy(rows(1 - zp), other_ref, sems.at[1]),
        pltpu.make_async_copy(out_w_ref, cut_ref.at[:, pl.ds(3 * width, 2 * width)], sems.at[2]),
    ]
    for m in range(3):
        start = pl.multiple_of((2 * m + zh) * width, 128)
        copies.append(
            pltpu.make_async_copy(
                qkv_ref.at[:, pl.ds(start, width)],
                cut_ref.at[:, pl.ds(m * width, width)],
                sems.at[3 + m],
            )
        )
    start_all(copies)
    for copy in copies:
        copy.wait()


def conv_kernel(
    far, near_hbm, own_hbm, band_hbm, taps_hbm, gain_hbm, out_ref,
    near_ref, turned_ref, table_ref, taps_ref, gain_ref, sems,
):
    y, _, zp, _, _, _ = place()
    pixels, _ = own_hbm.shape
    half = pixels // 2
    begin = pl.multiple_of((1 - zp if far else zp) * half, 16)
    pairs = [
        (near_hbm, near_ref),
        (taps_hbm, taps_ref),
        (gain_hbm, gain_ref),
        (own_hbm, table_ref.at[pl.ds(0, pixels)]),
        (band_hbm, table_ref.at[pl.ds(pixels, pixels)]),
    ]
    copies = [pltpu.make_async_copy(a, b, sems.at[i]) for i, (a, b) in enumerate(pairs)]
    start_all(copies)
    copies[0].wait()
    turned_ref[...] = near_ref[...].T
    near = turned_ref[pl.ds(begin, half), :]
    neighbours = near.shape[1]
    local = near - y * pixels
    local = jnp.where(local < 0, local + 2 * pixels, local)
    slots = lax.broadcasted_iota(jnp.int32, (half, 2 * pixels), 1)
    chosen = jnp.concatenate(
        [
            jnp.where(local[:, k : k + 1] == slots, 1.0, 0.0).astype(jnp.bfloat16)
            for k in range(neighbours)
        ],
        axis=0,
    )
    for copy in copies[1:]:
        copy.wait()
    gathered = jnp.dot(chosen, table_ref[...], preferred_element_type=jnp.float32)
    own = table_ref[pl.ds(begin, half), :].astype(jnp.float32)
    spatial = taps_ref[0:1, :] * own
    for k in range(neighbours):
        spatial = spatial + taps_ref[k + 1 : k + 2, :] * gathered[k * half : (k + 1) * half]
    hidden = (own + spatial).astype(jnp.bfloat16).astype(jnp.float32)
    inverse = lax.rsqrt(jnp.mean(hidden * hidden, axis=-1, keepdims=True) + 1e-05)
    out_ref[...] = (hidden * inverse * gain_ref[...]).astype(jnp.bfloat16)


def head_sums(products, width):
    depth = width * 2 // HEADS
    row_head = lax.broadcasted_iota(jnp.int32, (width, width), 0) // depth
    col_head = lax.broadcasted_iota(jnp.int32, (width, width), 1) // depth
    same = jnp.where(row_head == col_head, 0.125, 0.0).astype(jnp.bfloat16)
    pixels = products[0].shape[0]
    stacked = jnp.concatenate(products, axis=0)
    high = stacked.astype(jnp.bfloat16)
    low = (stacked - high.astype(jnp.float32)).astype(jnp.bfloat16)
    total = jnp.dot(high, same, preferred_element_type=jnp.float32)
    total = total + jnp.dot(low, same, preferred_element_type=jnp.float32)
    return [total[i * pixels : (i + 1) * pixels] for i in range(len(products))]


def wide(ref, frame, third, width, pixels):
    rows = ref[frame * pixels : (frame + 1) * pixels, third * width : (third + 1) * width]
    return rows.astype(jnp.float32)


def shard_rows(k, rows):
    _, _, _, _, x, core = place()
    f = (2 * x + core) ^ (2 * (k & 1) + (k >> 1))
    return pl.ds(pl.multiple_of(f * rows, 128), rows)


def forward_kernel(*refs):
    frames = 4
    row_refs, shards, refs = refs[:4], refs[4:8], refs[8:]
    qkv_ref, weights_ref, attended_ref, n_ref, w_ref, sems = refs
    _, t, _, _, _, _ = place()
    pixels, channels = row_refs[0].shape
    width = channels // 2
    rows = shards[0].shape[0]
    copies = [pltpu.make_async_copy(row_refs[k], n_ref.at[t ^ k], sems.at[k]) for k in range(frames)]
    copies += [
        pltpu.make_async_copy(
            shards[k].at[:, pl.ds(0, 3 * width)], w_ref.at[shard_rows(k, rows)], sems.at[frames + k]
        )
        for k in range(4)
    ]
    start_all(copies)
    for copy in copies:
        copy.wait()
    normed = n_ref[...].reshape(frames * pixels, channels)
    qkv_ref[...] = jnp.dot(normed, w_ref[...], preferred_element_type=jnp.float32).astype(
        jnp.bfloat16
    )
    q, k, v = (
        [wide(qkv_ref, i, third, width, pixels) for i in range(frames)] for third in range(3)
    )
    slot = 0
    for i in range(frames):
        scores = head_sums([q[i] * k[u] for u in range(i + 1)], width)
        largest = scores[0]
        for s in scores[1:]:
            largest = jnp.maximum(largest, s)
        powers = [jnp.exp(s - largest) for s in scores]
        total = powers[0]
        for p in powers[1:]:
            total = total + p
        scale = 1.0 / total
        seen = None
        for u in range(i + 1):
            weights = (powers[u] * scale).astype(jnp.bfloat16)
            weights_ref[slot] = weights
            slot += 1
            term = weights.astype(jnp.float32) * v[u]
            seen = term if seen is None else seen + term
        attended_ref[i * pixels : (i + 1) * pixels, :] = seen.astype(jnp.bfloat16)


def backward_kernel(*refs):
    frames = 4
    row_refs, pair_refs, shards, refs = refs[:4], refs[4:6], refs[6:10], refs[10:]
    qkv_ref, weights_ref, attended_ref, refs = refs[0], refs[1], refs[2], refs[3:]
    keep_ref, send_ref, n_ref, u_ref, out_w_ref, sums_ref, out_sums_ref, sems = refs
    _, t, _, zh, x, core = place()
    pixels, channels = row_refs[0].shape
    width = out_w_ref.shape[0]
    rows = shards[0].shape[0]
    row_copies = [
        pltpu.make_async_copy(row_refs[k], n_ref.at[t ^ k], sems.at[k]) for k in range(frames)
    ]
    up_copies = [
        pltpu.make_async_copy(pair_refs[k & 1].at[k >> 1], u_ref.at[t ^ k], sems.at[frames + k])
        for k in range(frames)
    ]

    def out_copy(shard, k):
        start = pl.multiple_of((core ^ k) * rows, 128)
        return pltpu.make_async_copy(
            shard.at[:, pl.ds(3 * width, channels)],
            out_w_ref.at[pl.ds(start, rows)],
            sems.at[2 * frames + k],
        )

    start_all(up_copies)
    for k in range(2):

        @pl.when(x == zh)
        def _(k=k):
            out_copy(shards[2 * k], k).start()

        @pl.when(x != zh)
        def _(k=k):
            out_copy(shards[2 * k + 1], k).start()

    start_all(row_copies)
    for copy in up_copies + [out_copy(shards[2 * k], k) for k in range(2)]:
        copy.wait()
    upstream = u_ref[...].reshape(frames * pixels, channels)
    grads = lax.dot_general(
        upstream, out_w_ref[...], (((1,), (1,)), ((), ())), preferred_element_type=jnp.float32
    ).astype(jnp.bfloat16)
    g = [grads[i * pixels : (i + 1) * pixels].astype(jnp.float32) for i in range(frames)]
    q, k, v = (
        [wide(qkv_ref, i, third, width, pixels) for i in range(frames)] for third in range(3)
    )
    dq, dk, dv = [], [None] * frames, [None] * frames

    def plus(total, term):
        return term if total is None else total + term

    slot = 0
    for i in range(frames):
        dprob = head_sums([g[i] * v[u] for u in range(i + 1)], width)
        weights = [weights_ref[slot + u].astype(jnp.float32) for u in range(i + 1)]
        slot += i + 1
        delta = weights[0] * dprob[0]
        for u in range(1, i + 1):
            delta = delta + weights[u] * dprob[u]
        grad_q = None
        for u in range(i + 1):
            ds = (weights[u] * (dprob[u] - delta)).astype(jnp.bfloat16).astype(jnp.float32)
            grad_q = plus(grad_q, ds * k[u])
            dk[u] = plus(dk[u], ds * q[i])
            dv[u] = plus(dv[u], weights[u] * g[i])
        dq.append(grad_q.astype(jnp.bfloat16))
    for copy in row_copies:
        copy.wait()
    normed = n_ref[...].reshape(frames * pixels, channels)
    thirds = (dq, [d.astype(jnp.bfloat16) for d in dk], [d.astype(jnp.bfloat16) for d in dv])

    def over_rows(lhs, rhs):
        return lax.dot_general(
            lhs, rhs, (((0,), (0,)), ((), ())), preferred_element_type=jnp.float32
        )

    for m, pieces in enumerate(thirds):
        grad = over_rows(normed, jnp.concatenate(pieces, axis=0))
        for lane in range(0, width, 128):
            sums_ref[lane // 128, pl.ds(m, channels, stride=3), :] = grad[:, lane : lane + 128]
    out_sums_ref[...] = over_rows(attended_ref[...], upstream)

    block = 64
    for x in range(2):
        for y in range(2):
            for zp in range(2):
                slot = (x * 2 + y) * 2 + zp
                for side, ref in ((core, keep_ref), (1 - core, send_ref)):
                    if y == 1 and zp == 1:
                        start = pl.multiple_of((2 * x + side) * block, block)
                        rows = out_sums_ref[pl.ds(start, block), :]
                        pieces = (rows[:, :width], rows[:, width:])
                    else:
                        pieces = []
                        for low in range(2):
                            index = y * 16 + (2 * zp + low) * 4 + 2 * x + side
                            start = pl.multiple_of(index * block, block)
                            pieces.append(
                                jnp.concatenate(
                                    [
                                        sums_ref[lane, pl.ds(start, block), :]
                                        for lane in range(width // 128)
                                    ],
                                    axis=1,
                                )
                            )
                    for low in range(2):
                        ref[slot, low * block : (low + 1) * block, :] = pieces[low].astype(ref.dtype)


def join_kernel(total_ref, got_ref, out_ref):
    y, _, zp, zh, _, _ = place()
    lanes = out_ref.shape[1]
    rows, width = got_ref.shape
    is_out = (y == 1) & (zp == 1)
    got = got_ref[...].astype(jnp.float32)
    for side in range(2):
        joined = jnp.where(is_out | (zh == side), total_ref[side], got)
        for lane in range(0, width, lanes):
            first = (side * width + lane) // lanes
            step = 2 * width // lanes
            out_ref[pl.ds(first, rows, stride=step), :] = joined[:, lane : lane + lanes]


def split_form(features, neighbours, conv_taps, norm_gain, qkv_weight, out_weight, cotangent):
    own = features[0, 0]
    pixels, channels = own.shape
    half, width, block = pixels // 2, channels // 2, channels // HEADS
    y, _, zp, zh, x, _ = place()
    narrow_type = jnp.bfloat16
    anywhere = pl.BlockSpec(memory_space=pl.ANY)
    in_vmem = pl.BlockSpec(memory_space=VMEM)
    piece = jax.ShapeDtypeStruct((half, channels), narrow_type)

    band = swap(own, "blk", 1)
    up_mine, up_other, cut = pl.pallas_call(
        prep_kernel,
        out_shape=(
            piece,
            piece,
            jax.ShapeDtypeStruct((qkv_weight.shape[0], 3 * width + channels), narrow_type),
        ),
        in_specs=[anywhere] * 3,
        out_specs=(in_vmem,) * 3,
        scratch_shapes=[pltpu.SemaphoreType.DMA((6,))],
        name="prep",
    )(cotangent[0, 0], qkv_weight, out_weight)

    cut_x = swap(cut, "fsdp", 2)
    up_2 = swap(up_other, "tm", 2)

    def conv(far):
        return pl.pallas_call(
            functools.partial(conv_kernel, far),
            out_shape=piece,
            in_specs=[anywhere] * 5,
            out_specs=in_vmem,
            scratch_shapes=[
                pltpu.VMEM((neighbours.shape[1], pixels), jnp.int32),
                pltpu.VMEM((pixels, neighbours.shape[1]), jnp.int32),
                pltpu.VMEM((2 * pixels, channels), narrow_type),
                pltpu.VMEM(conv_taps.shape, jnp.float32),
                pltpu.VMEM((1, channels), jnp.float32),
                pltpu.SemaphoreType.DMA((5,)),
            ],
            compiler_params=pltpu.CompilerParams(vmem_limit_bytes=16 << 20),
            name="conv_far" if far else "conv_near",
        )(neighbours.T, own, band, conv_taps, norm_gain.reshape(1, channels))

    n_other = conv(True)
    row_3 = swap(n_other, "tm", 3)
    row_2 = swap(n_other, "tm", 2)
    n_mine = conv(False)
    row_1 = swap(n_mine, "tm", 1)
    up_own = jnp.stack([up_mine, up_2])
    up_got = swap(up_own, "tm", 1)
    cut_c = swap(cut, "fsdp", 1)
    cut_xc = swap(cut_x, "fsdp", 1)

    qkv, weights, attended = pl.pallas_call(
        forward_kernel,
        out_shape=(
            jax.ShapeDtypeStruct((4 * half, 3 * width), narrow_type),
            jax.ShapeDtypeStruct((10, half, width), narrow_type),
            jax.ShapeDtypeStruct((4 * half, width), narrow_type),
        ),
        in_specs=[anywhere] * 8,
        out_specs=(in_vmem,) * 3,
        scratch_shapes=[
            pltpu.VMEM((4, half, channels), narrow_type),
            pltpu.VMEM((channels, 3 * width), narrow_type),
            pltpu.SemaphoreType.DMA((8,)),
        ],
        compiler_params=pltpu.CompilerParams(vmem_limit_bytes=24 << 20),
        name="forward",
    )(n_mine, row_1, row_2, row_3, cut, cut_x, cut_c, cut_xc)
    keep, send = pl.pallas_call(
        backward_kernel,
        out_shape=(
            jax.ShapeDtypeStruct((8, 2 * block, width), jnp.float32),
            jax.ShapeDtypeStruct((8, 2 * block, width), narrow_type),
        ),
        in_specs=[anywhere] * 10 + [in_vmem] * 3,
        out_specs=(in_vmem, in_vmem),
        scratch_shapes=[
            pltpu.VMEM((4, half, channels), narrow_type),
            pltpu.VMEM((4, half, channels), narrow_type),
            pltpu.VMEM((width, channels), narrow_type),
            pltpu.VMEM((width // 128, 3 * channels, 128), jnp.float32),
            pltpu.VMEM((width, channels), jnp.float32),
            pltpu.SemaphoreType.DMA((10,)),
        ],
        compiler_params=pltpu.CompilerParams(vmem_limit_bytes=28 << 20),
        name="backward",
    )(
        n_mine, row_1, row_2, row_3, up_own, up_got, cut, cut_x, cut_c, cut_xc,
        qkv, weights, attended,
    )

    def narrow(values):
        return values.astype(jnp.bfloat16)

    total = keep + swap(send, "fsdp", 1).astype(jnp.float32)
    total = total.reshape(2, 2, 2, 2 * block, width)
    first, second = total[..., : width // 2], total[..., width // 2 :]
    got_first = swap(narrow(pick(first, 1 - x, 0)), "fsdp", 2)
    got_second = swap(narrow(pick(second, 1 - y, 1)), "blk", 1)
    first = pick(first, x, 0) + got_first.astype(jnp.float32)
    second = pick(second, y, 1) + got_second.astype(jnp.float32)
    got_first = swap(narrow(pick(first, 1 - y, 0)), "blk", 1)
    got_second = swap(narrow(pick(second, 1 - x, 0)), "fsdp", 2)
    first = pick(first, y, 0) + got_first.astype(jnp.float32)
    second = pick(second, x, 0) + got_second.astype(jnp.float32)
    total = jnp.concatenate([first, second], axis=-1)
    total = pick(total, zp) + swap(narrow(pick(total, 1 - zp)), "tm", 2).astype(jnp.float32)
    total = total.reshape(2, block, width)
    got = swap(narrow(pick(total, 1 - zh)), "tm", 1)
    lanes = 128
    out = pl.pallas_call(
        join_kernel,
        out_shape=jax.ShapeDtypeStruct((block * channels // lanes, lanes), jnp.float32),
        in_specs=[in_vmem] * 2,
        out_specs=in_vmem,
        compiler_params=pltpu.CompilerParams(vmem_limit_bytes=4 << 20),
        name="join",
    )(total, got)
    return out.reshape(-1)


def with_halo(cells, sides, width):
    for axis, dim in sides:
        count = lax.axis_size(axis)
        ends = count - 1
        head = lax.slice_in_dim(cells, 0, width, axis=dim)
        tail = lax.slice_in_dim(cells, cells.shape[dim] - width, cells.shape[dim], axis=dim)
        cells = jnp.concatenate(
            [
                lax.ppermute(tail, axis, [(i, (i + 1) % count) for i in range(ends)]),
                cells,
                lax.ppermute(head, axis, [((i + 1) % count, i) for i in range(ends)]),
            ],
            axis=dim,
        )
    return cells


def halved(partial, axis, bit):
    count = lax.axis_size(axis)
    mine = (lax.axis_index(axis) >> bit) & 1
    keep = lax.dynamic_index_in_dim(partial, mine, 0, keepdims=False)
    send = lax.dynamic_index_in_dim(partial, 1 - mine, 0, keepdims=False)
    got = lax.ppermute(send.astype(jnp.bfloat16), axis, [(i, i ^ (1 << bit)) for i in range(count)])
    return keep + got.astype(jnp.float32)


def scattered_sum(summands):
    counts = [lax.axis_size(axis) for axis in ("blk", "tm", "fsdp")]
    bits = [count.bit_length() - 1 for count in counts]
    order = [("fsdp", bit) for bit in range(bits[2])]
    order += [("blk", bit) for bit in range(bits[0])]
    order += [("tm", bit) for bit in range(bits[1])]
    labels = [(axis, bit) for axis, many in zip(("blk", "tm", "fsdp"), bits) for bit in reversed(range(many))]
    partial = summands.reshape((2,) * len(labels) + (-1, 128))
    for axis, bit in order:
        place = labels.index((axis, bit))
        labels.pop(place)
        partial = halved(jnp.moveaxis(partial, place, 0), axis, bit)
    return partial.reshape(-1)


def rounded(values):
    return lax.optimization_barrier(values.astype(jnp.bfloat16)).astype(jnp.float32)


def attend_all(qkv_rows, grad_rows):
    frames, pixels, width = qkv_rows.shape
    channels = width // 3

    def split_heads(block):
        return block.reshape(frames, pixels, HEADS, channels // HEADS).astype(jnp.float32)

    queries = split_heads(qkv_rows[:, :, :channels])
    keys_all = split_heads(qkv_rows[:, :, channels : 2 * channels])
    values = split_heads(qkv_rows[:, :, 2 * channels :])
    grads = split_heads(grad_rows)
    scores = jnp.einsum("tpeh,upeh->petu", queries, keys_all) * 0.125
    causal = jnp.arange(frames)[:, None] >= jnp.arange(frames)[None, :]
    masked = jnp.where(causal, scores, -1e30)
    largest = jnp.max(masked, axis=-1, keepdims=True)
    totals = jnp.sum(jnp.exp(masked - largest), axis=-1, keepdims=True)
    log_total = largest + jnp.log(totals)
    weights = rounded(jnp.exp(masked - log_total))
    attended = jnp.einsum("petu,upeh->tpeh", weights, values)
    dprob = jnp.einsum("tpeh,upeh->petu", grads, values)
    delta = jnp.sum(weights * dprob, axis=-1, keepdims=True)
    dscore = rounded(weights * (dprob - delta) * 0.125)
    grad_query = jnp.einsum("petu,upeh->tpeh", dscore, keys_all)
    grad_key = jnp.einsum("petu,tpeh->upeh", dscore, queries)
    grad_value = jnp.einsum("petu,tpeh->upeh", weights, grads)
    joined = jnp.concatenate(
        [part.reshape(frames, pixels, channels) for part in (grad_query, grad_key, grad_value)],
        axis=-1,
    )
    return (
        attended.reshape(frames, pixels, channels).astype(jnp.bfloat16),
        joined.astype(jnp.bfloat16),
    )


def general_form(features, neighbours, conv_taps, norm_gain, qkv_weight, out_weight, cotangent):
    inputs = features[0, 0]
    upstream = cotangent[0, 0]
    pixels, channels = inputs.shape
    padded = with_halo(inputs, (("blk", 0),), HALO)
    first_pixel = lax.axis_index("blk") * pixels
    local_rows = neighbours - first_pixel + HALO
    inputs_f = inputs.astype(jnp.float32)
    spatial = conv_taps[0] * inputs_f
    for column in range(8):
        spatial = spatial + conv_taps[column + 1] * jnp.take(
            padded, local_rows[:, column], axis=0
        ).astype(jnp.float32)
    hidden_f = rounded(inputs_f + spatial)
    inverse = lax.rsqrt(jnp.mean(hidden_f * hidden_f, axis=-1, keepdims=True) + 1e-05)
    normed = (hidden_f * inverse * norm_gain).astype(jnp.bfloat16)
    full_qkv, full_out = (
        lax.all_gather(qkv_weight, "fsdp", axis=0, tiled=True),
        lax.all_gather(out_weight, "fsdp", axis=0, tiled=True),
    )
    att_grads = jnp.dot(upstream, full_out.T, preferred_element_type=jnp.float32).astype(
        jnp.bfloat16
    )
    swap_normed, swap_grads, swap_upstream = (
        lax.all_to_all(normed[None], "tm", split_axis=1, concat_axis=0, tiled=True),
        lax.all_to_all(att_grads[None], "tm", split_axis=1, concat_axis=0, tiled=True),
        lax.all_to_all(upstream[None], "tm", split_axis=1, concat_axis=0, tiled=True),
    )
    frames = swap_normed.shape[0]
    few_pixels = swap_normed.shape[1]
    flat_normed = swap_normed.reshape(-1, channels)
    qkv_rows = jnp.dot(flat_normed, full_qkv, preferred_element_type=jnp.float32).astype(
        jnp.bfloat16
    )
    qkv_rows = qkv_rows.reshape(frames, few_pixels, 3 * channels)
    attended_x, dqkv_x = attend_all(qkv_rows, swap_grads)
    grad_in = jnp.einsum(
        "pc,pd->cd",
        flat_normed,
        dqkv_x.reshape(-1, 3 * channels),
        preferred_element_type=jnp.float32,
    )
    grad_out = jnp.einsum(
        "pc,pd->cd",
        attended_x.reshape(-1, channels),
        swap_upstream.reshape(-1, channels),
        preferred_element_type=jnp.float32,
    )
    summands = jnp.concatenate([grad_in.reshape(-1), grad_out.reshape(-1)])
    return scattered_sum(summands)


def solution(mesh):
    sizes = mesh.shape

    def per_device(*arrays):
        pixels, channels = arrays[0].shape[-2:]
        devices = sizes["blk"] * sizes["tm"] * sizes["fsdp"]
        fits = (
            sizes["blk"] == 2
            and sizes["tm"] == sizes["fsdp"] == arrays[0].shape[0] * 4
            and devices == 4 * HEADS
            and pixels >= HALO
            and pixels % 32 == 0
            and channels == 64 * HEADS
        )
        if not fits:
            return general_form(*arrays)
        return split_form(*arrays)

    return jax.shard_map(
        per_device,
        mesh=mesh,
        in_specs=(
            P("fsdp", "tm", "blk", None),
            P("blk", None),
            P(),
            P(),
            P("fsdp", None),
            P("fsdp", None),
            P("fsdp", "tm", "blk", None),
        ),
        out_specs=P(("blk", "tm", "fsdp")),
        check_vma=False,
    )
```

```python
import functools

import jax
import jax.numpy as jnp
from jax import lax
from jax.experimental import pallas as pl
from jax.experimental.pallas import tpu as pltpu
from jax.sharding import PartitionSpec as P


HEADS = 8
HALO = 130
VMEM = pltpu.MemorySpace.VMEM


def swap(values, axis, mask):
    return lax.ppermute(values, axis, [(i, i ^ mask) for i in range(lax.axis_size(axis))])


def shift(values, axis, mask, to_core=1):
    cores = lax.axis_size("fsdp")
    if axis == "fsdp":
        return lax.ppermute(values, axis, [(i, i ^ mask) for i in range(1, cores, 2)])
    pairs = [
        (i * cores + j, (i ^ mask) * cores + j + to_core - 1)
        for i in range(lax.axis_size(axis))
        for j in range(1, cores, 2)
    ]
    return lax.ppermute(values, (axis, "fsdp"), pairs)


def pick(values, index, dim=0):
    return lax.dynamic_index_in_dim(values, index, dim, keepdims=False)


def place():
    t, f = lax.axis_index("tm"), lax.axis_index("fsdp")
    return lax.axis_index("blk"), t, t >> 1, t & 1, f >> 1, f & 1


def start_all(copies):
    for copy in copies:
        copy.start()


def prep_kernel(up_ref, qkv_ref, out_w_ref, mine_ref, other_ref, cut_ref, sems):
    _, _, zp, zh, _, _ = place()
    half = mine_ref.shape[0]
    width = out_w_ref.shape[1] // 2
    rows = lambda h: up_ref.at[pl.ds(pl.multiple_of(h * half, 16), half)]
    copies = [
        pltpu.make_async_copy(rows(zp), mine_ref, sems.at[0]),
        pltpu.make_async_copy(rows(1 - zp), other_ref, sems.at[1]),
        pltpu.make_async_copy(out_w_ref, cut_ref.at[:, pl.ds(3 * width, 2 * width)], sems.at[2]),
    ]
    for m in range(3):
        start = pl.multiple_of((2 * m + zh) * width, 128)
        copies.append(
            pltpu.make_async_copy(
                qkv_ref.at[:, pl.ds(start, width)],
                cut_ref.at[:, pl.ds(m * width, width)],
                sems.at[3 + m],
            )
        )
    start_all(copies)
    for copy in copies:
        copy.wait()


def conv_kernel(
    far, near_hbm, own_hbm, band_hbm, taps_hbm, gain_hbm, out_ref,
    near_ref, turned_ref, table_ref, taps_ref, gain_ref, sems,
):
    y, _, zp, _, _, _ = place()
    pixels, _ = own_hbm.shape
    half = pixels // 2
    begin = pl.multiple_of((1 - zp if far else zp) * half, 16)
    pairs = [
        (near_hbm, near_ref),
        (taps_hbm, taps_ref),
        (gain_hbm, gain_ref),
        (own_hbm, table_ref.at[pl.ds(0, pixels)]),
        (band_hbm, table_ref.at[pl.ds(pixels, pixels)]),
    ]
    copies = [pltpu.make_async_copy(a, b, sems.at[i]) for i, (a, b) in enumerate(pairs)]
    start_all(copies)
    copies[0].wait()
    turned_ref[...] = near_ref[...].T
    near = turned_ref[pl.ds(begin, half), :]
    neighbours = near.shape[1]
    local = near - y * pixels
    local = jnp.where(local < 0, local + 2 * pixels, local)
    slots = lax.broadcasted_iota(jnp.int32, (half, 2 * pixels), 1)
    chosen = jnp.concatenate(
        [
            jnp.where(local[:, k : k + 1] == slots, 1.0, 0.0).astype(jnp.bfloat16)
            for k in range(neighbours)
        ],
        axis=0,
    )
    for copy in copies[1:]:
        copy.wait()
    gathered = jnp.dot(chosen, table_ref[...], preferred_element_type=jnp.float32)
    own = table_ref[pl.ds(begin, half), :].astype(jnp.float32)
    spatial = taps_ref[0:1, :] * own
    for k in range(neighbours):
        spatial = spatial + taps_ref[k + 1 : k + 2, :] * gathered[k * half : (k + 1) * half]
    hidden = (own + spatial).astype(jnp.bfloat16).astype(jnp.float32)
    inverse = lax.rsqrt(jnp.mean(hidden * hidden, axis=-1, keepdims=True) + 1e-05)
    out_ref[...] = (hidden * inverse * gain_ref[...]).astype(jnp.bfloat16)


def head_sums(products, width):
    depth = width * 2 // HEADS
    row_head = lax.broadcasted_iota(jnp.int32, (width, width), 0) // depth
    col_head = lax.broadcasted_iota(jnp.int32, (width, width), 1) // depth
    same = jnp.where(row_head == col_head, 0.125, 0.0).astype(jnp.bfloat16)
    pixels = products[0].shape[0]
    stacked = jnp.concatenate(products, axis=0)
    high = stacked.astype(jnp.bfloat16)
    low = (stacked - high.astype(jnp.float32)).astype(jnp.bfloat16)
    total = jnp.dot(high, same, preferred_element_type=jnp.float32)
    total = total + jnp.dot(low, same, preferred_element_type=jnp.float32)
    return [total[i * pixels : (i + 1) * pixels] for i in range(len(products))]


def wide(ref, frame, third, width, pixels):
    rows = ref[frame * pixels : (frame + 1) * pixels, third * width : (third + 1) * width]
    return rows.astype(jnp.float32)


def shard_rows(k, rows):
    _, _, _, _, x, core = place()
    f = (2 * x + core) ^ (2 * (k & 1) + (k >> 1))
    return pl.ds(pl.multiple_of(f * rows, 128), rows)


def forward_kernel(*refs):
    frames = 4
    row_refs, shards, refs = refs[:4], refs[4:8], refs[8:]
    qkv_ref, weights_ref, attended_ref, n_ref, w_ref, sems = refs
    _, t, _, _, _, _ = place()
    pixels, channels = row_refs[0].shape
    width = channels // 2
    rows = shards[0].shape[0]
    copies = [pltpu.make_async_copy(row_refs[k], n_ref.at[t ^ k], sems.at[k]) for k in range(frames)]
    copies += [
        pltpu.make_async_copy(
            shards[k].at[:, pl.ds(0, 3 * width)], w_ref.at[shard_rows(k, rows)], sems.at[frames + k]
        )
        for k in range(4)
    ]
    start_all(copies)
    for copy in copies:
        copy.wait()
    normed = n_ref[...].reshape(frames * pixels, channels)
    qkv_ref[...] = jnp.dot(normed, w_ref[...], preferred_element_type=jnp.float32).astype(
        jnp.bfloat16
    )
    q, k, v = (
        [wide(qkv_ref, i, third, width, pixels) for i in range(frames)] for third in range(3)
    )
    slot = 0
    for i in range(frames):
        scores = head_sums([q[i] * k[u] for u in range(i + 1)], width)
        largest = scores[0]
        for s in scores[1:]:
            largest = jnp.maximum(largest, s)
        powers = [jnp.exp(s - largest) for s in scores]
        total = powers[0]
        for p in powers[1:]:
            total = total + p
        scale = 1.0 / total
        seen = None
        for u in range(i + 1):
            weights = (powers[u] * scale).astype(jnp.bfloat16)
            weights_ref[slot] = weights
            slot += 1
            term = weights.astype(jnp.float32) * v[u]
            seen = term if seen is None else seen + term
        attended_ref[i * pixels : (i + 1) * pixels, :] = seen.astype(jnp.bfloat16)


def backward_kernel(*refs):
    frames = 4
    row_refs, pair_refs, shards, refs = refs[:4], refs[4:6], refs[6:10], refs[10:]
    qkv_ref, weights_ref, attended_ref, refs = refs[0], refs[1], refs[2], refs[3:]
    keep_refs, send_refs, refs = refs[:2], refs[2:4], refs[4:]
    n_ref, u_ref, out_w_ref, sums_ref, out_sums_ref, sems = refs
    _, t, _, zh, x, core = place()
    pixels, channels = row_refs[0].shape
    width = out_w_ref.shape[0]
    rows = shards[0].shape[0]
    row_copies = [
        pltpu.make_async_copy(row_refs[k], n_ref.at[t ^ k], sems.at[k]) for k in range(frames)
    ]
    up_copies = [
        pltpu.make_async_copy(pair_refs[k & 1].at[k >> 1], u_ref.at[t ^ k], sems.at[frames + k])
        for k in range(frames)
    ]

    def out_copy(shard, k):
        start = pl.multiple_of((core ^ k) * rows, 128)
        return pltpu.make_async_copy(
            shard.at[:, pl.ds(3 * width, channels)],
            out_w_ref.at[pl.ds(start, rows)],
            sems.at[2 * frames + k],
        )

    start_all(up_copies)
    for k in range(2):

        @pl.when(x == zh)
        def _(k=k):
            out_copy(shards[2 * k], k).start()

        @pl.when(x != zh)
        def _(k=k):
            out_copy(shards[2 * k + 1], k).start()

    start_all(row_copies)
    for copy in up_copies + [out_copy(shards[2 * k], k) for k in range(2)]:
        copy.wait()
    upstream = u_ref[...].reshape(frames * pixels, channels)
    grads = lax.dot_general(
        upstream, out_w_ref[...], (((1,), (1,)), ((), ())), preferred_element_type=jnp.float32
    ).astype(jnp.bfloat16)
    g = [grads[i * pixels : (i + 1) * pixels].astype(jnp.float32) for i in range(frames)]
    q, k, v = (
        [wide(qkv_ref, i, third, width, pixels) for i in range(frames)] for third in range(3)
    )
    dq, dk, dv = [], [None] * frames, [None] * frames

    def plus(total, term):
        return term if total is None else total + term

    slot = 0
    for i in range(frames):
        dprob = head_sums([g[i] * v[u] for u in range(i + 1)], width)
        weights = [weights_ref[slot + u].astype(jnp.float32) for u in range(i + 1)]
        slot += i + 1
        delta = weights[0] * dprob[0]
        for u in range(1, i + 1):
            delta = delta + weights[u] * dprob[u]
        grad_q = None
        for u in range(i + 1):
            ds = (weights[u] * (dprob[u] - delta)).astype(jnp.bfloat16).astype(jnp.float32)
            grad_q = plus(grad_q, ds * k[u])
            dk[u] = plus(dk[u], ds * q[i])
            dv[u] = plus(dv[u], weights[u] * g[i])
        dq.append(grad_q.astype(jnp.bfloat16))
    for copy in row_copies:
        copy.wait()
    normed = n_ref[...].reshape(frames * pixels, channels)
    thirds = (dq, [d.astype(jnp.bfloat16) for d in dk], [d.astype(jnp.bfloat16) for d in dv])

    def over_rows(lhs, rhs):
        return lax.dot_general(
            lhs, rhs, (((0,), (0,)), ((), ())), preferred_element_type=jnp.float32
        )

    for m, pieces in enumerate(thirds):
        grad = over_rows(normed, jnp.concatenate(pieces, axis=0))
        for lane in range(0, width, 128):
            sums_ref[lane // 128, pl.ds(m, channels, stride=3), :] = grad[:, lane : lane + 128]
    out_sums_ref[...] = over_rows(attended_ref[...], upstream)

    block = depth = channels // HEADS

    def store(path_refs):
        for side in range(2):
            for slot in range(8):
                at_x, at_y, at_zp = slot >> 2, (slot >> 1) & 1, slot & 1
                for low in range(2):
                    index = at_y * 16 + (2 * at_zp + low) * 4 + 2 * at_x + side
                    for path in range(2):
                        if index < 3 * HEADS:
                            first = index * block
                            piece = sums_ref[path, first : first + block, :]
                        else:
                            first = (2 * at_x + side) * block
                            lane = low * width + path * 128
                            piece = out_sums_ref[first : first + block, lane : lane + 128]
                        a, b = (at_x, at_y) if path == 0 else (at_y, at_x)
                        rows_at = slice(low * block, (low + 1) * block)
                        ref = path_refs[path]
                        ref[a, b, at_zp, side, rows_at, :] = piece.astype(ref.dtype)

    @pl.when(core == 0)
    def _():
        store(send_refs)

    @pl.when(core == 1)
    def _():
        store(keep_refs)


def join_kernel(total_0_ref, total_1_ref, handed_ref, got_ref, got_handed_ref, out_ref):
    y, _, zp, zh, _, core = place()
    paths, rows, _ = got_ref.shape
    is_out = (y == 1) & (zp == 1)

    def join(totals, other):
        for path in range(paths):
            got = other[path].astype(jnp.float32)
            for side in range(2):
                mine = totals[path][side * rows : (side + 1) * rows, :]
                joined = jnp.where(is_out | (zh == side), mine, got)
                out_ref[pl.ds(side * paths + path, rows, stride=2 * paths), :] = joined

    @pl.when(core == 0)
    def _():
        join([handed_ref.at[0], handed_ref.at[1]], got_handed_ref)

    @pl.when(core == 1)
    def _():
        join([total_0_ref.at[1], total_1_ref.at[1]], got_ref)


def split_form(features, neighbours, conv_taps, norm_gain, qkv_weight, out_weight, cotangent):
    own = features[0, 0]
    pixels, channels = own.shape
    half, width, block = pixels // 2, channels // 2, channels // HEADS
    y, _, zp, zh, x, _ = place()
    narrow_type = jnp.bfloat16
    anywhere = pl.BlockSpec(memory_space=pl.ANY)
    in_vmem = pl.BlockSpec(memory_space=VMEM)
    piece = jax.ShapeDtypeStruct((half, channels), narrow_type)

    band = swap(own, "blk", 1)
    up_mine, up_other, cut = pl.pallas_call(
        prep_kernel,
        out_shape=(
            piece,
            piece,
            jax.ShapeDtypeStruct((qkv_weight.shape[0], 3 * width + channels), narrow_type),
        ),
        in_specs=[anywhere] * 3,
        out_specs=(in_vmem,) * 3,
        scratch_shapes=[pltpu.SemaphoreType.DMA((6,))],
        name="prep",
    )(cotangent[0, 0], qkv_weight, out_weight)

    cut_x = swap(cut, "fsdp", 2)
    up_2 = swap(up_other, "tm", 2)

    def conv(far):
        return pl.pallas_call(
            functools.partial(conv_kernel, far),
            out_shape=piece,
            in_specs=[anywhere] * 5,
            out_specs=in_vmem,
            scratch_shapes=[
                pltpu.VMEM((neighbours.shape[1], pixels), jnp.int32),
                pltpu.VMEM((pixels, neighbours.shape[1]), jnp.int32),
                pltpu.VMEM((2 * pixels, channels), narrow_type),
                pltpu.VMEM(conv_taps.shape, jnp.float32),
                pltpu.VMEM((1, channels), jnp.float32),
                pltpu.SemaphoreType.DMA((5,)),
            ],
            compiler_params=pltpu.CompilerParams(vmem_limit_bytes=16 << 20),
            name="conv_far" if far else "conv_near",
        )(neighbours.T, own, band, conv_taps, norm_gain.reshape(1, channels))

    n_other = conv(True)
    row_3 = swap(n_other, "tm", 3)
    row_2 = swap(n_other, "tm", 2)
    n_mine = conv(False)
    row_1 = swap(n_mine, "tm", 1)
    up_own = jnp.stack([up_mine, up_2])
    up_got = swap(up_own, "tm", 1)
    cut_c = swap(cut, "fsdp", 1)
    cut_xc = swap(cut_x, "fsdp", 1)

    qkv, weights, attended = pl.pallas_call(
        forward_kernel,
        out_shape=(
            jax.ShapeDtypeStruct((4 * half, 3 * width), narrow_type),
            jax.ShapeDtypeStruct((10, half, width), narrow_type),
            jax.ShapeDtypeStruct((4 * half, width), narrow_type),
        ),
        in_specs=[anywhere] * 8,
        out_specs=(in_vmem,) * 3,
        scratch_shapes=[
            pltpu.VMEM((4, half, channels), narrow_type),
            pltpu.VMEM((channels, 3 * width), narrow_type),
            pltpu.SemaphoreType.DMA((8,)),
        ],
        compiler_params=pltpu.CompilerParams(vmem_limit_bytes=24 << 20),
        name="forward",
    )(n_mine, row_1, row_2, row_3, cut, cut_x, cut_c, cut_xc)
    *keep, send_0, send_1 = pl.pallas_call(
        backward_kernel,
        out_shape=(
            *(jax.ShapeDtypeStruct((2,) * 4 + (2 * block, 128), jnp.float32),) * 2,
            *(jax.ShapeDtypeStruct((2,) * 4 + (2 * block, 128), narrow_type),) * 2,
        ),
        in_specs=[anywhere] * 10 + [in_vmem] * 3,
        out_specs=(in_vmem,) * 4,
        scratch_shapes=[
            pltpu.VMEM((4, half, channels), narrow_type),
            pltpu.VMEM((4, half, channels), narrow_type),
            pltpu.VMEM((width, channels), narrow_type),
            pltpu.VMEM((width // 128, 3 * channels, 128), jnp.float32),
            pltpu.VMEM((width, channels), jnp.float32),
            pltpu.SemaphoreType.DMA((10,)),
        ],
        compiler_params=pltpu.CompilerParams(vmem_limit_bytes=28 << 20),
        name="backward",
    )(
        n_mine, row_1, row_2, row_3, up_own, up_got, cut, cut_x, cut_c, cut_xc,
        qkv, weights, attended,
    )

    def narrow(values):
        return values.astype(jnp.bfloat16)

    def plus(*terms):
        total = terms[0].astype(jnp.float32)
        for term in terms[1:]:
            total = total + term.astype(jnp.float32)
        return total

    cores = lax.axis_size("fsdp")
    up = [(i, i + 1) for i in range(0, cores, 2)]
    paths = [
        [keep[0], lax.ppermute(send_0, "fsdp", up)],
        [keep[1], lax.ppermute(send_1, "fsdp", up)],
    ]
    hops = (("fsdp", 2, x), ("blk", 1, y))
    for stage in range(2):
        got = []
        for path in range(2):
            axis, mask, index = hops[path ^ stage]
            far = plus(*(pick(part, 1 - index) for part in paths[path]))
            got.append(shift(narrow(far), axis, mask))
        for path in range(2):
            index = hops[path ^ stage][2]
            paths[path] = [pick(part, index) for part in paths[path]] + [got[path]]
    far = jnp.stack([plus(*(pick(part, 1 - zp) for part in path)) for path in paths])
    got = shift(narrow(far), "tm", 2)
    totals = [
        plus(*(pick(part, zp) for part in path), got[i]) for i, path in enumerate(paths)
    ]

    def both(core):
        rows = [pick(total[core].reshape(2, block, 128), 1 - zh) for total in totals]
        return narrow(jnp.stack(rows))

    got = shift(both(1), "tm", 1)
    got_handed = shift(both(0), "tm", 1, 0)
    handed = lax.ppermute(
        jnp.stack([total[0] for total in totals]), "fsdp", [(j, i) for i, j in up]
    )
    out = pl.pallas_call(
        join_kernel,
        out_shape=jax.ShapeDtypeStruct((block * channels // 128, 128), jnp.float32),
        in_specs=[in_vmem] * 5,
        out_specs=in_vmem,
        compiler_params=pltpu.CompilerParams(vmem_limit_bytes=4 << 20),
        name="join",
    )(*totals, handed, got, got_handed)
    return out.reshape(-1)


def with_halo(cells, sides, width):
    for axis, dim in sides:
        count = lax.axis_size(axis)
        ends = count - 1
        head = lax.slice_in_dim(cells, 0, width, axis=dim)
        tail = lax.slice_in_dim(cells, cells.shape[dim] - width, cells.shape[dim], axis=dim)
        cells = jnp.concatenate(
            [
                lax.ppermute(tail, axis, [(i, (i + 1) % count) for i in range(ends)]),
                cells,
                lax.ppermute(head, axis, [((i + 1) % count, i) for i in range(ends)]),
            ],
            axis=dim,
        )
    return cells


def halved(partial, axis, bit):
    count = lax.axis_size(axis)
    mine = (lax.axis_index(axis) >> bit) & 1
    keep = lax.dynamic_index_in_dim(partial, mine, 0, keepdims=False)
    send = lax.dynamic_index_in_dim(partial, 1 - mine, 0, keepdims=False)
    got = lax.ppermute(send.astype(jnp.bfloat16), axis, [(i, i ^ (1 << bit)) for i in range(count)])
    return keep + got.astype(jnp.float32)


def scattered_sum(summands):
    counts = [lax.axis_size(axis) for axis in ("blk", "tm", "fsdp")]
    bits = [count.bit_length() - 1 for count in counts]
    order = [("fsdp", bit) for bit in range(bits[2])]
    order += [("blk", bit) for bit in range(bits[0])]
    order += [("tm", bit) for bit in range(bits[1])]
    labels = [(axis, bit) for axis, many in zip(("blk", "tm", "fsdp"), bits) for bit in reversed(range(many))]
    partial = summands.reshape((2,) * len(labels) + (-1, 128))
    for axis, bit in order:
        place = labels.index((axis, bit))
        labels.pop(place)
        partial = halved(jnp.moveaxis(partial, place, 0), axis, bit)
    return partial.reshape(-1)


def rounded(values):
    return lax.optimization_barrier(values.astype(jnp.bfloat16)).astype(jnp.float32)


def attend_all(qkv_rows, grad_rows):
    frames, pixels, width = qkv_rows.shape
    channels = width // 3

    def split_heads(block):
        return block.reshape(frames, pixels, HEADS, channels // HEADS).astype(jnp.float32)

    queries = split_heads(qkv_rows[:, :, :channels])
    keys_all = split_heads(qkv_rows[:, :, channels : 2 * channels])
    values = split_heads(qkv_rows[:, :, 2 * channels :])
    grads = split_heads(grad_rows)
    scores = jnp.einsum("tpeh,upeh->petu", queries, keys_all) * 0.125
    causal = jnp.arange(frames)[:, None] >= jnp.arange(frames)[None, :]
    masked = jnp.where(causal, scores, -1e30)
    largest = jnp.max(masked, axis=-1, keepdims=True)
    totals = jnp.sum(jnp.exp(masked - largest), axis=-1, keepdims=True)
    log_total = largest + jnp.log(totals)
    weights = rounded(jnp.exp(masked - log_total))
    attended = jnp.einsum("petu,upeh->tpeh", weights, values)
    dprob = jnp.einsum("tpeh,upeh->petu", grads, values)
    delta = jnp.sum(weights * dprob, axis=-1, keepdims=True)
    dscore = rounded(weights * (dprob - delta) * 0.125)
    grad_query = jnp.einsum("petu,upeh->tpeh", dscore, keys_all)
    grad_key = jnp.einsum("petu,tpeh->upeh", dscore, queries)
    grad_value = jnp.einsum("petu,tpeh->upeh", weights, grads)
    joined = jnp.concatenate(
        [part.reshape(frames, pixels, channels) for part in (grad_query, grad_key, grad_value)],
        axis=-1,
    )
    return (
        attended.reshape(frames, pixels, channels).astype(jnp.bfloat16),
        joined.astype(jnp.bfloat16),
    )


def general_form(features, neighbours, conv_taps, norm_gain, qkv_weight, out_weight, cotangent):
    inputs = features[0, 0]
    upstream = cotangent[0, 0]
    pixels, channels = inputs.shape
    padded = with_halo(inputs, (("blk", 0),), HALO)
    first_pixel = lax.axis_index("blk") * pixels
    local_rows = neighbours - first_pixel + HALO
    inputs_f = inputs.astype(jnp.float32)
    spatial = conv_taps[0] * inputs_f
    for column in range(8):
        spatial = spatial + conv_taps[column + 1] * jnp.take(
            padded, local_rows[:, column], axis=0
        ).astype(jnp.float32)
    hidden_f = rounded(inputs_f + spatial)
    inverse = lax.rsqrt(jnp.mean(hidden_f * hidden_f, axis=-1, keepdims=True) + 1e-05)
    normed = (hidden_f * inverse * norm_gain).astype(jnp.bfloat16)
    full_qkv, full_out = (
        lax.all_gather(qkv_weight, "fsdp", axis=0, tiled=True),
        lax.all_gather(out_weight, "fsdp", axis=0, tiled=True),
    )
    att_grads = jnp.dot(upstream, full_out.T, preferred_element_type=jnp.float32).astype(
        jnp.bfloat16
    )
    swap_normed, swap_grads, swap_upstream = (
        lax.all_to_all(normed[None], "tm", split_axis=1, concat_axis=0, tiled=True),
        lax.all_to_all(att_grads[None], "tm", split_axis=1, concat_axis=0, tiled=True),
        lax.all_to_all(upstream[None], "tm", split_axis=1, concat_axis=0, tiled=True),
    )
    frames = swap_normed.shape[0]
    few_pixels = swap_normed.shape[1]
    flat_normed = swap_normed.reshape(-1, channels)
    qkv_rows = jnp.dot(flat_normed, full_qkv, preferred_element_type=jnp.float32).astype(
        jnp.bfloat16
    )
    qkv_rows = qkv_rows.reshape(frames, few_pixels, 3 * channels)
    attended_x, dqkv_x = attend_all(qkv_rows, swap_grads)
    grad_in = jnp.einsum(
        "pc,pd->cd",
        flat_normed,
        dqkv_x.reshape(-1, 3 * channels),
        preferred_element_type=jnp.float32,
    )
    grad_out = jnp.einsum(
        "pc,pd->cd",
        attended_x.reshape(-1, channels),
        swap_upstream.reshape(-1, channels),
        preferred_element_type=jnp.float32,
    )
    summands = jnp.concatenate([grad_in.reshape(-1), grad_out.reshape(-1)])
    return scattered_sum(summands)


def solution(mesh):
    sizes = mesh.shape

    def per_device(*arrays):
        pixels, channels = arrays[0].shape[-2:]
        devices = sizes["blk"] * sizes["tm"] * sizes["fsdp"]
        fits = (
            sizes["blk"] == 2
            and sizes["tm"] == sizes["fsdp"] == arrays[0].shape[0] * 4
            and devices == 4 * HEADS
            and pixels >= HALO
            and pixels % 32 == 0
            and channels == 64 * HEADS
        )
        if not fits:
            return general_form(*arrays)
        return split_form(*arrays)

    return jax.shard_map(
        per_device,
        mesh=mesh,
        in_specs=(
            P("fsdp", "tm", "blk", None),
            P("blk", None),
            P(),
            P(),
            P("fsdp", None),
            P("fsdp", None),
            P("fsdp", "tm", "blk", None),
        ),
        out_specs=P(("blk", "tm", "fsdp")),
        check_vma=False,
    )
```

```python
import functools

import jax
import jax.numpy as jnp
from jax import lax
from jax.experimental import pallas as pl
from jax.experimental.pallas import tpu as pltpu
from jax.sharding import PartitionSpec as P


HEADS = 8
HALO = 130
VMEM = pltpu.MemorySpace.VMEM


def swap(values, axis, mask):
    return lax.ppermute(values, axis, [(i, i ^ mask) for i in range(lax.axis_size(axis))])


def pick(values, index, dim=0):
    return lax.dynamic_index_in_dim(values, index, dim, keepdims=False)


def place():
    t, f = lax.axis_index("tm"), lax.axis_index("fsdp")
    return lax.axis_index("blk"), t, t >> 1, t & 1, f >> 1, f & 1


def start_all(copies):
    for copy in copies:
        copy.start()


def conv_kernel(
    far, near_hbm, own_hbm, band_hbm, taps_hbm, gain_hbm, out_ref,
    near_ref, turned_ref, table_ref, taps_ref, gain_ref, sems,
):
    y, _, zp, _, _, _ = place()
    pixels, _ = own_hbm.shape
    half = pixels // 2
    begin = pl.multiple_of((1 - zp if far else zp) * half, 16)
    pairs = [
        (near_hbm, near_ref),
        (taps_hbm, taps_ref),
        (gain_hbm, gain_ref),
        (own_hbm, table_ref.at[pl.ds(0, pixels)]),
        (band_hbm, table_ref.at[pl.ds(pixels, pixels)]),
    ]
    copies = [pltpu.make_async_copy(a, b, sems.at[i]) for i, (a, b) in enumerate(pairs)]
    start_all(copies)
    copies[0].wait()
    turned_ref[...] = near_ref[...].T
    near = turned_ref[pl.ds(begin, half), :]
    neighbours = near.shape[1]
    local = near - y * pixels
    local = jnp.where(local < 0, local + 2 * pixels, local)
    slots = lax.broadcasted_iota(jnp.int32, (half, 2 * pixels), 1)
    chosen = jnp.concatenate(
        [
            jnp.where(local[:, k : k + 1] == slots, 1.0, 0.0).astype(jnp.bfloat16)
            for k in range(neighbours)
        ],
        axis=0,
    )
    for copy in copies[1:]:
        copy.wait()
    gathered = jnp.dot(chosen, table_ref[...], preferred_element_type=jnp.float32)
    own = table_ref[pl.ds(begin, half), :].astype(jnp.float32)
    spatial = taps_ref[0:1, :] * own
    for k in range(neighbours):
        spatial = spatial + taps_ref[k + 1 : k + 2, :] * gathered[k * half : (k + 1) * half]
    hidden = (own + spatial).astype(jnp.bfloat16).astype(jnp.float32)
    inverse = lax.rsqrt(jnp.mean(hidden * hidden, axis=-1, keepdims=True) + 1e-05)
    out_ref[...] = (hidden * inverse * gain_ref[...]).astype(jnp.bfloat16)


def head_sums(products, width):
    depth = width * 2 // HEADS
    row_head = lax.broadcasted_iota(jnp.int32, (width, width), 0) // depth
    col_head = lax.broadcasted_iota(jnp.int32, (width, width), 1) // depth
    same = jnp.where(row_head == col_head, 0.125, 0.0).astype(jnp.bfloat16)
    pixels = products[0].shape[0]
    stacked = jnp.concatenate(products, axis=0)
    high = stacked.astype(jnp.bfloat16)
    low = (stacked - high.astype(jnp.float32)).astype(jnp.bfloat16)
    total = jnp.dot(high, same, preferred_element_type=jnp.float32)
    total = total + jnp.dot(low, same, preferred_element_type=jnp.float32)
    return [total[i * pixels : (i + 1) * pixels] for i in range(len(products))]


def wide(ref, frame, third, width, pixels):
    rows = ref[frame * pixels : (frame + 1) * pixels, third * width : (third + 1) * width]
    return rows.astype(jnp.float32)


def shard_rows(k, rows):
    _, _, _, _, x, core = place()
    f = (2 * x + core) ^ (2 * (k & 1) + (k >> 1))
    return pl.ds(pl.multiple_of(f * rows, 128), rows)


def forward_kernel(*refs):
    frames = 4
    row_refs, shards, refs = refs[:4], refs[4:8], refs[8:]
    qkv_ref, weights_ref, attended_ref, n_ref, w_ref, sems = refs
    _, t, _, zh, _, _ = place()
    pixels, channels = row_refs[0].shape
    width = channels // 2
    rows = shards[0].shape[0]
    copies = [pltpu.make_async_copy(row_refs[k], n_ref.at[t ^ k], sems.at[k]) for k in range(frames)]
    for k in range(4):
        for m in range(3):
            columns = pl.ds(pl.multiple_of((2 * m + zh) * width, 128), width)
            copies.append(
                pltpu.make_async_copy(
                    shards[k].at[:, columns],
                    w_ref.at[shard_rows(k, rows), pl.ds(m * width, width)],
                    sems.at[frames + 3 * k + m],
                )
            )
    start_all(copies)
    for copy in copies:
        copy.wait()
    normed = n_ref[...].reshape(frames * pixels, channels)
    qkv_ref[...] = jnp.dot(normed, w_ref[...], preferred_element_type=jnp.float32).astype(
        jnp.bfloat16
    )
    q, k, v = (
        [wide(qkv_ref, i, third, width, pixels) for i in range(frames)] for third in range(3)
    )
    slot = 0
    for i in range(frames):
        scores = head_sums([q[i] * k[u] for u in range(i + 1)], width)
        largest = scores[0]
        for s in scores[1:]:
            largest = jnp.maximum(largest, s)
        powers = [jnp.exp(s - largest) for s in scores]
        total = powers[0]
        for p in powers[1:]:
            total = total + p
        scale = 1.0 / total
        seen = None
        for u in range(i + 1):
            weights = (powers[u] * scale).astype(jnp.bfloat16)
            weights_ref[slot] = weights
            slot += 1
            term = weights.astype(jnp.float32) * v[u]
            seen = term if seen is None else seen + term
        attended_ref[i * pixels : (i + 1) * pixels, :] = seen.astype(jnp.bfloat16)


def backward_kernel(*refs):
    frames = 4
    row_refs, pair_refs, out_refs, refs = refs[:4], refs[4:6], refs[6:8], refs[8:]
    qkv_ref, weights_ref, attended_ref, refs = refs[0], refs[1], refs[2], refs[3:]
    keep_ref, send_ref, n_ref, u_ref, out_w_ref, sums_ref, out_sums_ref, sems = refs
    _, t, _, zh, _, core = place()
    pixels, channels = row_refs[0].shape
    width = out_w_ref.shape[0]
    rows = out_refs[0].shape[0]
    row_copies = [
        pltpu.make_async_copy(row_refs[k], n_ref.at[t ^ k], sems.at[k]) for k in range(frames)
    ]
    up_copies = [
        pltpu.make_async_copy(pair_refs[k & 1].at[k >> 1], u_ref.at[t ^ k], sems.at[frames + k])
        for k in range(frames)
    ]

    for k in range(2):
        start = pl.multiple_of((core ^ k) * rows, 128)
        up_copies.append(
            pltpu.make_async_copy(
                out_refs[k], out_w_ref.at[pl.ds(start, rows)], sems.at[2 * frames + k]
            )
        )
    start_all(up_copies)
    start_all(row_copies)
    for copy in up_copies:
        copy.wait()
    upstream = u_ref[...].reshape(frames * pixels, channels)
    grads = lax.dot_general(
        upstream, out_w_ref[...], (((1,), (1,)), ((), ())), preferred_element_type=jnp.float32
    ).astype(jnp.bfloat16)
    g = [grads[i * pixels : (i + 1) * pixels].astype(jnp.float32) for i in range(frames)]
    q, k, v = (
        [wide(qkv_ref, i, third, width, pixels) for i in range(frames)] for third in range(3)
    )
    dq, dk, dv = [], [None] * frames, [None] * frames

    def plus(total, term):
        return term if total is None else total + term

    slot = 0
    for i in range(frames):
        dprob = head_sums([g[i] * v[u] for u in range(i + 1)], width)
        weights = [weights_ref[slot + u].astype(jnp.float32) for u in range(i + 1)]
        slot += i + 1
        delta = weights[0] * dprob[0]
        for u in range(1, i + 1):
            delta = delta + weights[u] * dprob[u]
        grad_q = None
        for u in range(i + 1):
            ds = (weights[u] * (dprob[u] - delta)).astype(jnp.bfloat16).astype(jnp.float32)
            grad_q = plus(grad_q, ds * k[u])
            dk[u] = plus(dk[u], ds * q[i])
            dv[u] = plus(dv[u], weights[u] * g[i])
        dq.append(grad_q.astype(jnp.bfloat16))
    for copy in row_copies:
        copy.wait()
    normed = n_ref[...].reshape(frames * pixels, channels)
    thirds = (dq, [d.astype(jnp.bfloat16) for d in dk], [d.astype(jnp.bfloat16) for d in dv])

    def over_rows(lhs, rhs):
        return lax.dot_general(
            lhs, rhs, (((0,), (0,)), ((), ())), preferred_element_type=jnp.float32
        )

    for m, pieces in enumerate(thirds):
        grad = over_rows(normed, jnp.concatenate(pieces, axis=0))
        for lane in range(0, width, 128):
            sums_ref[lane // 128, pl.ds(m, channels, stride=3), :] = grad[:, lane : lane + 128]
    out_sums_ref[...] = over_rows(attended_ref[...], upstream)

    block = channels // HEADS
    for slot in range(8):
        at_x, at_y, at_zp = slot >> 2, (slot >> 1) & 1, slot & 1
        for side, ref in ((core, keep_ref), (1 - core, send_ref)):
            for low in range(2):
                rows_at = slice(low * block, (low + 1) * block)
                first = at_y * 16 + (2 * at_zp + low) * 4 + 2 * at_x
                if first < 3 * HEADS:
                    start = pl.multiple_of((first + (side ^ zh ^ low)) * block, block)
                    for lane in range(width // 128):
                        piece = sums_ref[lane, pl.ds(start, block), :]
                        lanes_at = slice(lane * 128, (lane + 1) * 128)
                        ref[slot, rows_at, lanes_at] = piece.astype(ref.dtype)
                else:
                    start = pl.multiple_of((2 * at_x + side) * block, block)
                    piece = out_sums_ref[pl.ds(start, block), low * width : (low + 1) * width]
                    ref[slot, rows_at, :] = piece.astype(ref.dtype)


def join_kernel(total_ref, got_ref, out_ref):
    y, _, zp, zh, _, _ = place()
    lanes = out_ref.shape[1]
    rows, width = got_ref.shape
    is_out = (y == 1) & (zp == 1)
    got = got_ref[...].astype(jnp.float32)
    for side in range(2):
        joined = jnp.where(is_out | (zh == side), total_ref[side], got)
        for lane in range(0, width, lanes):
            first = (side * width + lane) // lanes
            step = 2 * width // lanes
            out_ref[pl.ds(first, rows, stride=step), :] = joined[:, lane : lane + lanes]


def split_form(features, neighbours, conv_taps, norm_gain, qkv_weight, out_weight, cotangent):
    own = features[0, 0]
    pixels, channels = own.shape
    half, width, block = pixels // 2, channels // 2, channels // HEADS
    y, _, zp, zh, x, _ = place()
    narrow_type = jnp.bfloat16
    anywhere = pl.BlockSpec(memory_space=pl.ANY)
    in_vmem = pl.BlockSpec(memory_space=VMEM)
    piece = jax.ShapeDtypeStruct((half, channels), narrow_type)

    band = swap(own, "blk", 1)
    qkv_x = swap(qkv_weight, "fsdp", 2)
    out_x = swap(out_weight, "fsdp", 2)
    halves = cotangent[0, 0].reshape(2, half, channels)
    up_2 = swap(pick(halves, 1 - zp), "tm", 2)

    def conv(far):
        return pl.pallas_call(
            functools.partial(conv_kernel, far),
            out_shape=piece,
            in_specs=[anywhere] * 5,
            out_specs=in_vmem,
            scratch_shapes=[
                pltpu.VMEM((neighbours.shape[1], pixels), jnp.int32),
                pltpu.VMEM((pixels, neighbours.shape[1]), jnp.int32),
                pltpu.VMEM((2 * pixels, channels), narrow_type),
                pltpu.VMEM(conv_taps.shape, jnp.float32),
                pltpu.VMEM((1, channels), jnp.float32),
                pltpu.SemaphoreType.DMA((5,)),
            ],
            compiler_params=pltpu.CompilerParams(vmem_limit_bytes=16 << 20),
            name="conv_far" if far else "conv_near",
        )(neighbours.T, own, band, conv_taps, norm_gain.reshape(1, channels))

    n_other = conv(True)
    row_3 = swap(n_other, "tm", 3)
    row_2 = swap(n_other, "tm", 2)
    n_mine = conv(False)
    row_1 = swap(n_mine, "tm", 1)
    up_own = jnp.stack([pick(halves, zp), up_2])
    up_got = swap(up_own, "tm", 1)
    qkv_c = swap(qkv_weight, "fsdp", 1)
    qkv_xc = swap(qkv_x, "fsdp", 1)
    out_rows = jnp.where(x == zh, out_weight, out_x)
    out_c = swap(out_rows, "fsdp", 1)

    qkv, weights, attended = pl.pallas_call(
        forward_kernel,
        out_shape=(
            jax.ShapeDtypeStruct((4 * half, 3 * width), narrow_type),
            jax.ShapeDtypeStruct((10, half, width), narrow_type),
            jax.ShapeDtypeStruct((4 * half, width), narrow_type),
        ),
        in_specs=[anywhere] * 8,
        out_specs=(in_vmem,) * 3,
        scratch_shapes=[
            pltpu.VMEM((4, half, channels), narrow_type),
            pltpu.VMEM((channels, 3 * width), narrow_type),
            pltpu.SemaphoreType.DMA((16,)),
        ],
        compiler_params=pltpu.CompilerParams(vmem_limit_bytes=24 << 20),
        name="forward",
    )(n_mine, row_1, row_2, row_3, qkv_weight, qkv_x, qkv_c, qkv_xc)
    keep, send = pl.pallas_call(
        backward_kernel,
        out_shape=(
            jax.ShapeDtypeStruct((8, 2 * block, width), jnp.float32),
            jax.ShapeDtypeStruct((8, 2 * block, width), narrow_type),
        ),
        in_specs=[anywhere] * 8 + [in_vmem] * 3,
        out_specs=(in_vmem, in_vmem),
        scratch_shapes=[
            pltpu.VMEM((4, half, channels), narrow_type),
            pltpu.VMEM((4, half, channels), narrow_type),
            pltpu.VMEM((width, channels), narrow_type),
            pltpu.VMEM((width // 128, 3 * channels, 128), jnp.float32),
            pltpu.VMEM((width, channels), jnp.float32),
            pltpu.SemaphoreType.DMA((10,)),
        ],
        compiler_params=pltpu.CompilerParams(vmem_limit_bytes=28 << 20),
        name="backward",
    )(
        n_mine, row_1, row_2, row_3, up_own, up_got, out_rows, out_c, qkv, weights, attended
    )

    def narrow(values):
        return values.astype(jnp.bfloat16)

    total = keep + swap(send, "fsdp", 1).astype(jnp.float32)
    total = total.reshape(2, 2, 2, 2 * block, width)
    first, second = total[..., : width // 2], total[..., width // 2 :]
    got_first = swap(narrow(pick(first, 1 - x, 0)), "fsdp", 2)
    got_second = swap(narrow(pick(second, 1 - y, 1)), "blk", 1)
    first = pick(first, x, 0) + got_first.astype(jnp.float32)
    second = pick(second, y, 1) + got_second.astype(jnp.float32)
    got_first = swap(narrow(pick(first, 1 - y, 0)), "blk", 1)
    got_second = swap(narrow(pick(second, 1 - x, 0)), "fsdp", 2)
    first = pick(first, y, 0) + got_first.astype(jnp.float32)
    second = pick(second, x, 0) + got_second.astype(jnp.float32)
    total = jnp.concatenate([first, second], axis=-1)
    total = pick(total, zp) + swap(narrow(pick(total, 1 - zp)), "tm", 2).astype(jnp.float32)
    total = total.reshape(2, block, width)
    cores = lax.axis_size("fsdp")
    crossed = [(i, i ^ cores ^ 1) for i in range(lax.axis_size("tm") * cores)]
    got = lax.ppermute(narrow(pick(total, 1 - zh)), ("tm", "fsdp"), crossed)
    lanes = 128
    out = pl.pallas_call(
        join_kernel,
        out_shape=jax.ShapeDtypeStruct((block * channels // lanes, lanes), jnp.float32),
        in_specs=[in_vmem] * 2,
        out_specs=in_vmem,
        compiler_params=pltpu.CompilerParams(vmem_limit_bytes=4 << 20),
        name="join",
    )(total, got)
    return out.reshape(-1)


def with_halo(cells, sides, width):
    for axis, dim in sides:
        count = lax.axis_size(axis)
        ends = count - 1
        head = lax.slice_in_dim(cells, 0, width, axis=dim)
        tail = lax.slice_in_dim(cells, cells.shape[dim] - width, cells.shape[dim], axis=dim)
        cells = jnp.concatenate(
            [
                lax.ppermute(tail, axis, [(i, (i + 1) % count) for i in range(ends)]),
                cells,
                lax.ppermute(head, axis, [((i + 1) % count, i) for i in range(ends)]),
            ],
            axis=dim,
        )
    return cells


def halved(partial, axis, bit):
    count = lax.axis_size(axis)
    mine = (lax.axis_index(axis) >> bit) & 1
    keep = lax.dynamic_index_in_dim(partial, mine, 0, keepdims=False)
    send = lax.dynamic_index_in_dim(partial, 1 - mine, 0, keepdims=False)
    got = lax.ppermute(send.astype(jnp.bfloat16), axis, [(i, i ^ (1 << bit)) for i in range(count)])
    return keep + got.astype(jnp.float32)


def scattered_sum(summands):
    counts = [lax.axis_size(axis) for axis in ("blk", "tm", "fsdp")]
    bits = [count.bit_length() - 1 for count in counts]
    order = [("fsdp", bit) for bit in range(bits[2])]
    order += [("blk", bit) for bit in range(bits[0])]
    order += [("tm", bit) for bit in range(bits[1])]
    labels = [(axis, bit) for axis, many in zip(("blk", "tm", "fsdp"), bits) for bit in reversed(range(many))]
    partial = summands.reshape((2,) * len(labels) + (-1, 128))
    for axis, bit in order:
        place = labels.index((axis, bit))
        labels.pop(place)
        partial = halved(jnp.moveaxis(partial, place, 0), axis, bit)
    return partial.reshape(-1)


def rounded(values):
    return lax.optimization_barrier(values.astype(jnp.bfloat16)).astype(jnp.float32)


def attend_all(qkv_rows, grad_rows):
    frames, pixels, width = qkv_rows.shape
    channels = width // 3

    def split_heads(block):
        return block.reshape(frames, pixels, HEADS, channels // HEADS).astype(jnp.float32)

    queries = split_heads(qkv_rows[:, :, :channels])
    keys_all = split_heads(qkv_rows[:, :, channels : 2 * channels])
    values = split_heads(qkv_rows[:, :, 2 * channels :])
    grads = split_heads(grad_rows)
    scores = jnp.einsum("tpeh,upeh->petu", queries, keys_all) * 0.125
    causal = jnp.arange(frames)[:, None] >= jnp.arange(frames)[None, :]
    masked = jnp.where(causal, scores, -1e30)
    largest = jnp.max(masked, axis=-1, keepdims=True)
    totals = jnp.sum(jnp.exp(masked - largest), axis=-1, keepdims=True)
    log_total = largest + jnp.log(totals)
    weights = rounded(jnp.exp(masked - log_total))
    attended = jnp.einsum("petu,upeh->tpeh", weights, values)
    dprob = jnp.einsum("tpeh,upeh->petu", grads, values)
    delta = jnp.sum(weights * dprob, axis=-1, keepdims=True)
    dscore = rounded(weights * (dprob - delta) * 0.125)
    grad_query = jnp.einsum("petu,upeh->tpeh", dscore, keys_all)
    grad_key = jnp.einsum("petu,tpeh->upeh", dscore, queries)
    grad_value = jnp.einsum("petu,tpeh->upeh", weights, grads)
    joined = jnp.concatenate(
        [part.reshape(frames, pixels, channels) for part in (grad_query, grad_key, grad_value)],
        axis=-1,
    )
    return (
        attended.reshape(frames, pixels, channels).astype(jnp.bfloat16),
        joined.astype(jnp.bfloat16),
    )


def general_form(features, neighbours, conv_taps, norm_gain, qkv_weight, out_weight, cotangent):
    inputs = features[0, 0]
    upstream = cotangent[0, 0]
    pixels, channels = inputs.shape
    padded = with_halo(inputs, (("blk", 0),), HALO)
    first_pixel = lax.axis_index("blk") * pixels
    local_rows = neighbours - first_pixel + HALO
    inputs_f = inputs.astype(jnp.float32)
    spatial = conv_taps[0] * inputs_f
    for column in range(8):
        spatial = spatial + conv_taps[column + 1] * jnp.take(
            padded, local_rows[:, column], axis=0
        ).astype(jnp.float32)
    hidden_f = rounded(inputs_f + spatial)
    inverse = lax.rsqrt(jnp.mean(hidden_f * hidden_f, axis=-1, keepdims=True) + 1e-05)
    normed = (hidden_f * inverse * norm_gain).astype(jnp.bfloat16)
    full_qkv, full_out = (
        lax.all_gather(qkv_weight, "fsdp", axis=0, tiled=True),
        lax.all_gather(out_weight, "fsdp", axis=0, tiled=True),
    )
    att_grads = jnp.dot(upstream, full_out.T, preferred_element_type=jnp.float32).astype(
        jnp.bfloat16
    )
    swap_normed, swap_grads, swap_upstream = (
        lax.all_to_all(normed[None], "tm", split_axis=1, concat_axis=0, tiled=True),
        lax.all_to_all(att_grads[None], "tm", split_axis=1, concat_axis=0, tiled=True),
        lax.all_to_all(upstream[None], "tm", split_axis=1, concat_axis=0, tiled=True),
    )
    frames = swap_normed.shape[0]
    few_pixels = swap_normed.shape[1]
    flat_normed = swap_normed.reshape(-1, channels)
    qkv_rows = jnp.dot(flat_normed, full_qkv, preferred_element_type=jnp.float32).astype(
        jnp.bfloat16
    )
    qkv_rows = qkv_rows.reshape(frames, few_pixels, 3 * channels)
    attended_x, dqkv_x = attend_all(qkv_rows, swap_grads)
    grad_in = jnp.einsum(
        "pc,pd->cd",
        flat_normed,
        dqkv_x.reshape(-1, 3 * channels),
        preferred_element_type=jnp.float32,
    )
    grad_out = jnp.einsum(
        "pc,pd->cd",
        attended_x.reshape(-1, channels),
        swap_upstream.reshape(-1, channels),
        preferred_element_type=jnp.float32,
    )
    summands = jnp.concatenate([grad_in.reshape(-1), grad_out.reshape(-1)])
    return scattered_sum(summands)


def solution(mesh):
    sizes = mesh.shape

    def per_device(*arrays):
        pixels, channels = arrays[0].shape[-2:]
        devices = sizes["blk"] * sizes["tm"] * sizes["fsdp"]
        fits = (
            sizes["blk"] == 2
            and sizes["tm"] == sizes["fsdp"] == arrays[0].shape[0] * 4
            and devices == 4 * HEADS
            and pixels >= HALO
            and pixels % 32 == 0
            and channels == 64 * HEADS
        )
        if not fits:
            return general_form(*arrays)
        return split_form(*arrays)

    return jax.shard_map(
        per_device,
        mesh=mesh,
        in_specs=(
            P("fsdp", "tm", "blk", None),
            P("blk", None),
            P(),
            P(),
            P("fsdp", None),
            P("fsdp", None),
            P("fsdp", "tm", "blk", None),
        ),
        out_specs=P(("blk", "tm", "fsdp")),
        check_vma=False,
    )
```

```python
import functools

import jax
import jax.numpy as jnp
from jax import lax
from jax.experimental import pallas as pl
from jax.experimental.pallas import tpu as pltpu
from jax.sharding import PartitionSpec as P


HEADS = 8
HALO = 130
VMEM = pltpu.MemorySpace.VMEM


def swap(values, axis, mask):
    return lax.ppermute(values, axis, [(i, i ^ mask) for i in range(lax.axis_size(axis))])


def pick(values, index, dim=0):
    return lax.dynamic_index_in_dim(values, index, dim, keepdims=False)


def place():
    t, f = lax.axis_index("tm"), lax.axis_index("fsdp")
    return lax.axis_index("blk"), t, t >> 1, t & 1, f >> 1, f & 1


def start_all(copies):
    for copy in copies:
        copy.start()


def conv_kernel(
    far, near_hbm, own_hbm, band_hbm, taps_hbm, gain_hbm, out_ref,
    near_ref, turned_ref, table_ref, taps_ref, gain_ref, sems,
):
    y, _, zp, _, _, _ = place()
    pixels, _ = own_hbm.shape
    half = pixels // 2
    begin = pl.multiple_of((1 - zp if far else zp) * half, 16)
    pairs = [
        (near_hbm, near_ref),
        (taps_hbm, taps_ref),
        (gain_hbm, gain_ref),
        (own_hbm, table_ref.at[pl.ds(0, pixels)]),
        (band_hbm, table_ref.at[pl.ds(pixels, pixels)]),
    ]
    copies = [pltpu.make_async_copy(a, b, sems.at[i]) for i, (a, b) in enumerate(pairs)]
    start_all(copies)
    copies[0].wait()
    turned_ref[...] = near_ref[...].T
    near = turned_ref[pl.ds(begin, half), :]
    neighbours = near.shape[1]
    local = near - y * pixels
    local = jnp.where(local < 0, local + 2 * pixels, local)
    slots = lax.broadcasted_iota(jnp.int32, (half, 2 * pixels), 1)
    chosen = jnp.concatenate(
        [
            jnp.where(local[:, k : k + 1] == slots, 1.0, 0.0).astype(jnp.bfloat16)
            for k in range(neighbours)
        ],
        axis=0,
    )
    for copy in copies[1:]:
        copy.wait()
    gathered = jnp.dot(chosen, table_ref[...], preferred_element_type=jnp.float32)
    own = table_ref[pl.ds(begin, half), :].astype(jnp.float32)
    spatial = taps_ref[0:1, :] * own
    for k in range(neighbours):
        spatial = spatial + taps_ref[k + 1 : k + 2, :] * gathered[k * half : (k + 1) * half]
    hidden = (own + spatial).astype(jnp.bfloat16).astype(jnp.float32)
    inverse = lax.rsqrt(jnp.mean(hidden * hidden, axis=-1, keepdims=True) + 1e-05)
    out_ref[...] = (hidden * inverse * gain_ref[...]).astype(jnp.bfloat16)


def head_sums(products, width):
    depth = width * 2 // HEADS
    row_head = lax.broadcasted_iota(jnp.int32, (width, width), 0) // depth
    col_head = lax.broadcasted_iota(jnp.int32, (width, width), 1) // depth
    same = jnp.where(row_head == col_head, 0.125, 0.0).astype(jnp.bfloat16)
    pixels = products[0].shape[0]
    stacked = jnp.concatenate(products, axis=0)
    high = stacked.astype(jnp.bfloat16)
    low = (stacked - high.astype(jnp.float32)).astype(jnp.bfloat16)
    total = jnp.dot(high, same, preferred_element_type=jnp.float32)
    total = total + jnp.dot(low, same, preferred_element_type=jnp.float32)
    return [total[i * pixels : (i + 1) * pixels] for i in range(len(products))]


def wide(ref, frame, third, width, pixels):
    rows = ref[frame * pixels : (frame + 1) * pixels, third * width : (third + 1) * width]
    return rows.astype(jnp.float32)


def shard_rows(k, rows):
    _, _, _, _, x, core = place()
    f = (2 * x + core) ^ (2 * (k & 1) + (k >> 1))
    return pl.ds(pl.multiple_of(f * rows, 128), rows)


def weights_kernel(own_ref, *refs):
    shards, refs = refs[:4], refs[4:]
    w_ref, qkv_ref, sems = refs
    _, _, _, zh, _, _ = place()
    width = w_ref.shape[1] // 3
    rows = shards[0].shape[0]
    copies = []
    for k in range(4):
        for m in range(3):
            columns = pl.ds(pl.multiple_of((2 * m + zh) * width, 128), width)
            copies.append(
                pltpu.make_async_copy(
                    shards[k].at[:, columns],
                    w_ref.at[shard_rows(k, rows), pl.ds(m * width, width)],
                    sems.at[3 * k + m],
                )
            )
    start_all(copies)
    for copy in copies:
        copy.wait()
    qkv_ref[...] = jnp.dot(
        own_ref[...], w_ref[...], preferred_element_type=jnp.float32
    ).astype(jnp.bfloat16)


def forward_kernel(own_ref, row_1_ref, row_2_ref, row_3_ref, own_qkv_ref, w_ref, *refs):
    frames = 4
    qkv_ref, weights_ref, attended_ref, n_ref = refs
    _, t, _, _, _, _ = place()
    pixels, channels = own_ref.shape
    width = channels // 2
    others = (row_1_ref, row_2_ref, row_3_ref)
    for i, ref in enumerate((own_ref,) + others):
        n_ref[t ^ i] = ref[...]
    arrived = jnp.concatenate([ref[...] for ref in others], axis=0)
    arrived = jnp.dot(arrived, w_ref[...], preferred_element_type=jnp.float32)
    arrived = arrived.astype(jnp.bfloat16)
    qkv_ref[pl.ds(pl.multiple_of(t * pixels, 16), pixels), :] = own_qkv_ref[...]
    for i in range(1, frames):
        start = pl.multiple_of((t ^ i) * pixels, 16)
        qkv_ref[pl.ds(start, pixels), :] = arrived[(i - 1) * pixels : i * pixels]
    q, k, v = (
        [wide(qkv_ref, i, third, width, pixels) for i in range(frames)] for third in range(3)
    )
    slot = 0
    for i in range(frames):
        scores = head_sums([q[i] * k[u] for u in range(i + 1)], width)
        largest = scores[0]
        for s in scores[1:]:
            largest = jnp.maximum(largest, s)
        powers = [jnp.exp(s - largest) for s in scores]
        total = powers[0]
        for p in powers[1:]:
            total = total + p
        scale = 1.0 / total
        seen = None
        for u in range(i + 1):
            weights = (powers[u] * scale).astype(jnp.bfloat16)
            weights_ref[slot] = weights
            slot += 1
            term = weights.astype(jnp.float32) * v[u]
            seen = term if seen is None else seen + term
        attended_ref[i * pixels : (i + 1) * pixels, :] = seen.astype(jnp.bfloat16)


def backward_kernel(*refs):
    frames = 4
    pair_refs, out_refs, refs = refs[:2], refs[2:4], refs[4:]
    n_ref, qkv_ref, weights_ref, attended_ref, refs = *refs[:4], refs[4:]
    keep_ref, send_ref, u_ref, g_ref, sums_ref, out_sums_ref = refs
    _, t, _, zh, _, core = place()
    _, pixels, channels = n_ref.shape
    width = out_sums_ref.shape[0]
    first, second = out_refs[0][...], out_refs[1][...]
    out_w = jnp.where(
        core == 0,
        jnp.concatenate([first, second], axis=0),
        jnp.concatenate([second, first], axis=0),
    )
    for i, ref in enumerate(pair_refs):
        pieces = ref[...].reshape(2 * pixels, channels)
        products = lax.dot_general(
            pieces, out_w, (((1,), (1,)), ((), ())), preferred_element_type=jnp.float32
        )
        for j in range(2):
            at = t ^ (2 * j + i)
            g_ref[at] = products[j * pixels : (j + 1) * pixels].astype(jnp.bfloat16)
            u_ref[at] = ref[j]
    normed = n_ref[...].reshape(frames * pixels, channels)
    upstream = u_ref[...].reshape(frames * pixels, channels)
    g = [g_ref[i].astype(jnp.float32) for i in range(frames)]
    q, k, v = (
        [wide(qkv_ref, i, third, width, pixels) for i in range(frames)] for third in range(3)
    )

    def over_rows(lhs, rhs):
        return lax.dot_general(
            lhs, rhs, (((0,), (0,)), ((), ())), preferred_element_type=jnp.float32
        )

    def plus(total, term):
        return term if total is None else total + term

    def keep_sum(m, pieces):
        pieces = [piece.astype(jnp.bfloat16) for piece in pieces]
        grad = over_rows(normed, jnp.concatenate(pieces, axis=0))
        for lane in range(0, width, 128):
            sums_ref[lane // 128, pl.ds(m, channels, stride=3), :] = grad[:, lane : lane + 128]

    out_sums_ref[...] = over_rows(attended_ref[...], upstream)
    firsts = [i * (i + 1) // 2 for i in range(frames)]
    dv = [None] * frames
    for i in range(frames):
        for u in range(i + 1):
            dv[u] = plus(dv[u], weights_ref[firsts[i] + u].astype(jnp.float32) * g[i])
    keep_sum(2, dv)
    dq, dk = [], [None] * frames
    for i in range(frames):
        dprob = head_sums([g[i] * v[u] for u in range(i + 1)], width)
        weights = [weights_ref[firsts[i] + u].astype(jnp.float32) for u in range(i + 1)]
        delta = weights[0] * dprob[0]
        for u in range(1, i + 1):
            delta = delta + weights[u] * dprob[u]
        grad_q = None
        for u in range(i + 1):
            ds = (weights[u] * (dprob[u] - delta)).astype(jnp.bfloat16).astype(jnp.float32)
            grad_q = plus(grad_q, ds * k[u])
            dk[u] = plus(dk[u], ds * q[i])
        dq.append(grad_q)
    keep_sum(0, dq)
    keep_sum(1, dk)

    block = channels // HEADS
    for slot in range(8):
        at_x, at_y, at_zp = slot >> 2, (slot >> 1) & 1, slot & 1
        for side, ref in ((core, keep_ref), (1 - core, send_ref)):
            for low in range(2):
                rows_at = slice(low * block, (low + 1) * block)
                first = at_y * 16 + (2 * at_zp + low) * 4 + 2 * at_x
                if first < 3 * HEADS:
                    start = pl.multiple_of((first + (side ^ zh ^ low)) * block, block)
                    for lane in range(width // 128):
                        piece = sums_ref[lane, pl.ds(start, block), :]
                        lanes_at = slice(lane * 128, (lane + 1) * 128)
                        ref[slot, rows_at, lanes_at] = piece.astype(ref.dtype)
                else:
                    start = pl.multiple_of((2 * at_x + side) * block, block)
                    piece = out_sums_ref[pl.ds(start, block), low * width : (low + 1) * width]
                    ref[slot, rows_at, :] = piece.astype(ref.dtype)


def join_kernel(total_ref, got_ref, out_ref):
    y, _, zp, zh, _, _ = place()
    lanes = out_ref.shape[1]
    rows, width = got_ref.shape
    is_out = (y == 1) & (zp == 1)
    got = got_ref[...].astype(jnp.float32)
    for side in range(2):
        joined = jnp.where(is_out | (zh == side), total_ref[side], got)
        for lane in range(0, width, lanes):
            first = (side * width + lane) // lanes
            step = 2 * width // lanes
            out_ref[pl.ds(first, rows, stride=step), :] = joined[:, lane : lane + lanes]


def split_form(features, neighbours, conv_taps, norm_gain, qkv_weight, out_weight, cotangent):
    own = features[0, 0]
    pixels, channels = own.shape
    half, width, block = pixels // 2, channels // 2, channels // HEADS
    y, _, zp, zh, x, _ = place()
    narrow_type = jnp.bfloat16
    anywhere = pl.BlockSpec(memory_space=pl.ANY)
    in_vmem = pl.BlockSpec(memory_space=VMEM)
    piece = jax.ShapeDtypeStruct((half, channels), narrow_type)

    band = swap(own, "blk", 1)
    qkv_x = swap(qkv_weight, "fsdp", 2)
    out_x = swap(out_weight, "fsdp", 2)
    halves = cotangent[0, 0].reshape(2, half, channels)
    up_2 = swap(pick(halves, 1 - zp), "tm", 2)

    def conv(far):
        return pl.pallas_call(
            functools.partial(conv_kernel, far),
            out_shape=piece,
            in_specs=[anywhere] * 5,
            out_specs=in_vmem,
            scratch_shapes=[
                pltpu.VMEM((neighbours.shape[1], pixels), jnp.int32),
                pltpu.VMEM((pixels, neighbours.shape[1]), jnp.int32),
                pltpu.VMEM((2 * pixels, channels), narrow_type),
                pltpu.VMEM(conv_taps.shape, jnp.float32),
                pltpu.VMEM((1, channels), jnp.float32),
                pltpu.SemaphoreType.DMA((5,)),
            ],
            compiler_params=pltpu.CompilerParams(vmem_limit_bytes=16 << 20),
            name="conv_far" if far else "conv_near",
        )(neighbours.T, own, band, conv_taps, norm_gain.reshape(1, channels))

    n_other = conv(True)
    row_3 = swap(n_other, "tm", 3)
    row_2 = swap(n_other, "tm", 2)
    n_mine = conv(False)
    row_1 = swap(n_mine, "tm", 1)
    up_own = jnp.stack([pick(halves, zp), up_2])
    up_got = swap(up_own, "tm", 1)
    qkv_c = swap(qkv_weight, "fsdp", 1)
    qkv_xc = swap(qkv_x, "fsdp", 1)
    out_rows = jnp.where(x == zh, out_weight, out_x)
    out_c = swap(out_rows, "fsdp", 1)

    full_qkv, own_qkv = pl.pallas_call(
        weights_kernel,
        out_shape=(
            jax.ShapeDtypeStruct((channels, 3 * width), narrow_type),
            jax.ShapeDtypeStruct((half, 3 * width), narrow_type),
        ),
        in_specs=[in_vmem] + [anywhere] * 4,
        out_specs=(in_vmem,) * 2,
        scratch_shapes=[pltpu.SemaphoreType.DMA((12,))],
        compiler_params=pltpu.CompilerParams(vmem_limit_bytes=16 << 20),
        name="weights",
    )(n_mine, qkv_weight, qkv_x, qkv_c, qkv_xc)
    qkv, weights, attended, normed = pl.pallas_call(
        forward_kernel,
        out_shape=(
            jax.ShapeDtypeStruct((4 * half, 3 * width), narrow_type),
            jax.ShapeDtypeStruct((10, half, width), narrow_type),
            jax.ShapeDtypeStruct((4 * half, width), narrow_type),
            jax.ShapeDtypeStruct((4, half, channels), narrow_type),
        ),
        in_specs=[in_vmem] * 6,
        out_specs=(in_vmem,) * 4,
        compiler_params=pltpu.CompilerParams(vmem_limit_bytes=24 << 20),
        name="forward",
    )(n_mine, row_1, row_2, row_3, own_qkv, full_qkv)
    keep, send = pl.pallas_call(
        backward_kernel,
        out_shape=(
            jax.ShapeDtypeStruct((8, 2 * block, width), jnp.float32),
            jax.ShapeDtypeStruct((8, 2 * block, width), narrow_type),
        ),
        in_specs=[in_vmem] * 8,
        out_specs=(in_vmem, in_vmem),
        scratch_shapes=[
            pltpu.VMEM((4, half, channels), narrow_type),
            pltpu.VMEM((4, half, width), narrow_type),
            pltpu.VMEM((width // 128, 3 * channels, 128), jnp.float32),
            pltpu.VMEM((width, channels), jnp.float32),
        ],
        compiler_params=pltpu.CompilerParams(vmem_limit_bytes=28 << 20),
        name="backward",
    )(up_own, up_got, out_rows, out_c, normed, qkv, weights, attended)

    def narrow(values):
        return values.astype(jnp.bfloat16)

    total = keep + swap(send, "fsdp", 1).astype(jnp.float32)
    total = total.reshape(2, 2, 2, 2 * block, width)
    first, second = total[..., : width // 2], total[..., width // 2 :]
    got_first = swap(narrow(pick(first, 1 - x, 0)), "fsdp", 2)
    got_second = swap(narrow(pick(second, 1 - y, 1)), "blk", 1)
    first = pick(first, x, 0) + got_first.astype(jnp.float32)
    second = pick(second, y, 1) + got_second.astype(jnp.float32)
    got_first = swap(narrow(pick(first, 1 - y, 0)), "blk", 1)
    got_second = swap(narrow(pick(second, 1 - x, 0)), "fsdp", 2)
    first = pick(first, y, 0) + got_first.astype(jnp.float32)
    second = pick(second, x, 0) + got_second.astype(jnp.float32)
    total = jnp.concatenate([first, second], axis=-1)
    total = pick(total, zp) + swap(narrow(pick(total, 1 - zp)), "tm", 2).astype(jnp.float32)
    total = total.reshape(2, block, width)
    cores = lax.axis_size("fsdp")
    crossed = [(i, i ^ cores ^ 1) for i in range(lax.axis_size("tm") * cores)]
    got = lax.ppermute(narrow(pick(total, 1 - zh)), ("tm", "fsdp"), crossed)
    lanes = 128
    out = pl.pallas_call(
        join_kernel,
        out_shape=jax.ShapeDtypeStruct((block * channels // lanes, lanes), jnp.float32),
        in_specs=[in_vmem] * 2,
        out_specs=in_vmem,
        compiler_params=pltpu.CompilerParams(vmem_limit_bytes=4 << 20),
        name="join",
    )(total, got)
    return out.reshape(-1)


def with_halo(cells, sides, width):
    for axis, dim in sides:
        count = lax.axis_size(axis)
        ends = count - 1
        head = lax.slice_in_dim(cells, 0, width, axis=dim)
        tail = lax.slice_in_dim(cells, cells.shape[dim] - width, cells.shape[dim], axis=dim)
        cells = jnp.concatenate(
            [
                lax.ppermute(tail, axis, [(i, (i + 1) % count) for i in range(ends)]),
                cells,
                lax.ppermute(head, axis, [((i + 1) % count, i) for i in range(ends)]),
            ],
            axis=dim,
        )
    return cells


def halved(partial, axis, bit):
    count = lax.axis_size(axis)
    mine = (lax.axis_index(axis) >> bit) & 1
    keep = lax.dynamic_index_in_dim(partial, mine, 0, keepdims=False)
    send = lax.dynamic_index_in_dim(partial, 1 - mine, 0, keepdims=False)
    got = lax.ppermute(send.astype(jnp.bfloat16), axis, [(i, i ^ (1 << bit)) for i in range(count)])
    return keep + got.astype(jnp.float32)


def scattered_sum(summands):
    counts = [lax.axis_size(axis) for axis in ("blk", "tm", "fsdp")]
    bits = [count.bit_length() - 1 for count in counts]
    order = [("fsdp", bit) for bit in range(bits[2])]
    order += [("blk", bit) for bit in range(bits[0])]
    order += [("tm", bit) for bit in range(bits[1])]
    labels = [(axis, bit) for axis, many in zip(("blk", "tm", "fsdp"), bits) for bit in reversed(range(many))]
    partial = summands.reshape((2,) * len(labels) + (-1, 128))
    for axis, bit in order:
        place = labels.index((axis, bit))
        labels.pop(place)
        partial = halved(jnp.moveaxis(partial, place, 0), axis, bit)
    return partial.reshape(-1)


def rounded(values):
    return lax.optimization_barrier(values.astype(jnp.bfloat16)).astype(jnp.float32)


def attend_all(qkv_rows, grad_rows):
    frames, pixels, width = qkv_rows.shape
    channels = width // 3

    def split_heads(block):
        return block.reshape(frames, pixels, HEADS, channels // HEADS).astype(jnp.float32)

    queries = split_heads(qkv_rows[:, :, :channels])
    keys_all = split_heads(qkv_rows[:, :, channels : 2 * channels])
    values = split_heads(qkv_rows[:, :, 2 * channels :])
    grads = split_heads(grad_rows)
    scores = jnp.einsum("tpeh,upeh->petu", queries, keys_all) * 0.125
    causal = jnp.arange(frames)[:, None] >= jnp.arange(frames)[None, :]
    masked = jnp.where(causal, scores, -1e30)
    largest = jnp.max(masked, axis=-1, keepdims=True)
    totals = jnp.sum(jnp.exp(masked - largest), axis=-1, keepdims=True)
    log_total = largest + jnp.log(totals)
    weights = rounded(jnp.exp(masked - log_total))
    attended = jnp.einsum("petu,upeh->tpeh", weights, values)
    dprob = jnp.einsum("tpeh,upeh->petu", grads, values)
    delta = jnp.sum(weights * dprob, axis=-1, keepdims=True)
    dscore = rounded(weights * (dprob - delta) * 0.125)
    grad_query = jnp.einsum("petu,upeh->tpeh", dscore, keys_all)
    grad_key = jnp.einsum("petu,tpeh->upeh", dscore, queries)
    grad_value = jnp.einsum("petu,tpeh->upeh", weights, grads)
    joined = jnp.concatenate(
        [part.reshape(frames, pixels, channels) for part in (grad_query, grad_key, grad_value)],
        axis=-1,
    )
    return (
        attended.reshape(frames, pixels, channels).astype(jnp.bfloat16),
        joined.astype(jnp.bfloat16),
    )


def general_form(features, neighbours, conv_taps, norm_gain, qkv_weight, out_weight, cotangent):
    inputs = features[0, 0]
    upstream = cotangent[0, 0]
    pixels, channels = inputs.shape
    padded = with_halo(inputs, (("blk", 0),), HALO)
    first_pixel = lax.axis_index("blk") * pixels
    local_rows = neighbours - first_pixel + HALO
    inputs_f = inputs.astype(jnp.float32)
    spatial = conv_taps[0] * inputs_f
    for column in range(8):
        spatial = spatial + conv_taps[column + 1] * jnp.take(
            padded, local_rows[:, column], axis=0
        ).astype(jnp.float32)
    hidden_f = rounded(inputs_f + spatial)
    inverse = lax.rsqrt(jnp.mean(hidden_f * hidden_f, axis=-1, keepdims=True) + 1e-05)
    normed = (hidden_f * inverse * norm_gain).astype(jnp.bfloat16)
    full_qkv, full_out = (
        lax.all_gather(qkv_weight, "fsdp", axis=0, tiled=True),
        lax.all_gather(out_weight, "fsdp", axis=0, tiled=True),
    )
    att_grads = jnp.dot(upstream, full_out.T, preferred_element_type=jnp.float32).astype(
        jnp.bfloat16
    )
    swap_normed, swap_grads, swap_upstream = (
        lax.all_to_all(normed[None], "tm", split_axis=1, concat_axis=0, tiled=True),
        lax.all_to_all(att_grads[None], "tm", split_axis=1, concat_axis=0, tiled=True),
        lax.all_to_all(upstream[None], "tm", split_axis=1, concat_axis=0, tiled=True),
    )
    frames = swap_normed.shape[0]
    few_pixels = swap_normed.shape[1]
    flat_normed = swap_normed.reshape(-1, channels)
    qkv_rows = jnp.dot(flat_normed, full_qkv, preferred_element_type=jnp.float32).astype(
        jnp.bfloat16
    )
    qkv_rows = qkv_rows.reshape(frames, few_pixels, 3 * channels)
    attended_x, dqkv_x = attend_all(qkv_rows, swap_grads)
    grad_in = jnp.einsum(
        "pc,pd->cd",
        flat_normed,
        dqkv_x.reshape(-1, 3 * channels),
        preferred_element_type=jnp.float32,
    )
    grad_out = jnp.einsum(
        "pc,pd->cd",
        attended_x.reshape(-1, channels),
        swap_upstream.reshape(-1, channels),
        preferred_element_type=jnp.float32,
    )
    summands = jnp.concatenate([grad_in.reshape(-1), grad_out.reshape(-1)])
    return scattered_sum(summands)


def solution(mesh):
    sizes = mesh.shape

    def per_device(*arrays):
        pixels, channels = arrays[0].shape[-2:]
        devices = sizes["blk"] * sizes["tm"] * sizes["fsdp"]
        fits = (
            sizes["blk"] == 2
            and sizes["tm"] == sizes["fsdp"] == arrays[0].shape[0] * 4
            and devices == 4 * HEADS
            and pixels >= HALO
            and pixels % 32 == 0
            and channels == 64 * HEADS
        )
        if not fits:
            return general_form(*arrays)
        return split_form(*arrays)

    return jax.shard_map(
        per_device,
        mesh=mesh,
        in_specs=(
            P("fsdp", "tm", "blk", None),
            P("blk", None),
            P(),
            P(),
            P("fsdp", None),
            P("fsdp", None),
            P("fsdp", "tm", "blk", None),
        ),
        out_specs=P(("blk", "tm", "fsdp")),
        check_vma=False,
    )
```

```python
import functools

import jax
import jax.numpy as jnp
from jax import lax
from jax.experimental import pallas as pl
from jax.experimental.pallas import tpu as pltpu
from jax.sharding import PartitionSpec as P


HEADS = 8
HALO = 130
VMEM = pltpu.MemorySpace.VMEM


def swap(values, axis, mask):
    return lax.ppermute(values, axis, [(i, i ^ mask) for i in range(lax.axis_size(axis))])


def pick(values, index, dim=0):
    return lax.dynamic_index_in_dim(values, index, dim, keepdims=False)


def place():
    t, f = lax.axis_index("tm"), lax.axis_index("fsdp")
    return lax.axis_index("blk"), t, t >> 1, t & 1, f >> 1, f & 1


def start_all(copies):
    for copy in copies:
        copy.start()


def conv_kernel(far, near_ref, own_ref, band_ref, taps_ref, gain_ref, out_ref, turned_ref):
    y, _, zp, _, _, _ = place()
    pixels, _ = own_ref.shape
    half = pixels // 2
    begin = pl.multiple_of((1 - zp if far else zp) * half, 16)
    turned_ref[...] = near_ref[...].T
    near = turned_ref[pl.ds(begin, half), :]
    neighbours = near.shape[1]
    local = near - y * pixels
    local = jnp.where(local < 0, local + 2 * pixels, local)
    slots = lax.broadcasted_iota(jnp.int32, (half, 2 * pixels), 1)
    chosen = jnp.concatenate(
        [
            jnp.where(local[:, k : k + 1] == slots, 1.0, 0.0).astype(jnp.bfloat16)
            for k in range(neighbours)
        ],
        axis=0,
    )
    table = jnp.concatenate([own_ref[...], band_ref[...]], axis=0)
    gathered = jnp.dot(chosen, table, preferred_element_type=jnp.float32)
    own = own_ref[pl.ds(begin, half), :].astype(jnp.float32)
    spatial = taps_ref[0:1, :] * own
    for k in range(neighbours):
        spatial = spatial + taps_ref[k + 1 : k + 2, :] * gathered[k * half : (k + 1) * half]
    hidden = (own + spatial).astype(jnp.bfloat16).astype(jnp.float32)
    inverse = lax.rsqrt(jnp.mean(hidden * hidden, axis=-1, keepdims=True) + 1e-05)
    out_ref[...] = (hidden * inverse * gain_ref[...]).astype(jnp.bfloat16)


def head_sums(products, width):
    depth = width * 2 // HEADS
    row_head = lax.broadcasted_iota(jnp.int32, (width, width), 0) // depth
    col_head = lax.broadcasted_iota(jnp.int32, (width, width), 1) // depth
    same = jnp.where(row_head == col_head, 0.125, 0.0).astype(jnp.bfloat16)
    pixels = products[0].shape[0]
    stacked = jnp.concatenate(products, axis=0)
    high = stacked.astype(jnp.bfloat16)
    low = (stacked - high.astype(jnp.float32)).astype(jnp.bfloat16)
    total = jnp.dot(high, same, preferred_element_type=jnp.float32)
    total = total + jnp.dot(low, same, preferred_element_type=jnp.float32)
    return [total[i * pixels : (i + 1) * pixels] for i in range(len(products))]


def wide(ref, frame, third, width, pixels):
    rows = ref[frame * pixels : (frame + 1) * pixels, third * width : (third + 1) * width]
    return rows.astype(jnp.float32)


def shard_rows(k, rows):
    _, _, _, _, x, core = place()
    f = (2 * x + core) ^ (2 * (k & 1) + (k >> 1))
    return pl.ds(pl.multiple_of(f * rows, 128), rows)


def weights_kernel(own_ref, *refs):
    shards, refs = refs[:4], refs[4:]
    w_ref, qkv_ref, sems = refs
    _, _, _, zh, _, _ = place()
    width = w_ref.shape[1] // 3
    rows = shards[0].shape[0]
    copies = []
    for k in range(4):
        for m in range(3):
            columns = pl.ds(pl.multiple_of((2 * m + zh) * width, 128), width)
            copies.append(
                pltpu.make_async_copy(
                    shards[k].at[:, columns],
                    w_ref.at[shard_rows(k, rows), pl.ds(m * width, width)],
                    sems.at[3 * k + m],
                )
            )
    start_all(copies)
    for copy in copies:
        copy.wait()
    qkv_ref[...] = jnp.dot(
        own_ref[...], w_ref[...], preferred_element_type=jnp.float32
    ).astype(jnp.bfloat16)


def forward_kernel(own_ref, row_1_ref, row_2_ref, row_3_ref, own_qkv_ref, w_ref, *refs):
    frames = 4
    qkv_ref, weights_ref, attended_ref, n_ref = refs
    _, t, _, _, _, _ = place()
    pixels, channels = own_ref.shape
    width = channels // 2
    others = (row_1_ref, row_2_ref, row_3_ref)
    for i, ref in enumerate((own_ref,) + others):
        n_ref[t ^ i] = ref[...]
    arrived = jnp.concatenate([ref[...] for ref in others], axis=0)
    arrived = jnp.dot(arrived, w_ref[...], preferred_element_type=jnp.float32)
    arrived = arrived.astype(jnp.bfloat16)
    qkv_ref[pl.ds(pl.multiple_of(t * pixels, 16), pixels), :] = own_qkv_ref[...]
    for i in range(1, frames):
        start = pl.multiple_of((t ^ i) * pixels, 16)
        qkv_ref[pl.ds(start, pixels), :] = arrived[(i - 1) * pixels : i * pixels]
    q, k, v = (
        [wide(qkv_ref, i, third, width, pixels) for i in range(frames)] for third in range(3)
    )
    slot = 0
    for i in range(frames):
        scores = head_sums([q[i] * k[u] for u in range(i + 1)], width)
        largest = scores[0]
        for s in scores[1:]:
            largest = jnp.maximum(largest, s)
        powers = [jnp.exp(s - largest) for s in scores]
        total = powers[0]
        for p in powers[1:]:
            total = total + p
        scale = 1.0 / total
        seen = None
        for u in range(i + 1):
            weights = (powers[u] * scale).astype(jnp.bfloat16)
            weights_ref[slot] = weights
            slot += 1
            term = weights.astype(jnp.float32) * v[u]
            seen = term if seen is None else seen + term
        attended_ref[i * pixels : (i + 1) * pixels, :] = seen.astype(jnp.bfloat16)


def backward_kernel(*refs):
    frames = 4
    piece_refs, out_refs, refs = refs[:4], refs[4:6], refs[6:]
    n_ref, qkv_ref, weights_ref, attended_ref, refs = *refs[:4], refs[4:]
    keep_ref, send_ref, u_ref, g_ref, sums_ref, out_sums_ref = refs
    _, t, _, zh, _, core = place()
    _, pixels, channels = n_ref.shape
    width = out_sums_ref.shape[0]
    first, second = out_refs[0][...], out_refs[1][...]
    out_w = jnp.where(
        core == 0,
        jnp.concatenate([first, second], axis=0),
        jnp.concatenate([second, first], axis=0),
    )
    pieces = jnp.concatenate([ref[...] for ref in piece_refs], axis=0)
    products = lax.dot_general(
        pieces, out_w, (((1,), (1,)), ((), ())), preferred_element_type=jnp.float32
    )
    for i, ref in enumerate(piece_refs):
        g_ref[t ^ i] = products[i * pixels : (i + 1) * pixels].astype(jnp.bfloat16)
        u_ref[t ^ i] = ref[...]
    normed = n_ref[...].reshape(frames * pixels, channels)
    upstream = u_ref[...].reshape(frames * pixels, channels)
    g = [g_ref[i].astype(jnp.float32) for i in range(frames)]
    q, k, v = (
        [wide(qkv_ref, i, third, width, pixels) for i in range(frames)] for third in range(3)
    )

    def over_rows(lhs, rhs):
        return lax.dot_general(
            lhs, rhs, (((0,), (0,)), ((), ())), preferred_element_type=jnp.float32
        )

    def plus(total, term):
        return term if total is None else total + term

    def keep_sum(m, pieces):
        pieces = [piece.astype(jnp.bfloat16) for piece in pieces]
        grad = over_rows(normed, jnp.concatenate(pieces, axis=0))
        for lane in range(0, width, 128):
            sums_ref[lane // 128, pl.ds(m, channels, stride=3), :] = grad[:, lane : lane + 128]

    out_sums_ref[...] = over_rows(attended_ref[...], upstream)
    firsts = [i * (i + 1) // 2 for i in range(frames)]
    dv = [None] * frames
    for i in range(frames):
        for u in range(i + 1):
            dv[u] = plus(dv[u], weights_ref[firsts[i] + u].astype(jnp.float32) * g[i])
    keep_sum(2, dv)
    dq, dk = [], [None] * frames
    for i in range(frames):
        dprob = head_sums([g[i] * v[u] for u in range(i + 1)], width)
        weights = [weights_ref[firsts[i] + u].astype(jnp.float32) for u in range(i + 1)]
        delta = weights[0] * dprob[0]
        for u in range(1, i + 1):
            delta = delta + weights[u] * dprob[u]
        grad_q = None
        for u in range(i + 1):
            ds = (weights[u] * (dprob[u] - delta)).astype(jnp.bfloat16).astype(jnp.float32)
            grad_q = plus(grad_q, ds * k[u])
            dk[u] = plus(dk[u], ds * q[i])
        dq.append(grad_q)
    keep_sum(0, dq)
    keep_sum(1, dk)

    block = channels // HEADS
    for slot in range(8):
        at_x, at_y, at_zp = slot >> 2, (slot >> 1) & 1, slot & 1
        for side, ref in ((core, keep_ref), (1 - core, send_ref)):
            for low in range(2):
                rows_at = slice(low * block, (low + 1) * block)
                first = at_y * 16 + (2 * at_zp + low) * 4 + 2 * at_x
                if first < 3 * HEADS:
                    start = pl.multiple_of((first + (side ^ zh ^ low)) * block, block)
                    for lane in range(width // 128):
                        piece = sums_ref[lane, pl.ds(start, block), :]
                        lanes_at = slice(lane * 128, (lane + 1) * 128)
                        ref[slot, rows_at, lanes_at] = piece.astype(ref.dtype)
                else:
                    start = pl.multiple_of((2 * at_x + side) * block, block)
                    piece = out_sums_ref[pl.ds(start, block), low * width : (low + 1) * width]
                    ref[slot, rows_at, :] = piece.astype(ref.dtype)


def join_kernel(total_ref, got_ref, out_ref):
    y, _, zp, zh, _, _ = place()
    lanes = out_ref.shape[1]
    rows, width = got_ref.shape
    is_out = (y == 1) & (zp == 1)
    got = got_ref[...].astype(jnp.float32)
    for side in range(2):
        joined = jnp.where(is_out | (zh == side), total_ref[side], got)
        for lane in range(0, width, lanes):
            first = (side * width + lane) // lanes
            step = 2 * width // lanes
            out_ref[pl.ds(first, rows, stride=step), :] = joined[:, lane : lane + lanes]


def split_form(features, neighbours, conv_taps, norm_gain, qkv_weight, out_weight, cotangent):
    own = features[0, 0]
    pixels, channels = own.shape
    half, width, block = pixels // 2, channels // 2, channels // HEADS
    y, _, zp, zh, x, _ = place()
    narrow_type = jnp.bfloat16
    anywhere = pl.BlockSpec(memory_space=pl.ANY)
    in_vmem = pl.BlockSpec(memory_space=VMEM)
    piece = jax.ShapeDtypeStruct((half, channels), narrow_type)

    band = swap(own, "blk", 1)
    qkv_x = swap(qkv_weight, "fsdp", 2)
    out_x = swap(out_weight, "fsdp", 2)
    halves = cotangent[0, 0].reshape(2, half, channels)
    up_2 = swap(pick(halves, 1 - zp), "tm", 2)

    def conv(far):
        return pl.pallas_call(
            functools.partial(conv_kernel, far),
            out_shape=piece,
            in_specs=[in_vmem] * 5,
            out_specs=in_vmem,
            scratch_shapes=[pltpu.VMEM((pixels, neighbours.shape[1]), jnp.int32)],
            compiler_params=pltpu.CompilerParams(vmem_limit_bytes=16 << 20),
            name="conv_far" if far else "conv_near",
        )(neighbours.T, own, band, conv_taps, norm_gain.reshape(1, channels))

    n_other = conv(True)
    row_3 = swap(n_other, "tm", 3)
    row_2 = swap(n_other, "tm", 2)
    n_mine = conv(False)
    row_1 = swap(n_mine, "tm", 1)
    up_mine = pick(halves, zp)
    up_1 = swap(up_mine, "tm", 1)
    up_3 = swap(up_2, "tm", 1)
    qkv_c = swap(qkv_weight, "fsdp", 1)
    qkv_xc = swap(qkv_x, "fsdp", 1)
    out_rows = jnp.where(x == zh, out_weight, out_x)
    out_c = swap(out_rows, "fsdp", 1)

    full_qkv, own_qkv = pl.pallas_call(
        weights_kernel,
        out_shape=(
            jax.ShapeDtypeStruct((channels, 3 * width), narrow_type),
            jax.ShapeDtypeStruct((half, 3 * width), narrow_type),
        ),
        in_specs=[in_vmem] + [anywhere] * 4,
        out_specs=(in_vmem,) * 2,
        scratch_shapes=[pltpu.SemaphoreType.DMA((12,))],
        compiler_params=pltpu.CompilerParams(vmem_limit_bytes=16 << 20),
        name="weights",
    )(n_mine, qkv_weight, qkv_x, qkv_c, qkv_xc)
    qkv, weights, attended, normed = pl.pallas_call(
        forward_kernel,
        out_shape=(
            jax.ShapeDtypeStruct((4 * half, 3 * width), narrow_type),
            jax.ShapeDtypeStruct((10, half, width), narrow_type),
            jax.ShapeDtypeStruct((4 * half, width), narrow_type),
            jax.ShapeDtypeStruct((4, half, channels), narrow_type),
        ),
        in_specs=[in_vmem] * 6,
        out_specs=(in_vmem,) * 4,
        compiler_params=pltpu.CompilerParams(vmem_limit_bytes=24 << 20),
        name="forward",
    )(n_mine, row_1, row_2, row_3, own_qkv, full_qkv)
    keep, send = pl.pallas_call(
        backward_kernel,
        out_shape=(
            jax.ShapeDtypeStruct((8, 2 * block, width), jnp.float32),
            jax.ShapeDtypeStruct((8, 2 * block, width), narrow_type),
        ),
        in_specs=[in_vmem] * 10,
        out_specs=(in_vmem, in_vmem),
        scratch_shapes=[
            pltpu.VMEM((4, half, channels), narrow_type),
            pltpu.VMEM((4, half, width), narrow_type),
            pltpu.VMEM((width // 128, 3 * channels, 128), jnp.float32),
            pltpu.VMEM((width, channels), jnp.float32),
        ],
        compiler_params=pltpu.CompilerParams(vmem_limit_bytes=28 << 20),
        name="backward",
    )(up_mine, up_1, up_2, up_3, out_rows, out_c, normed, qkv, weights, attended)

    def narrow(values):
        return values.astype(jnp.bfloat16)

    total = keep + swap(send, "fsdp", 1).astype(jnp.float32)
    total = total.reshape(2, 2, 2, 2 * block, width)
    first, second = total[..., : width // 2], total[..., width // 2 :]
    got_first = swap(narrow(pick(first, 1 - x, 0)), "fsdp", 2)
    got_second = swap(narrow(pick(second, 1 - y, 1)), "blk", 1)
    first = pick(first, x, 0) + got_first.astype(jnp.float32)
    second = pick(second, y, 1) + got_second.astype(jnp.float32)
    got_first = swap(narrow(pick(first, 1 - y, 0)), "blk", 1)
    got_second = swap(narrow(pick(second, 1 - x, 0)), "fsdp", 2)
    first = pick(first, y, 0) + got_first.astype(jnp.float32)
    second = pick(second, x, 0) + got_second.astype(jnp.float32)
    total = jnp.concatenate([first, second], axis=-1)
    total = pick(total, zp) + swap(narrow(pick(total, 1 - zp)), "tm", 2).astype(jnp.float32)
    total = total.reshape(2, block, width)
    cores = lax.axis_size("fsdp")
    crossed = [(i, i ^ cores ^ 1) for i in range(lax.axis_size("tm") * cores)]
    got = lax.ppermute(narrow(pick(total, 1 - zh)), ("tm", "fsdp"), crossed)
    lanes = 128
    out = pl.pallas_call(
        join_kernel,
        out_shape=jax.ShapeDtypeStruct((block * channels // lanes, lanes), jnp.float32),
        in_specs=[in_vmem] * 2,
        out_specs=in_vmem,
        compiler_params=pltpu.CompilerParams(vmem_limit_bytes=4 << 20),
        name="join",
    )(total, got)
    return out.reshape(-1)


def with_halo(cells, sides, width):
    for axis, dim in sides:
        count = lax.axis_size(axis)
        ends = count - 1
        head = lax.slice_in_dim(cells, 0, width, axis=dim)
        tail = lax.slice_in_dim(cells, cells.shape[dim] - width, cells.shape[dim], axis=dim)
        cells = jnp.concatenate(
            [
                lax.ppermute(tail, axis, [(i, (i + 1) % count) for i in range(ends)]),
                cells,
                lax.ppermute(head, axis, [((i + 1) % count, i) for i in range(ends)]),
            ],
            axis=dim,
        )
    return cells


def halved(partial, axis, bit):
    count = lax.axis_size(axis)
    mine = (lax.axis_index(axis) >> bit) & 1
    keep = lax.dynamic_index_in_dim(partial, mine, 0, keepdims=False)
    send = lax.dynamic_index_in_dim(partial, 1 - mine, 0, keepdims=False)
    got = lax.ppermute(send.astype(jnp.bfloat16), axis, [(i, i ^ (1 << bit)) for i in range(count)])
    return keep + got.astype(jnp.float32)


def scattered_sum(summands):
    counts = [lax.axis_size(axis) for axis in ("blk", "tm", "fsdp")]
    bits = [count.bit_length() - 1 for count in counts]
    order = [("fsdp", bit) for bit in range(bits[2])]
    order += [("blk", bit) for bit in range(bits[0])]
    order += [("tm", bit) for bit in range(bits[1])]
    labels = [(axis, bit) for axis, many in zip(("blk", "tm", "fsdp"), bits) for bit in reversed(range(many))]
    partial = summands.reshape((2,) * len(labels) + (-1, 128))
    for axis, bit in order:
        place = labels.index((axis, bit))
        labels.pop(place)
        partial = halved(jnp.moveaxis(partial, place, 0), axis, bit)
    return partial.reshape(-1)


def rounded(values):
    return lax.optimization_barrier(values.astype(jnp.bfloat16)).astype(jnp.float32)


def attend_all(qkv_rows, grad_rows):
    frames, pixels, width = qkv_rows.shape
    channels = width // 3

    def split_heads(block):
        return block.reshape(frames, pixels, HEADS, channels // HEADS).astype(jnp.float32)

    queries = split_heads(qkv_rows[:, :, :channels])
    keys_all = split_heads(qkv_rows[:, :, channels : 2 * channels])
    values = split_heads(qkv_rows[:, :, 2 * channels :])
    grads = split_heads(grad_rows)
    scores = jnp.einsum("tpeh,upeh->petu", queries, keys_all) * 0.125
    causal = jnp.arange(frames)[:, None] >= jnp.arange(frames)[None, :]
    masked = jnp.where(causal, scores, -1e30)
    largest = jnp.max(masked, axis=-1, keepdims=True)
    totals = jnp.sum(jnp.exp(masked - largest), axis=-1, keepdims=True)
    log_total = largest + jnp.log(totals)
    weights = rounded(jnp.exp(masked - log_total))
    attended = jnp.einsum("petu,upeh->tpeh", weights, values)
    dprob = jnp.einsum("tpeh,upeh->petu", grads, values)
    delta = jnp.sum(weights * dprob, axis=-1, keepdims=True)
    dscore = rounded(weights * (dprob - delta) * 0.125)
    grad_query = jnp.einsum("petu,upeh->tpeh", dscore, keys_all)
    grad_key = jnp.einsum("petu,tpeh->upeh", dscore, queries)
    grad_value = jnp.einsum("petu,tpeh->upeh", weights, grads)
    joined = jnp.concatenate(
        [part.reshape(frames, pixels, channels) for part in (grad_query, grad_key, grad_value)],
        axis=-1,
    )
    return (
        attended.reshape(frames, pixels, channels).astype(jnp.bfloat16),
        joined.astype(jnp.bfloat16),
    )


def general_form(features, neighbours, conv_taps, norm_gain, qkv_weight, out_weight, cotangent):
    inputs = features[0, 0]
    upstream = cotangent[0, 0]
    pixels, channels = inputs.shape
    padded = with_halo(inputs, (("blk", 0),), HALO)
    first_pixel = lax.axis_index("blk") * pixels
    local_rows = neighbours - first_pixel + HALO
    inputs_f = inputs.astype(jnp.float32)
    spatial = conv_taps[0] * inputs_f
    for column in range(8):
        spatial = spatial + conv_taps[column + 1] * jnp.take(
            padded, local_rows[:, column], axis=0
        ).astype(jnp.float32)
    hidden_f = rounded(inputs_f + spatial)
    inverse = lax.rsqrt(jnp.mean(hidden_f * hidden_f, axis=-1, keepdims=True) + 1e-05)
    normed = (hidden_f * inverse * norm_gain).astype(jnp.bfloat16)
    full_qkv, full_out = (
        lax.all_gather(qkv_weight, "fsdp", axis=0, tiled=True),
        lax.all_gather(out_weight, "fsdp", axis=0, tiled=True),
    )
    att_grads = jnp.dot(upstream, full_out.T, preferred_element_type=jnp.float32).astype(
        jnp.bfloat16
    )
    swap_normed, swap_grads, swap_upstream = (
        lax.all_to_all(normed[None], "tm", split_axis=1, concat_axis=0, tiled=True),
        lax.all_to_all(att_grads[None], "tm", split_axis=1, concat_axis=0, tiled=True),
        lax.all_to_all(upstream[None], "tm", split_axis=1, concat_axis=0, tiled=True),
    )
    frames = swap_normed.shape[0]
    few_pixels = swap_normed.shape[1]
    flat_normed = swap_normed.reshape(-1, channels)
    qkv_rows = jnp.dot(flat_normed, full_qkv, preferred_element_type=jnp.float32).astype(
        jnp.bfloat16
    )
    qkv_rows = qkv_rows.reshape(frames, few_pixels, 3 * channels)
    attended_x, dqkv_x = attend_all(qkv_rows, swap_grads)
    grad_in = jnp.einsum(
        "pc,pd->cd",
        flat_normed,
        dqkv_x.reshape(-1, 3 * channels),
        preferred_element_type=jnp.float32,
    )
    grad_out = jnp.einsum(
        "pc,pd->cd",
        attended_x.reshape(-1, channels),
        swap_upstream.reshape(-1, channels),
        preferred_element_type=jnp.float32,
    )
    summands = jnp.concatenate([grad_in.reshape(-1), grad_out.reshape(-1)])
    return scattered_sum(summands)


def solution(mesh):
    sizes = mesh.shape

    def per_device(*arrays):
        pixels, channels = arrays[0].shape[-2:]
        devices = sizes["blk"] * sizes["tm"] * sizes["fsdp"]
        fits = (
            sizes["blk"] == 2
            and sizes["tm"] == sizes["fsdp"] == arrays[0].shape[0] * 4
            and devices == 4 * HEADS
            and pixels >= HALO
            and pixels % 32 == 0
            and channels == 64 * HEADS
        )
        if not fits:
            return general_form(*arrays)
        return split_form(*arrays)

    return jax.shard_map(
        per_device,
        mesh=mesh,
        in_specs=(
            P("fsdp", "tm", "blk", None),
            P("blk", None),
            P(),
            P(),
            P("fsdp", None),
            P("fsdp", None),
            P("fsdp", "tm", "blk", None),
        ),
        out_specs=P(("blk", "tm", "fsdp")),
        check_vma=False,
    )
```

```python
import functools

import jax
import jax.numpy as jnp
from jax import lax
from jax.experimental import pallas as pl
from jax.experimental.pallas import tpu as pltpu
from jax.sharding import PartitionSpec as P


HEADS = 8
HALO = 130
VMEM = pltpu.MemorySpace.VMEM


def swap(values, axis, mask):
    return lax.ppermute(values, axis, [(i, i ^ mask) for i in range(lax.axis_size(axis))])


def pick(values, index, dim=0):
    return lax.dynamic_index_in_dim(values, index, dim, keepdims=False)


def place():
    t, f = lax.axis_index("tm"), lax.axis_index("fsdp")
    return lax.axis_index("blk"), t, t >> 1, t & 1, f >> 1, f & 1


def start_all(copies):
    for copy in copies:
        copy.start()


def conv_kernel(far, near_ref, own_ref, band_ref, taps_ref, gain_ref, out_ref, turned_ref):
    y, _, zp, _, _, _ = place()
    pixels, _ = own_ref.shape
    half = pixels // 2
    begin = pl.multiple_of((1 - zp if far else zp) * half, 16)
    turned_ref[...] = near_ref[...].T
    near = turned_ref[pl.ds(begin, half), :]
    neighbours = near.shape[1]
    local = near - y * pixels
    local = jnp.where(local < 0, local + 2 * pixels, local)
    slots = lax.broadcasted_iota(jnp.int32, (half, 2 * pixels), 1)
    chosen = jnp.concatenate(
        [
            jnp.where(local[:, k : k + 1] == slots, 1.0, 0.0).astype(jnp.bfloat16)
            for k in range(neighbours)
        ],
        axis=0,
    )
    table = jnp.concatenate([own_ref[...], band_ref[...]], axis=0)
    gathered = jnp.dot(chosen, table, preferred_element_type=jnp.float32)
    own = own_ref[pl.ds(begin, half), :].astype(jnp.float32)
    spatial = taps_ref[0:1, :] * own
    for k in range(neighbours):
        spatial = spatial + taps_ref[k + 1 : k + 2, :] * gathered[k * half : (k + 1) * half]
    hidden = (own + spatial).astype(jnp.bfloat16).astype(jnp.float32)
    inverse = lax.rsqrt(jnp.mean(hidden * hidden, axis=-1, keepdims=True) + 1e-05)
    out_ref[...] = (hidden * inverse * gain_ref[...]).astype(jnp.bfloat16)


def head_sums(products, width):
    depth = width * 2 // HEADS
    row_head = lax.broadcasted_iota(jnp.int32, (width, width), 0) // depth
    col_head = lax.broadcasted_iota(jnp.int32, (width, width), 1) // depth
    same = jnp.where(row_head == col_head, 0.125, 0.0).astype(jnp.bfloat16)
    pixels = products[0].shape[0]
    stacked = jnp.concatenate(products, axis=0)
    high = stacked.astype(jnp.bfloat16)
    low = (stacked - high.astype(jnp.float32)).astype(jnp.bfloat16)
    total = jnp.dot(high, same, preferred_element_type=jnp.float32)
    total = total + jnp.dot(low, same, preferred_element_type=jnp.float32)
    return [total[i * pixels : (i + 1) * pixels] for i in range(len(products))]


def wide(ref, frame, third, width, pixels):
    rows = ref[frame * pixels : (frame + 1) * pixels, third * width : (third + 1) * width]
    return rows.astype(jnp.float32)


def shard_rows(k, rows):
    _, _, _, _, x, core = place()
    f = (2 * x + core) ^ (2 * (k & 1) + (k >> 1))
    return pl.ds(pl.multiple_of(f * rows, 128), rows)


def weights_kernel(own_ref, *refs):
    shards, refs = refs[:4], refs[4:]
    w_ref, qkv_ref, sems = refs
    _, _, _, zh, _, _ = place()
    width = w_ref.shape[1] // 3
    rows = shards[0].shape[0]
    copies = []
    for k in range(4):
        for m in range(3):
            columns = pl.ds(pl.multiple_of((2 * m + zh) * width, 128), width)
            copies.append(
                pltpu.make_async_copy(
                    shards[k].at[:, columns],
                    w_ref.at[shard_rows(k, rows), pl.ds(m * width, width)],
                    sems.at[3 * k + m],
                )
            )
    start_all(copies)
    for copy in copies:
        copy.wait()
    qkv_ref[...] = jnp.dot(
        own_ref[...], w_ref[...], preferred_element_type=jnp.float32
    ).astype(jnp.bfloat16)


def forward_kernel(own_ref, row_1_ref, row_2_ref, row_3_ref, own_qkv_ref, w_ref, *refs):
    frames = 4
    qkv_ref, weights_ref, attended_ref, n_ref = refs
    _, t, _, _, _, _ = place()
    pixels, channels = own_ref.shape
    width = channels // 2
    others = (row_1_ref, row_2_ref, row_3_ref)
    for i, ref in enumerate((own_ref,) + others):
        n_ref[t ^ i] = ref[...]
    arrived = jnp.concatenate([ref[...] for ref in others], axis=0)
    arrived = jnp.dot(arrived, w_ref[...], preferred_element_type=jnp.float32)
    arrived = arrived.astype(jnp.bfloat16)
    qkv_ref[pl.ds(pl.multiple_of(t * pixels, 16), pixels), :] = own_qkv_ref[...]
    for i in range(1, frames):
        start = pl.multiple_of((t ^ i) * pixels, 16)
        qkv_ref[pl.ds(start, pixels), :] = arrived[(i - 1) * pixels : i * pixels]
    q, k, v = (
        [wide(qkv_ref, i, third, width, pixels) for i in range(frames)] for third in range(3)
    )
    slot = 0
    for i in range(frames):
        scores = head_sums([q[i] * k[u] for u in range(i + 1)], width)
        largest = scores[0]
        for s in scores[1:]:
            largest = jnp.maximum(largest, s)
        powers = [jnp.exp(s - largest) for s in scores]
        total = powers[0]
        for p in powers[1:]:
            total = total + p
        scale = 1.0 / total
        seen = None
        for u in range(i + 1):
            weights = (powers[u] * scale).astype(jnp.bfloat16)
            weights_ref[slot] = weights
            slot += 1
            term = weights.astype(jnp.float32) * v[u]
            seen = term if seen is None else seen + term
        attended_ref[i * pixels : (i + 1) * pixels, :] = seen.astype(jnp.bfloat16)


def backward_kernel(*refs):
    frames = 4
    piece_refs, out_refs, refs = refs[:4], refs[4:6], refs[6:]
    n_ref, qkv_ref, weights_ref, attended_ref, refs = *refs[:4], refs[4:]
    keep_refs, send_refs, (u_ref, g_ref, sums_ref, out_sums_ref) = refs[:2], refs[2:4], refs[4:]
    _, t, _, zh, _, core = place()
    _, pixels, channels = n_ref.shape
    width = out_sums_ref.shape[0]
    first, second = out_refs[0][...], out_refs[1][...]
    out_w = jnp.where(
        core == 0,
        jnp.concatenate([first, second], axis=0),
        jnp.concatenate([second, first], axis=0),
    )
    pieces = jnp.concatenate([ref[...] for ref in piece_refs], axis=0)
    products = lax.dot_general(
        pieces, out_w, (((1,), (1,)), ((), ())), preferred_element_type=jnp.float32
    )
    for i, ref in enumerate(piece_refs):
        g_ref[t ^ i] = products[i * pixels : (i + 1) * pixels].astype(jnp.bfloat16)
        u_ref[t ^ i] = ref[...]
    normed = n_ref[...].reshape(frames * pixels, channels)
    upstream = u_ref[...].reshape(frames * pixels, channels)
    g = [g_ref[i].astype(jnp.float32) for i in range(frames)]
    q, k, v = (
        [wide(qkv_ref, i, third, width, pixels) for i in range(frames)] for third in range(3)
    )

    def over_rows(lhs, rhs):
        return lax.dot_general(
            lhs, rhs, (((0,), (0,)), ((), ())), preferred_element_type=jnp.float32
        )

    def plus(total, term):
        return term if total is None else total + term

    def keep_sum(m, pieces):
        pieces = [piece.astype(jnp.bfloat16) for piece in pieces]
        grad = over_rows(normed, jnp.concatenate(pieces, axis=0))
        for lane in range(0, width, 128):
            sums_ref[lane // 128, pl.ds(m, channels, stride=3), :] = grad[:, lane : lane + 128]

    out_sums_ref[...] = over_rows(attended_ref[...], upstream)
    firsts = [i * (i + 1) // 2 for i in range(frames)]
    dv = [None] * frames
    for i in range(frames):
        for u in range(i + 1):
            dv[u] = plus(dv[u], weights_ref[firsts[i] + u].astype(jnp.float32) * g[i])
    keep_sum(2, dv)
    dq, dk = [], [None] * frames
    for i in range(frames):
        dprob = head_sums([g[i] * v[u] for u in range(i + 1)], width)
        weights = [weights_ref[firsts[i] + u].astype(jnp.float32) for u in range(i + 1)]
        delta = weights[0] * dprob[0]
        for u in range(1, i + 1):
            delta = delta + weights[u] * dprob[u]
        grad_q = None
        for u in range(i + 1):
            ds = (weights[u] * (dprob[u] - delta)).astype(jnp.bfloat16).astype(jnp.float32)
            grad_q = plus(grad_q, ds * k[u])
            dk[u] = plus(dk[u], ds * q[i])
        dq.append(grad_q)
    keep_sum(0, dq)
    keep_sum(1, dk)

    block = channels // HEADS
    for slot in range(8):
        at_x, at_y, at_zp = slot >> 2, (slot >> 1) & 1, slot & 1
        places = ((at_x, at_y, at_zp), (at_y, at_x, at_zp))
        for side, path_refs in ((1 - core, send_refs), (core, keep_refs)):
            for low in range(2):
                rows_at = slice(low * block, (low + 1) * block)
                first = at_y * 16 + (2 * at_zp + low) * 4 + 2 * at_x
                for path, ref in enumerate(path_refs):
                    if first < 3 * HEADS:
                        start = pl.multiple_of((first + (side ^ zh ^ low)) * block, block)
                        piece = sums_ref[path, pl.ds(start, block), :]
                    else:
                        start = pl.multiple_of((2 * at_x + side) * block, block)
                        lanes_at = low * width + path * 128
                        piece = out_sums_ref[pl.ds(start, block), lanes_at : lanes_at + 128]
                    ref[(*places[path], rows_at)] = piece.astype(ref.dtype)


def join_kernel(first_ref, second_ref, got_ref, out_ref):
    y, _, zp, zh, _, _ = place()
    paths, rows, _ = got_ref.shape
    is_out = (y == 1) & (zp == 1)
    for path, total_ref in enumerate((first_ref, second_ref)):
        got = got_ref[path].astype(jnp.float32)
        for side in range(2):
            mine = total_ref[side * rows : (side + 1) * rows, :]
            joined = jnp.where(is_out | (zh == side), mine, got)
            out_ref[pl.ds(side * paths + path, rows, stride=2 * paths), :] = joined


def split_form(features, neighbours, conv_taps, norm_gain, qkv_weight, out_weight, cotangent):
    own = features[0, 0]
    pixels, channels = own.shape
    half, width, block = pixels // 2, channels // 2, channels // HEADS
    y, _, zp, zh, x, _ = place()
    narrow_type = jnp.bfloat16
    anywhere = pl.BlockSpec(memory_space=pl.ANY)
    in_vmem = pl.BlockSpec(memory_space=VMEM)
    piece = jax.ShapeDtypeStruct((half, channels), narrow_type)

    band = swap(own, "blk", 1)
    qkv_x = swap(qkv_weight, "fsdp", 2)
    out_x = swap(out_weight, "fsdp", 2)
    halves = cotangent[0, 0].reshape(2, half, channels)
    up_2 = swap(pick(halves, 1 - zp), "tm", 2)

    def conv(far):
        return pl.pallas_call(
            functools.partial(conv_kernel, far),
            out_shape=piece,
            in_specs=[in_vmem] * 5,
            out_specs=in_vmem,
            scratch_shapes=[pltpu.VMEM((pixels, neighbours.shape[1]), jnp.int32)],
            compiler_params=pltpu.CompilerParams(vmem_limit_bytes=16 << 20),
            name="conv_far" if far else "conv_near",
        )(neighbours.T, own, band, conv_taps, norm_gain.reshape(1, channels))

    n_other = conv(True)
    row_3 = swap(n_other, "tm", 3)
    row_2 = swap(n_other, "tm", 2)
    n_mine = conv(False)
    row_1 = swap(n_mine, "tm", 1)
    later, _ = lax.optimization_barrier((halves, n_other))
    up_mine = pick(later, zp)
    up_1 = swap(up_mine, "tm", 1)
    up_3 = swap(up_2, "tm", 1)
    qkv_c = swap(qkv_weight, "fsdp", 1)
    qkv_xc = swap(qkv_x, "fsdp", 1)
    out_rows = jnp.where(x == zh, out_weight, out_x)
    out_c = swap(out_rows, "fsdp", 1)

    full_qkv, own_qkv = pl.pallas_call(
        weights_kernel,
        out_shape=(
            jax.ShapeDtypeStruct((channels, 3 * width), narrow_type),
            jax.ShapeDtypeStruct((half, 3 * width), narrow_type),
        ),
        in_specs=[in_vmem] + [anywhere] * 4,
        out_specs=(in_vmem,) * 2,
        scratch_shapes=[pltpu.SemaphoreType.DMA((12,))],
        compiler_params=pltpu.CompilerParams(vmem_limit_bytes=16 << 20),
        name="weights",
    )(n_mine, qkv_weight, qkv_x, qkv_c, qkv_xc)
    qkv, weights, attended, normed = pl.pallas_call(
        forward_kernel,
        out_shape=(
            jax.ShapeDtypeStruct((4 * half, 3 * width), narrow_type),
            jax.ShapeDtypeStruct((10, half, width), narrow_type),
            jax.ShapeDtypeStruct((4 * half, width), narrow_type),
            jax.ShapeDtypeStruct((4, half, channels), narrow_type),
        ),
        in_specs=[in_vmem] * 6,
        out_specs=(in_vmem,) * 4,
        compiler_params=pltpu.CompilerParams(vmem_limit_bytes=24 << 20),
        name="forward",
    )(n_mine, row_1, row_2, row_3, own_qkv, full_qkv)
    *keep, send_0, send_1 = pl.pallas_call(
        backward_kernel,
        out_shape=(
            *(jax.ShapeDtypeStruct((2, 2, 2, 2 * block, 128), jnp.float32),) * 2,
            *(jax.ShapeDtypeStruct((2, 2, 2, 2 * block, 128), narrow_type),) * 2,
        ),
        in_specs=[in_vmem] * 10,
        out_specs=(in_vmem,) * 4,
        scratch_shapes=[
            pltpu.VMEM((4, half, channels), narrow_type),
            pltpu.VMEM((4, half, width), narrow_type),
            pltpu.VMEM((width // 128, 3 * channels, 128), jnp.float32),
            pltpu.VMEM((width, channels), jnp.float32),
        ],
        compiler_params=pltpu.CompilerParams(vmem_limit_bytes=28 << 20),
        name="backward",
    )(up_mine, up_1, up_2, up_3, out_rows, out_c, normed, qkv, weights, attended)

    def narrow(values):
        return values.astype(jnp.bfloat16)

    hops = (("fsdp", 2, x), ("blk", 1, y))
    paths = [
        total + swap(send, "fsdp", 1).astype(jnp.float32)
        for total, send in zip(keep, (send_0, send_1))
    ]
    for stage in range(2):
        for path in range(2):
            axis, mask, index = hops[path ^ stage]
            got = swap(narrow(pick(paths[path], 1 - index)), axis, mask)
            paths[path] = pick(paths[path], index) + got.astype(jnp.float32)
    for path in range(2):
        got = swap(narrow(pick(paths[path], 1 - zp)), "tm", 2)
        paths[path] = pick(paths[path], zp) + got.astype(jnp.float32)
    far = jnp.stack([narrow(pick(total.reshape(2, block, 128), 1 - zh)) for total in paths])
    cores = lax.axis_size("fsdp")
    crossed = [(i, i ^ cores ^ 1) for i in range(lax.axis_size("tm") * cores)]
    got = lax.ppermute(far, ("tm", "fsdp"), crossed)
    out = pl.pallas_call(
        join_kernel,
        out_shape=jax.ShapeDtypeStruct((block * channels // 128, 128), jnp.float32),
        in_specs=[in_vmem] * 3,
        out_specs=in_vmem,
        compiler_params=pltpu.CompilerParams(vmem_limit_bytes=4 << 20),
        name="join",
    )(*paths, got)
    return out.reshape(-1)


def with_halo(cells, sides, width):
    for axis, dim in sides:
        count = lax.axis_size(axis)
        ends = count - 1
        head = lax.slice_in_dim(cells, 0, width, axis=dim)
        tail = lax.slice_in_dim(cells, cells.shape[dim] - width, cells.shape[dim], axis=dim)
        cells = jnp.concatenate(
            [
                lax.ppermute(tail, axis, [(i, (i + 1) % count) for i in range(ends)]),
                cells,
                lax.ppermute(head, axis, [((i + 1) % count, i) for i in range(ends)]),
            ],
            axis=dim,
        )
    return cells


def halved(partial, axis, bit):
    count = lax.axis_size(axis)
    mine = (lax.axis_index(axis) >> bit) & 1
    keep = lax.dynamic_index_in_dim(partial, mine, 0, keepdims=False)
    send = lax.dynamic_index_in_dim(partial, 1 - mine, 0, keepdims=False)
    got = lax.ppermute(send.astype(jnp.bfloat16), axis, [(i, i ^ (1 << bit)) for i in range(count)])
    return keep + got.astype(jnp.float32)


def scattered_sum(summands):
    counts = [lax.axis_size(axis) for axis in ("blk", "tm", "fsdp")]
    bits = [count.bit_length() - 1 for count in counts]
    order = [("fsdp", bit) for bit in range(bits[2])]
    order += [("blk", bit) for bit in range(bits[0])]
    order += [("tm", bit) for bit in range(bits[1])]
    labels = [(axis, bit) for axis, many in zip(("blk", "tm", "fsdp"), bits) for bit in reversed(range(many))]
    partial = summands.reshape((2,) * len(labels) + (-1, 128))
    for axis, bit in order:
        place = labels.index((axis, bit))
        labels.pop(place)
        partial = halved(jnp.moveaxis(partial, place, 0), axis, bit)
    return partial.reshape(-1)


def rounded(values):
    return lax.optimization_barrier(values.astype(jnp.bfloat16)).astype(jnp.float32)


def attend_all(qkv_rows, grad_rows):
    frames, pixels, width = qkv_rows.shape
    channels = width // 3

    def split_heads(block):
        return block.reshape(frames, pixels, HEADS, channels // HEADS).astype(jnp.float32)

    queries = split_heads(qkv_rows[:, :, :channels])
    keys_all = split_heads(qkv_rows[:, :, channels : 2 * channels])
    values = split_heads(qkv_rows[:, :, 2 * channels :])
    grads = split_heads(grad_rows)
    scores = jnp.einsum("tpeh,upeh->petu", queries, keys_all) * 0.125
    causal = jnp.arange(frames)[:, None] >= jnp.arange(frames)[None, :]
    masked = jnp.where(causal, scores, -1e30)
    largest = jnp.max(masked, axis=-1, keepdims=True)
    totals = jnp.sum(jnp.exp(masked - largest), axis=-1, keepdims=True)
    log_total = largest + jnp.log(totals)
    weights = rounded(jnp.exp(masked - log_total))
    attended = jnp.einsum("petu,upeh->tpeh", weights, values)
    dprob = jnp.einsum("tpeh,upeh->petu", grads, values)
    delta = jnp.sum(weights * dprob, axis=-1, keepdims=True)
    dscore = rounded(weights * (dprob - delta) * 0.125)
    grad_query = jnp.einsum("petu,upeh->tpeh", dscore, keys_all)
    grad_key = jnp.einsum("petu,tpeh->upeh", dscore, queries)
    grad_value = jnp.einsum("petu,tpeh->upeh", weights, grads)
    joined = jnp.concatenate(
        [part.reshape(frames, pixels, channels) for part in (grad_query, grad_key, grad_value)],
        axis=-1,
    )
    return (
        attended.reshape(frames, pixels, channels).astype(jnp.bfloat16),
        joined.astype(jnp.bfloat16),
    )


def general_form(features, neighbours, conv_taps, norm_gain, qkv_weight, out_weight, cotangent):
    inputs = features[0, 0]
    upstream = cotangent[0, 0]
    pixels, channels = inputs.shape
    padded = with_halo(inputs, (("blk", 0),), HALO)
    first_pixel = lax.axis_index("blk") * pixels
    local_rows = neighbours - first_pixel + HALO
    inputs_f = inputs.astype(jnp.float32)
    spatial = conv_taps[0] * inputs_f
    for column in range(8):
        spatial = spatial + conv_taps[column + 1] * jnp.take(
            padded, local_rows[:, column], axis=0
        ).astype(jnp.float32)
    hidden_f = rounded(inputs_f + spatial)
    inverse = lax.rsqrt(jnp.mean(hidden_f * hidden_f, axis=-1, keepdims=True) + 1e-05)
    normed = (hidden_f * inverse * norm_gain).astype(jnp.bfloat16)
    full_qkv, full_out = (
        lax.all_gather(qkv_weight, "fsdp", axis=0, tiled=True),
        lax.all_gather(out_weight, "fsdp", axis=0, tiled=True),
    )
    att_grads = jnp.dot(upstream, full_out.T, preferred_element_type=jnp.float32).astype(
        jnp.bfloat16
    )
    swap_normed, swap_grads, swap_upstream = (
        lax.all_to_all(normed[None], "tm", split_axis=1, concat_axis=0, tiled=True),
        lax.all_to_all(att_grads[None], "tm", split_axis=1, concat_axis=0, tiled=True),
        lax.all_to_all(upstream[None], "tm", split_axis=1, concat_axis=0, tiled=True),
    )
    frames = swap_normed.shape[0]
    few_pixels = swap_normed.shape[1]
    flat_normed = swap_normed.reshape(-1, channels)
    qkv_rows = jnp.dot(flat_normed, full_qkv, preferred_element_type=jnp.float32).astype(
        jnp.bfloat16
    )
    qkv_rows = qkv_rows.reshape(frames, few_pixels, 3 * channels)
    attended_x, dqkv_x = attend_all(qkv_rows, swap_grads)
    grad_in = jnp.einsum(
        "pc,pd->cd",
        flat_normed,
        dqkv_x.reshape(-1, 3 * channels),
        preferred_element_type=jnp.float32,
    )
    grad_out = jnp.einsum(
        "pc,pd->cd",
        attended_x.reshape(-1, channels),
        swap_upstream.reshape(-1, channels),
        preferred_element_type=jnp.float32,
    )
    summands = jnp.concatenate([grad_in.reshape(-1), grad_out.reshape(-1)])
    return scattered_sum(summands)


def solution(mesh):
    sizes = mesh.shape

    def per_device(*arrays):
        pixels, channels = arrays[0].shape[-2:]
        devices = sizes["blk"] * sizes["tm"] * sizes["fsdp"]
        fits = (
            sizes["blk"] == 2
            and sizes["tm"] == sizes["fsdp"] == arrays[0].shape[0] * 4
            and devices == 4 * HEADS
            and pixels >= HALO
            and pixels % 32 == 0
            and channels == 64 * HEADS
        )
        if not fits:
            return general_form(*arrays)
        return split_form(*arrays)

    return jax.shard_map(
        per_device,
        mesh=mesh,
        in_specs=(
            P("fsdp", "tm", "blk", None),
            P("blk", None),
            P(),
            P(),
            P("fsdp", None),
            P("fsdp", None),
            P("fsdp", "tm", "blk", None),
        ),
        out_specs=P(("blk", "tm", "fsdp")),
        check_vma=False,
    )
```

```python
import functools

import jax
import jax.numpy as jnp
from jax import lax
from jax.experimental import pallas as pl
from jax.experimental.pallas import tpu as pltpu
from jax.sharding import PartitionSpec as P


HEADS = 8
HALO = 130
VMEM = pltpu.MemorySpace.VMEM

CROSSED = (1, 1, 1, 1)


def swap(values, axis, mask):
    return lax.ppermute(values, axis, [(i, i ^ mask) for i in range(lax.axis_size(axis))])


def hop(values, axis, mask, crossed):
    cores = lax.axis_size("fsdp")
    if axis == "fsdp":
        return swap(values, axis, mask ^ crossed)
    pairs = [(i, i ^ mask * cores ^ crossed) for i in range(lax.axis_size(axis) * cores)]
    return lax.ppermute(values, (axis, "fsdp"), pairs)


def pick(values, index, dim=0):
    return lax.dynamic_index_in_dim(values, index, dim, keepdims=False)


def place():
    t, f = lax.axis_index("tm"), lax.axis_index("fsdp")
    return lax.axis_index("blk"), t, t >> 1, t & 1, f >> 1, f & 1


def start_all(copies):
    for copy in copies:
        copy.start()


def conv_kernel(far, near_ref, own_ref, band_ref, taps_ref, gain_ref, out_ref, turned_ref):
    y, _, zp, _, _, _ = place()
    pixels, _ = own_ref.shape
    half = pixels // 2
    begin = pl.multiple_of((1 - zp if far else zp) * half, 16)
    turned_ref[...] = near_ref[...].T
    near = turned_ref[pl.ds(begin, half), :]
    neighbours = near.shape[1]
    local = near - y * pixels
    local = jnp.where(local < 0, local + 2 * pixels, local)
    slots = lax.broadcasted_iota(jnp.int32, (half, 2 * pixels), 1)
    chosen = jnp.concatenate(
        [
            jnp.where(local[:, k : k + 1] == slots, 1.0, 0.0).astype(jnp.bfloat16)
            for k in range(neighbours)
        ],
        axis=0,
    )
    table = jnp.concatenate([own_ref[...], band_ref[...]], axis=0)
    gathered = jnp.dot(chosen, table, preferred_element_type=jnp.float32)
    own = own_ref[pl.ds(begin, half), :].astype(jnp.float32)
    spatial = taps_ref[0:1, :] * own
    for k in range(neighbours):
        spatial = spatial + taps_ref[k + 1 : k + 2, :] * gathered[k * half : (k + 1) * half]
    hidden = (own + spatial).astype(jnp.bfloat16).astype(jnp.float32)
    inverse = lax.rsqrt(jnp.mean(hidden * hidden, axis=-1, keepdims=True) + 1e-05)
    out_ref[...] = (hidden * inverse * gain_ref[...]).astype(jnp.bfloat16)


def head_sums(products, width):
    depth = width * 2 // HEADS
    row_head = lax.broadcasted_iota(jnp.int32, (width, width), 0) // depth
    col_head = lax.broadcasted_iota(jnp.int32, (width, width), 1) // depth
    same = jnp.where(row_head == col_head, 0.125, 0.0).astype(jnp.bfloat16)
    pixels = products[0].shape[0]
    stacked = jnp.concatenate(products, axis=0)
    high = stacked.astype(jnp.bfloat16)
    low = (stacked - high.astype(jnp.float32)).astype(jnp.bfloat16)
    total = jnp.dot(high, same, preferred_element_type=jnp.float32)
    total = total + jnp.dot(low, same, preferred_element_type=jnp.float32)
    return [total[i * pixels : (i + 1) * pixels] for i in range(len(products))]


def wide(ref, frame, third, width, pixels):
    rows = ref[frame * pixels : (frame + 1) * pixels, third * width : (third + 1) * width]
    return rows.astype(jnp.float32)


def shard_rows(k, rows):
    _, _, _, _, x, core = place()
    f = (2 * x + core) ^ (2 * (k & 1) + (k >> 1))
    return pl.ds(pl.multiple_of(f * rows, 128), rows)


def weights_kernel(own_ref, *refs):
    shards, refs = refs[:4], refs[4:]
    w_ref, qkv_ref, sems = refs
    _, _, _, zh, _, _ = place()
    width = w_ref.shape[1] // 3
    rows = shards[0].shape[0]
    copies = []
    for k in range(4):
        for m in range(3):
            columns = pl.ds(pl.multiple_of((2 * m + zh) * width, 128), width)
            copies.append(
                pltpu.make_async_copy(
                    shards[k].at[:, columns],
                    w_ref.at[shard_rows(k, rows), pl.ds(m * width, width)],
                    sems.at[3 * k + m],
                )
            )
    start_all(copies)
    for copy in copies:
        copy.wait()
    qkv_ref[...] = jnp.dot(
        own_ref[...], w_ref[...], preferred_element_type=jnp.float32
    ).astype(jnp.bfloat16)


def forward_kernel(own_ref, row_1_ref, row_2_ref, row_3_ref, own_qkv_ref, w_ref, *refs):
    frames = 4
    qkv_ref, weights_ref, attended_ref, n_ref = refs
    _, t, _, _, _, _ = place()
    pixels, channels = own_ref.shape
    width = channels // 2
    others = (row_1_ref, row_2_ref, row_3_ref)
    for i, ref in enumerate((own_ref,) + others):
        n_ref[t ^ i] = ref[...]
    arrived = jnp.concatenate([ref[...] for ref in others], axis=0)
    arrived = jnp.dot(arrived, w_ref[...], preferred_element_type=jnp.float32)
    arrived = arrived.astype(jnp.bfloat16)
    qkv_ref[pl.ds(pl.multiple_of(t * pixels, 16), pixels), :] = own_qkv_ref[...]
    for i in range(1, frames):
        start = pl.multiple_of((t ^ i) * pixels, 16)
        qkv_ref[pl.ds(start, pixels), :] = arrived[(i - 1) * pixels : i * pixels]
    q, k, v = (
        [wide(qkv_ref, i, third, width, pixels) for i in range(frames)] for third in range(3)
    )
    slot = 0
    for i in range(frames):
        scores = head_sums([q[i] * k[u] for u in range(i + 1)], width)
        largest = scores[0]
        for s in scores[1:]:
            largest = jnp.maximum(largest, s)
        powers = [jnp.exp(s - largest) for s in scores]
        total = powers[0]
        for p in powers[1:]:
            total = total + p
        scale = 1.0 / total
        seen = None
        for u in range(i + 1):
            weights = (powers[u] * scale).astype(jnp.bfloat16)
            weights_ref[slot] = weights
            slot += 1
            term = weights.astype(jnp.float32) * v[u]
            seen = term if seen is None else seen + term
        attended_ref[i * pixels : (i + 1) * pixels, :] = seen.astype(jnp.bfloat16)


def backward_kernel(*refs):
    frames = 4
    piece_refs, out_refs, refs = refs[:4], refs[4:6], refs[6:]
    n_ref, qkv_ref, weights_ref, attended_ref, refs = *refs[:4], refs[4:]
    keep_refs, send_refs, (u_ref, g_ref, sums_ref, out_sums_ref) = refs[:2], refs[2:4], refs[4:]
    y, t, zp, zh, x, core = place()
    _, pixels, channels = n_ref.shape
    width = out_sums_ref.shape[0]
    first, second = out_refs[0][...], out_refs[1][...]
    out_w = jnp.where(
        core == 0,
        jnp.concatenate([first, second], axis=0),
        jnp.concatenate([second, first], axis=0),
    )
    pieces = jnp.concatenate([ref[...] for ref in piece_refs], axis=0)
    products = lax.dot_general(
        pieces, out_w, (((1,), (1,)), ((), ())), preferred_element_type=jnp.float32
    )
    for i, ref in enumerate(piece_refs):
        g_ref[t ^ i] = products[i * pixels : (i + 1) * pixels].astype(jnp.bfloat16)
        u_ref[t ^ i] = ref[...]
    normed = n_ref[...].reshape(frames * pixels, channels)
    upstream = u_ref[...].reshape(frames * pixels, channels)
    g = [g_ref[i].astype(jnp.float32) for i in range(frames)]
    q, k, v = (
        [wide(qkv_ref, i, third, width, pixels) for i in range(frames)] for third in range(3)
    )

    def over_rows(lhs, rhs):
        return lax.dot_general(
            lhs, rhs, (((0,), (0,)), ((), ())), preferred_element_type=jnp.float32
        )

    def plus(total, term):
        return term if total is None else total + term

    def keep_sum(m, pieces):
        pieces = [piece.astype(jnp.bfloat16) for piece in pieces]
        grad = over_rows(normed, jnp.concatenate(pieces, axis=0))
        for lane in range(0, width, 128):
            sums_ref[lane // 128, pl.ds(m, channels, stride=3), :] = grad[:, lane : lane + 128]

    out_sums_ref[...] = over_rows(attended_ref[...], upstream)
    firsts = [i * (i + 1) // 2 for i in range(frames)]
    dv = [None] * frames
    for i in range(frames):
        for u in range(i + 1):
            dv[u] = plus(dv[u], weights_ref[firsts[i] + u].astype(jnp.float32) * g[i])
    keep_sum(2, dv)
    dq, dk = [], [None] * frames
    for i in range(frames):
        dprob = head_sums([g[i] * v[u] for u in range(i + 1)], width)
        weights = [weights_ref[firsts[i] + u].astype(jnp.float32) for u in range(i + 1)]
        delta = weights[0] * dprob[0]
        for u in range(1, i + 1):
            delta = delta + weights[u] * dprob[u]
        grad_q = None
        for u in range(i + 1):
            ds = (weights[u] * (dprob[u] - delta)).astype(jnp.bfloat16).astype(jnp.float32)
            grad_q = plus(grad_q, ds * k[u])
            dk[u] = plus(dk[u], ds * q[i])
        dq.append(grad_q)
    keep_sum(0, dq)
    keep_sum(1, dk)

    block = channels // HEADS
    for slot in range(8):
        at_x, at_y, at_zp = slot >> 2, (slot >> 1) & 1, slot & 1
        places = ((at_x, at_y, at_zp), (at_y, at_x, at_zp))
        first_flip, second_flip, z_flip = x ^ at_x, y ^ at_y, zp ^ at_zp
        flips = [
            CROSSED[0] * pair[0] ^ CROSSED[1] * pair[1] ^ CROSSED[2] * z_flip
            for pair in ((first_flip, second_flip), (second_flip, first_flip))
        ]
        for side, path_refs in ((1 - core, send_refs), (core, keep_refs)):
            for low in range(2):
                rows_at = slice(low * block, (low + 1) * block)
                first = at_y * 16 + (2 * at_zp + low) * 4 + 2 * at_x
                for path, ref in enumerate(path_refs):
                    if first < 3 * HEADS:
                        owner = side ^ flips[path] ^ CROSSED[3] * (zh ^ low)
                        start = pl.multiple_of((first + owner) * block, block)
                        piece = sums_ref[path, pl.ds(start, block), :]
                    else:
                        start = pl.multiple_of((2 * at_x + (side ^ flips[path])) * block, block)
                        lanes_at = low * width + path * 128
                        piece = out_sums_ref[pl.ds(start, block), lanes_at : lanes_at + 128]
                    ref[(*places[path], rows_at)] = piece.astype(ref.dtype)


def join_kernel(first_ref, second_ref, got_ref, out_ref):
    y, _, zp, zh, _, _ = place()
    paths, rows, _ = got_ref.shape
    is_out = (y == 1) & (zp == 1)
    for path, total_ref in enumerate((first_ref, second_ref)):
        got = got_ref[path].astype(jnp.float32)
        for side in range(2):
            mine = total_ref[side * rows : (side + 1) * rows, :]
            joined = jnp.where(is_out | (zh == side), mine, got)
            out_ref[pl.ds(side * paths + path, rows, stride=2 * paths), :] = joined


def split_form(features, neighbours, conv_taps, norm_gain, qkv_weight, out_weight, cotangent):
    own = features[0, 0]
    pixels, channels = own.shape
    half, width, block = pixels // 2, channels // 2, channels // HEADS
    y, _, zp, zh, x, _ = place()
    narrow_type = jnp.bfloat16
    anywhere = pl.BlockSpec(memory_space=pl.ANY)
    in_vmem = pl.BlockSpec(memory_space=VMEM)
    piece = jax.ShapeDtypeStruct((half, channels), narrow_type)

    band = swap(own, "blk", 1)
    qkv_x = swap(qkv_weight, "fsdp", 2)
    out_x = swap(out_weight, "fsdp", 2)
    halves = cotangent[0, 0].reshape(2, half, channels)
    up_2 = swap(pick(halves, 1 - zp), "tm", 2)

    def conv(far):
        return pl.pallas_call(
            functools.partial(conv_kernel, far),
            out_shape=piece,
            in_specs=[in_vmem] * 5,
            out_specs=in_vmem,
            scratch_shapes=[pltpu.VMEM((pixels, neighbours.shape[1]), jnp.int32)],
            compiler_params=pltpu.CompilerParams(vmem_limit_bytes=16 << 20),
            name="conv_far" if far else "conv_near",
        )(neighbours.T, own, band, conv_taps, norm_gain.reshape(1, channels))

    n_other = conv(True)
    row_3 = swap(n_other, "tm", 3)
    row_2 = swap(n_other, "tm", 2)
    n_mine = conv(False)
    row_1 = swap(n_mine, "tm", 1)
    later, _ = lax.optimization_barrier((halves, n_other))
    up_mine = pick(later, zp)
    up_1 = swap(up_mine, "tm", 1)
    up_3 = swap(up_2, "tm", 1)
    qkv_c = swap(qkv_weight, "fsdp", 1)
    qkv_xc = swap(qkv_x, "fsdp", 1)
    out_rows = jnp.where(x == zh, out_weight, out_x)
    out_c = swap(out_rows, "fsdp", 1)

    full_qkv, own_qkv = pl.pallas_call(
        weights_kernel,
        out_shape=(
            jax.ShapeDtypeStruct((channels, 3 * width), narrow_type),
            jax.ShapeDtypeStruct((half, 3 * width), narrow_type),
        ),
        in_specs=[in_vmem] + [anywhere] * 4,
        out_specs=(in_vmem,) * 2,
        scratch_shapes=[pltpu.SemaphoreType.DMA((12,))],
        compiler_params=pltpu.CompilerParams(vmem_limit_bytes=16 << 20),
        name="weights",
    )(n_mine, qkv_weight, qkv_x, qkv_c, qkv_xc)
    qkv, weights, attended, normed = pl.pallas_call(
        forward_kernel,
        out_shape=(
            jax.ShapeDtypeStruct((4 * half, 3 * width), narrow_type),
            jax.ShapeDtypeStruct((10, half, width), narrow_type),
            jax.ShapeDtypeStruct((4 * half, width), narrow_type),
            jax.ShapeDtypeStruct((4, half, channels), narrow_type),
        ),
        in_specs=[in_vmem] * 6,
        out_specs=(in_vmem,) * 4,
        compiler_params=pltpu.CompilerParams(vmem_limit_bytes=24 << 20),
        name="forward",
    )(n_mine, row_1, row_2, row_3, own_qkv, full_qkv)
    *keep, send_0, send_1 = pl.pallas_call(
        backward_kernel,
        out_shape=(
            *(jax.ShapeDtypeStruct((2, 2, 2, 2 * block, 128), jnp.float32),) * 2,
            *(jax.ShapeDtypeStruct((2, 2, 2, 2 * block, 128), narrow_type),) * 2,
        ),
        in_specs=[in_vmem] * 10,
        out_specs=(in_vmem,) * 4,
        scratch_shapes=[
            pltpu.VMEM((4, half, channels), narrow_type),
            pltpu.VMEM((4, half, width), narrow_type),
            pltpu.VMEM((width // 128, 3 * channels, 128), jnp.float32),
            pltpu.VMEM((width, channels), jnp.float32),
        ],
        compiler_params=pltpu.CompilerParams(vmem_limit_bytes=28 << 20),
        name="backward",
    )(up_mine, up_1, up_2, up_3, out_rows, out_c, normed, qkv, weights, attended)

    def narrow(values):
        return values.astype(jnp.bfloat16)

    hops = (("fsdp", 2, x), ("blk", 1, y))
    paths = [
        total + swap(send, "fsdp", 1).astype(jnp.float32)
        for total, send in zip(keep, (send_0, send_1))
    ]
    for stage in range(2):
        for path in range(2):
            axis, mask, index = hops[path ^ stage]
            got = hop(narrow(pick(paths[path], 1 - index)), axis, mask, CROSSED[stage])
            paths[path] = pick(paths[path], index) + got.astype(jnp.float32)
    for path in range(2):
        got = hop(narrow(pick(paths[path], 1 - zp)), "tm", 2, CROSSED[2])
        paths[path] = pick(paths[path], zp) + got.astype(jnp.float32)
    far = jnp.stack([narrow(pick(total.reshape(2, block, 128), 1 - zh)) for total in paths])
    got = hop(far, "tm", 1, CROSSED[3])
    out = pl.pallas_call(
        join_kernel,
        out_shape=jax.ShapeDtypeStruct((block * channels // 128, 128), jnp.float32),
        in_specs=[in_vmem] * 3,
        out_specs=in_vmem,
        compiler_params=pltpu.CompilerParams(vmem_limit_bytes=4 << 20),
        name="join",
    )(*paths, got)
    return out.reshape(-1)


def with_halo(cells, sides, width):
    for axis, dim in sides:
        count = lax.axis_size(axis)
        ends = count - 1
        head = lax.slice_in_dim(cells, 0, width, axis=dim)
        tail = lax.slice_in_dim(cells, cells.shape[dim] - width, cells.shape[dim], axis=dim)
        cells = jnp.concatenate(
            [
                lax.ppermute(tail, axis, [(i, (i + 1) % count) for i in range(ends)]),
                cells,
                lax.ppermute(head, axis, [((i + 1) % count, i) for i in range(ends)]),
            ],
            axis=dim,
        )
    return cells


def halved(partial, axis, bit):
    count = lax.axis_size(axis)
    mine = (lax.axis_index(axis) >> bit) & 1
    keep = lax.dynamic_index_in_dim(partial, mine, 0, keepdims=False)
    send = lax.dynamic_index_in_dim(partial, 1 - mine, 0, keepdims=False)
    got = lax.ppermute(send.astype(jnp.bfloat16), axis, [(i, i ^ (1 << bit)) for i in range(count)])
    return keep + got.astype(jnp.float32)


def scattered_sum(summands):
    counts = [lax.axis_size(axis) for axis in ("blk", "tm", "fsdp")]
    bits = [count.bit_length() - 1 for count in counts]
    order = [("fsdp", bit) for bit in range(bits[2])]
    order += [("blk", bit) for bit in range(bits[0])]
    order += [("tm", bit) for bit in range(bits[1])]
    labels = [(axis, bit) for axis, many in zip(("blk", "tm", "fsdp"), bits) for bit in reversed(range(many))]
    partial = summands.reshape((2,) * len(labels) + (-1, 128))
    for axis, bit in order:
        place = labels.index((axis, bit))
        labels.pop(place)
        partial = halved(jnp.moveaxis(partial, place, 0), axis, bit)
    return partial.reshape(-1)


def rounded(values):
    return lax.optimization_barrier(values.astype(jnp.bfloat16)).astype(jnp.float32)


def attend_all(qkv_rows, grad_rows):
    frames, pixels, width = qkv_rows.shape
    channels = width // 3

    def split_heads(block):
        return block.reshape(frames, pixels, HEADS, channels // HEADS).astype(jnp.float32)

    queries = split_heads(qkv_rows[:, :, :channels])
    keys_all = split_heads(qkv_rows[:, :, channels : 2 * channels])
    values = split_heads(qkv_rows[:, :, 2 * channels :])
    grads = split_heads(grad_rows)
    scores = jnp.einsum("tpeh,upeh->petu", queries, keys_all) * 0.125
    causal = jnp.arange(frames)[:, None] >= jnp.arange(frames)[None, :]
    masked = jnp.where(causal, scores, -1e30)
    largest = jnp.max(masked, axis=-1, keepdims=True)
    totals = jnp.sum(jnp.exp(masked - largest), axis=-1, keepdims=True)
    log_total = largest + jnp.log(totals)
    weights = rounded(jnp.exp(masked - log_total))
    attended = jnp.einsum("petu,upeh->tpeh", weights, values)
    dprob = jnp.einsum("tpeh,upeh->petu", grads, values)
    delta = jnp.sum(weights * dprob, axis=-1, keepdims=True)
    dscore = rounded(weights * (dprob - delta) * 0.125)
    grad_query = jnp.einsum("petu,upeh->tpeh", dscore, keys_all)
    grad_key = jnp.einsum("petu,tpeh->upeh", dscore, queries)
    grad_value = jnp.einsum("petu,tpeh->upeh", weights, grads)
    joined = jnp.concatenate(
        [part.reshape(frames, pixels, channels) for part in (grad_query, grad_key, grad_value)],
        axis=-1,
    )
    return (
        attended.reshape(frames, pixels, channels).astype(jnp.bfloat16),
        joined.astype(jnp.bfloat16),
    )


def general_form(features, neighbours, conv_taps, norm_gain, qkv_weight, out_weight, cotangent):
    inputs = features[0, 0]
    upstream = cotangent[0, 0]
    pixels, channels = inputs.shape
    padded = with_halo(inputs, (("blk", 0),), HALO)
    first_pixel = lax.axis_index("blk") * pixels
    local_rows = neighbours - first_pixel + HALO
    inputs_f = inputs.astype(jnp.float32)
    spatial = conv_taps[0] * inputs_f
    for column in range(8):
        spatial = spatial + conv_taps[column + 1] * jnp.take(
            padded, local_rows[:, column], axis=0
        ).astype(jnp.float32)
    hidden_f = rounded(inputs_f + spatial)
    inverse = lax.rsqrt(jnp.mean(hidden_f * hidden_f, axis=-1, keepdims=True) + 1e-05)
    normed = (hidden_f * inverse * norm_gain).astype(jnp.bfloat16)
    full_qkv, full_out = (
        lax.all_gather(qkv_weight, "fsdp", axis=0, tiled=True),
        lax.all_gather(out_weight, "fsdp", axis=0, tiled=True),
    )
    att_grads = jnp.dot(upstream, full_out.T, preferred_element_type=jnp.float32).astype(
        jnp.bfloat16
    )
    swap_normed, swap_grads, swap_upstream = (
        lax.all_to_all(normed[None], "tm", split_axis=1, concat_axis=0, tiled=True),
        lax.all_to_all(att_grads[None], "tm", split_axis=1, concat_axis=0, tiled=True),
        lax.all_to_all(upstream[None], "tm", split_axis=1, concat_axis=0, tiled=True),
    )
    frames = swap_normed.shape[0]
    few_pixels = swap_normed.shape[1]
    flat_normed = swap_normed.reshape(-1, channels)
    qkv_rows = jnp.dot(flat_normed, full_qkv, preferred_element_type=jnp.float32).astype(
        jnp.bfloat16
    )
    qkv_rows = qkv_rows.reshape(frames, few_pixels, 3 * channels)
    attended_x, dqkv_x = attend_all(qkv_rows, swap_grads)
    grad_in = jnp.einsum(
        "pc,pd->cd",
        flat_normed,
        dqkv_x.reshape(-1, 3 * channels),
        preferred_element_type=jnp.float32,
    )
    grad_out = jnp.einsum(
        "pc,pd->cd",
        attended_x.reshape(-1, channels),
        swap_upstream.reshape(-1, channels),
        preferred_element_type=jnp.float32,
    )
    summands = jnp.concatenate([grad_in.reshape(-1), grad_out.reshape(-1)])
    return scattered_sum(summands)


def solution(mesh):
    sizes = mesh.shape

    def per_device(*arrays):
        pixels, channels = arrays[0].shape[-2:]
        devices = sizes["blk"] * sizes["tm"] * sizes["fsdp"]
        fits = (
            sizes["blk"] == 2
            and sizes["tm"] == sizes["fsdp"] == arrays[0].shape[0] * 4
            and devices == 4 * HEADS
            and pixels >= HALO
            and pixels % 32 == 0
            and channels == 64 * HEADS
        )
        if not fits:
            return general_form(*arrays)
        return split_form(*arrays)

    return jax.shard_map(
        per_device,
        mesh=mesh,
        in_specs=(
            P("fsdp", "tm", "blk", None),
            P("blk", None),
            P(),
            P(),
            P("fsdp", None),
            P("fsdp", None),
            P("fsdp", "tm", "blk", None),
        ),
        out_specs=P(("blk", "tm", "fsdp")),
        check_vma=False,
    )
```

```python
import functools

import jax
import jax.numpy as jnp
from jax import lax
from jax.experimental import pallas as pl
from jax.experimental.pallas import tpu as pltpu
from jax.sharding import PartitionSpec as P


HEADS = 8
HALO = 130
VMEM = pltpu.MemorySpace.VMEM

CROSSED = (1, 1, 1, 1)


def swap(values, axis, mask):
    return lax.ppermute(values, axis, [(i, i ^ mask) for i in range(lax.axis_size(axis))])


def hop(values, axis, mask, crossed):
    cores = lax.axis_size("fsdp")
    if axis == "fsdp":
        return swap(values, axis, mask ^ crossed)
    pairs = [(i, i ^ mask * cores ^ crossed) for i in range(lax.axis_size(axis) * cores)]
    return lax.ppermute(values, (axis, "fsdp"), pairs)


def pick(values, index, dim=0):
    return lax.dynamic_index_in_dim(values, index, dim, keepdims=False)


def place():
    t, f = lax.axis_index("tm"), lax.axis_index("fsdp")
    return lax.axis_index("blk"), t, t >> 1, t & 1, f >> 1, f & 1


def start_all(copies):
    for copy in copies:
        copy.start()


def conv_kernel(far, near_ref, own_ref, band_ref, taps_ref, out_ref, turned_ref):
    y, _, zp, _, _, _ = place()
    pixels, _ = own_ref.shape
    half = pixels // 2
    begin = pl.multiple_of((1 - zp if far else zp) * half, 16)
    turned_ref[...] = near_ref[...].T
    near = turned_ref[pl.ds(begin, half), :]
    neighbours = near.shape[1]
    local = near - y * pixels
    local = jnp.where(local < 0, local + 2 * pixels, local)
    slots = lax.broadcasted_iota(jnp.int32, (half, 2 * pixels), 1)
    chosen = jnp.concatenate(
        [
            jnp.where(local[:, k : k + 1] == slots, 1.0, 0.0).astype(jnp.bfloat16)
            for k in range(neighbours)
        ],
        axis=0,
    )
    table = jnp.concatenate([own_ref[...], band_ref[...]], axis=0)
    gathered = jnp.dot(chosen, table, preferred_element_type=jnp.float32)
    own = own_ref[pl.ds(begin, half), :].astype(jnp.float32)
    spatial = taps_ref[0:1, :] * own
    for k in range(neighbours):
        spatial = spatial + taps_ref[k + 1 : k + 2, :] * gathered[k * half : (k + 1) * half]
    hidden = (own + spatial).astype(jnp.bfloat16).astype(jnp.float32)
    inverse = lax.rsqrt(jnp.mean(hidden * hidden, axis=-1, keepdims=True) + 1e-05)
    out_ref[...] = (hidden * inverse * taps_ref[neighbours + 1 :, :]).astype(jnp.bfloat16)


def head_sums(products, width):
    depth = width * 2 // HEADS
    row_head = lax.broadcasted_iota(jnp.int32, (width, width), 0) // depth
    col_head = lax.broadcasted_iota(jnp.int32, (width, width), 1) // depth
    same = jnp.where(row_head == col_head, 0.125, 0.0).astype(jnp.bfloat16)
    pixels = products[0].shape[0]
    stacked = jnp.concatenate(products, axis=0)
    high = stacked.astype(jnp.bfloat16)
    low = (stacked - high.astype(jnp.float32)).astype(jnp.bfloat16)
    total = jnp.dot(high, same, preferred_element_type=jnp.float32)
    total = total + jnp.dot(low, same, preferred_element_type=jnp.float32)
    return [total[i * pixels : (i + 1) * pixels] for i in range(len(products))]


def wide(ref, frame, third, width, pixels):
    rows = ref[frame * pixels : (frame + 1) * pixels, third * width : (third + 1) * width]
    return rows.astype(jnp.float32)


def shard_rows(k, rows):
    _, _, _, _, x, core = place()
    f = (2 * x + core) ^ (2 * (k & 1) + (k >> 1))
    return pl.ds(pl.multiple_of(f * rows, 128), rows)


def weights_kernel(own_ref, *refs):
    shards, refs = refs[:4], refs[4:]
    w_ref, qkv_ref, sems = refs
    _, _, _, zh, _, _ = place()
    width = w_ref.shape[1] // 3
    rows = shards[0].shape[0]
    copies = []
    for k in range(4):
        for m in range(3):
            columns = pl.ds(pl.multiple_of((2 * m + zh) * width, 128), width)
            copies.append(
                pltpu.make_async_copy(
                    shards[k].at[:, columns],
                    w_ref.at[shard_rows(k, rows), pl.ds(m * width, width)],
                    sems.at[3 * k + m],
                )
            )
    start_all(copies)
    for copy in copies:
        copy.wait()
    qkv_ref[...] = jnp.dot(
        own_ref[...], w_ref[...], preferred_element_type=jnp.float32
    ).astype(jnp.bfloat16)


def forward_kernel(own_ref, row_1_ref, row_2_ref, row_3_ref, own_qkv_ref, w_ref, *refs):
    frames = 4
    qkv_ref, weights_ref, attended_ref, n_ref = refs
    _, t, _, _, _, _ = place()
    pixels, channels = own_ref.shape
    width = channels // 2
    others = (row_1_ref, row_2_ref, row_3_ref)
    for i, ref in enumerate((own_ref,) + others):
        n_ref[t ^ i] = ref[...]
    arrived = jnp.concatenate([ref[...] for ref in others], axis=0)
    arrived = jnp.dot(arrived, w_ref[...], preferred_element_type=jnp.float32)
    arrived = arrived.astype(jnp.bfloat16)
    qkv_ref[pl.ds(pl.multiple_of(t * pixels, 16), pixels), :] = own_qkv_ref[...]
    for i in range(1, frames):
        start = pl.multiple_of((t ^ i) * pixels, 16)
        qkv_ref[pl.ds(start, pixels), :] = arrived[(i - 1) * pixels : i * pixels]
    q, k, v = (
        [wide(qkv_ref, i, third, width, pixels) for i in range(frames)] for third in range(3)
    )
    slot = 0
    for i in range(frames):
        scores = head_sums([q[i] * k[u] for u in range(i + 1)], width)
        largest = scores[0]
        for s in scores[1:]:
            largest = jnp.maximum(largest, s)
        powers = [jnp.exp(s - largest) for s in scores]
        total = powers[0]
        for p in powers[1:]:
            total = total + p
        scale = 1.0 / total
        seen = None
        for u in range(i + 1):
            weights = (powers[u] * scale).astype(jnp.bfloat16)
            weights_ref[slot] = weights
            slot += 1
            term = weights.astype(jnp.float32) * v[u]
            seen = term if seen is None else seen + term
        attended_ref[i * pixels : (i + 1) * pixels, :] = seen.astype(jnp.bfloat16)


def backward_kernel(*refs):
    frames = 4
    piece_refs, out_refs, refs = refs[:4], refs[4:6], refs[6:]
    n_ref, qkv_ref, weights_ref, attended_ref, refs = *refs[:4], refs[4:]
    keep_refs, send_refs, (u_ref, g_ref, sums_ref, out_sums_ref) = refs[:2], refs[2:4], refs[4:]
    y, t, zp, zh, x, core = place()
    _, pixels, channels = n_ref.shape
    width = out_sums_ref.shape[0]
    first, second = out_refs[0][...], out_refs[1][...]
    out_w = jnp.where(
        core == 0,
        jnp.concatenate([first, second], axis=0),
        jnp.concatenate([second, first], axis=0),
    )
    pieces = jnp.concatenate([ref[...] for ref in piece_refs], axis=0)
    products = lax.dot_general(
        pieces, out_w, (((1,), (1,)), ((), ())), preferred_element_type=jnp.float32
    )
    for i, ref in enumerate(piece_refs):
        g_ref[t ^ i] = products[i * pixels : (i + 1) * pixels].astype(jnp.bfloat16)
        u_ref[t ^ i] = ref[...]
    normed = n_ref[...].reshape(frames * pixels, channels)
    upstream = u_ref[...].reshape(frames * pixels, channels)
    g = [g_ref[i].astype(jnp.float32) for i in range(frames)]
    q, k, v = (
        [wide(qkv_ref, i, third, width, pixels) for i in range(frames)] for third in range(3)
    )

    def over_rows(lhs, rhs):
        return lax.dot_general(
            lhs, rhs, (((0,), (0,)), ((), ())), preferred_element_type=jnp.float32
        )

    def plus(total, term):
        return term if total is None else total + term

    def keep_sum(m, pieces):
        pieces = [piece.astype(jnp.bfloat16) for piece in pieces]
        grad = over_rows(normed, jnp.concatenate(pieces, axis=0))
        for lane in range(0, width, 128):
            sums_ref[lane // 128, pl.ds(m, channels, stride=3), :] = grad[:, lane : lane + 128]

    out_sums_ref[...] = over_rows(attended_ref[...], upstream)
    firsts = [i * (i + 1) // 2 for i in range(frames)]
    dv = [None] * frames
    for i in range(frames):
        for u in range(i + 1):
            dv[u] = plus(dv[u], weights_ref[firsts[i] + u].astype(jnp.float32) * g[i])
    keep_sum(2, dv)
    dq, dk = [], [None] * frames
    for i in range(frames):
        dprob = head_sums([g[i] * v[u] for u in range(i + 1)], width)
        weights = [weights_ref[firsts[i] + u].astype(jnp.float32) for u in range(i + 1)]
        delta = weights[0] * dprob[0]
        for u in range(1, i + 1):
            delta = delta + weights[u] * dprob[u]
        grad_q = None
        for u in range(i + 1):
            ds = (weights[u] * (dprob[u] - delta)).astype(jnp.bfloat16).astype(jnp.float32)
            grad_q = plus(grad_q, ds * k[u])
            dk[u] = plus(dk[u], ds * q[i])
        dq.append(grad_q)
    keep_sum(0, dq)
    keep_sum(1, dk)

    block = channels // HEADS
    for slot in range(8):
        at_x, at_y, at_zp = slot >> 2, (slot >> 1) & 1, slot & 1
        places = ((at_x, at_y, at_zp), (at_y, at_x, at_zp))
        first_flip, second_flip, z_flip = x ^ at_x, y ^ at_y, zp ^ at_zp
        flips = [
            CROSSED[0] * pair[0] ^ CROSSED[1] * pair[1] ^ CROSSED[2] * z_flip
            for pair in ((first_flip, second_flip), (second_flip, first_flip))
        ]
        for side, path_refs in ((1 - core, send_refs), (core, keep_refs)):
            for low in range(2):
                rows_at = slice(low * block, (low + 1) * block)
                first = at_y * 16 + (2 * at_zp + low) * 4 + 2 * at_x
                for path, ref in enumerate(path_refs):
                    if first < 3 * HEADS:
                        owner = side ^ flips[path] ^ CROSSED[3] * (zh ^ low)
                        start = pl.multiple_of((first + owner) * block, block)
                        piece = sums_ref[path, pl.ds(start, block), :]
                    else:
                        start = pl.multiple_of((2 * at_x + (side ^ flips[path])) * block, block)
                        lanes_at = low * width + path * 128
                        piece = out_sums_ref[pl.ds(start, block), lanes_at : lanes_at + 128]
                    ref[(*places[path], rows_at)] = piece.astype(ref.dtype)


def join_kernel(first_ref, second_ref, got_first_ref, got_second_ref, out_ref):
    y, _, zp, zh, _, _ = place()
    rows, _ = got_first_ref.shape
    got_refs = (got_first_ref, got_second_ref)
    paths = len(got_refs)
    is_out = (y == 1) & (zp == 1)
    for path, total_ref in enumerate((first_ref, second_ref)):
        got = got_refs[path][...].astype(jnp.float32)
        for side in range(2):
            mine = total_ref[side * rows : (side + 1) * rows, :]
            joined = jnp.where(is_out | (zh == side), mine, got)
            out_ref[pl.ds(side * paths + path, rows, stride=2 * paths), :] = joined


def split_form(features, neighbours, conv_taps, norm_gain, qkv_weight, out_weight, cotangent):
    own = features[0, 0]
    pixels, channels = own.shape
    half, width, block = pixels // 2, channels // 2, channels // HEADS
    y, _, zp, zh, x, _ = place()
    narrow_type = jnp.bfloat16
    anywhere = pl.BlockSpec(memory_space=pl.ANY)
    in_vmem = pl.BlockSpec(memory_space=VMEM)
    piece = jax.ShapeDtypeStruct((half, channels), narrow_type)

    band = swap(own, "blk", 1)
    qkv_x = swap(qkv_weight, "fsdp", 2)
    out_x = swap(out_weight, "fsdp", 2)
    halves = cotangent[0, 0].reshape(2, half, channels)
    up_2 = swap(pick(halves, 1 - zp), "tm", 2)

    scales = jnp.concatenate([conv_taps, norm_gain.reshape(1, channels)], axis=0)

    def conv(far):
        return pl.pallas_call(
            functools.partial(conv_kernel, far),
            out_shape=piece,
            in_specs=[in_vmem] * 4,
            out_specs=in_vmem,
            scratch_shapes=[pltpu.VMEM((pixels, neighbours.shape[1]), jnp.int32)],
            compiler_params=pltpu.CompilerParams(vmem_limit_bytes=16 << 20),
            name="conv_far" if far else "conv_near",
        )(neighbours.T, own, band, scales)

    n_other = conv(True)
    row_3 = swap(n_other, "tm", 3)
    row_2 = swap(n_other, "tm", 2)
    n_mine = conv(False)
    row_1 = swap(n_mine, "tm", 1)
    later, _ = lax.optimization_barrier((halves, n_other))
    up_mine = pick(later, zp)
    up_1 = swap(up_mine, "tm", 1)
    up_3 = swap(up_2, "tm", 1)
    qkv_c = swap(qkv_weight, "fsdp", 1)
    qkv_xc = swap(qkv_x, "fsdp", 1)
    out_rows = jnp.where(x == zh, out_weight, out_x)
    out_c = swap(out_rows, "fsdp", 1)

    full_qkv, own_qkv = pl.pallas_call(
        weights_kernel,
        out_shape=(
            jax.ShapeDtypeStruct((channels, 3 * width), narrow_type),
            jax.ShapeDtypeStruct((half, 3 * width), narrow_type),
        ),
        in_specs=[in_vmem] + [anywhere] * 4,
        out_specs=(in_vmem,) * 2,
        scratch_shapes=[pltpu.SemaphoreType.DMA((12,))],
        compiler_params=pltpu.CompilerParams(vmem_limit_bytes=16 << 20),
        name="weights",
    )(n_mine, qkv_weight, qkv_x, qkv_c, qkv_xc)
    qkv, weights, attended, normed = pl.pallas_call(
        forward_kernel,
        out_shape=(
            jax.ShapeDtypeStruct((4 * half, 3 * width), narrow_type),
            jax.ShapeDtypeStruct((10, half, width), narrow_type),
            jax.ShapeDtypeStruct((4 * half, width), narrow_type),
            jax.ShapeDtypeStruct((4, half, channels), narrow_type),
        ),
        in_specs=[in_vmem] * 6,
        out_specs=(in_vmem,) * 4,
        compiler_params=pltpu.CompilerParams(vmem_limit_bytes=24 << 20),
        name="forward",
    )(n_mine, row_1, row_2, row_3, own_qkv, full_qkv)
    *keep, send_0, send_1 = pl.pallas_call(
        backward_kernel,
        out_shape=(
            *(jax.ShapeDtypeStruct((2, 2, 2, 2 * block, 128), jnp.float32),) * 2,
            *(jax.ShapeDtypeStruct((2, 2, 2, 2 * block, 128), narrow_type),) * 2,
        ),
        in_specs=[in_vmem] * 10,
        out_specs=(in_vmem,) * 4,
        scratch_shapes=[
            pltpu.VMEM((4, half, channels), narrow_type),
            pltpu.VMEM((4, half, width), narrow_type),
            pltpu.VMEM((width // 128, 3 * channels, 128), jnp.float32),
            pltpu.VMEM((width, channels), jnp.float32),
        ],
        compiler_params=pltpu.CompilerParams(vmem_limit_bytes=28 << 20),
        name="backward",
    )(up_mine, up_1, up_2, up_3, out_rows, out_c, normed, qkv, weights, attended)

    def narrow(values):
        return values.astype(jnp.bfloat16)

    hops = (("fsdp", 2, x), ("blk", 1, y))
    paths = [
        total + swap(send, "fsdp", 1).astype(jnp.float32)
        for total, send in zip(keep, (send_0, send_1))
    ]
    for stage in range(2):
        for path in range(2):
            axis, mask, index = hops[path ^ stage]
            got = hop(narrow(pick(paths[path], 1 - index)), axis, mask, CROSSED[stage])
            paths[path] = pick(paths[path], index) + got.astype(jnp.float32)
    for path in range(2):
        got = hop(narrow(pick(paths[path], 1 - zp)), "tm", 2, CROSSED[2])
        paths[path] = pick(paths[path], zp) + got.astype(jnp.float32)
    got = [
        hop(narrow(pick(total.reshape(2, block, 128), 1 - zh)), "tm", 1, CROSSED[3])
        for total in paths
    ]
    out = pl.pallas_call(
        join_kernel,
        out_shape=jax.ShapeDtypeStruct((block * channels // 128, 128), jnp.float32),
        in_specs=[in_vmem] * 4,
        out_specs=in_vmem,
        compiler_params=pltpu.CompilerParams(vmem_limit_bytes=4 << 20),
        name="join",
    )(*paths, *got)
    return out.reshape(-1)


def with_halo(cells, sides, width):
    for axis, dim in sides:
        count = lax.axis_size(axis)
        ends = count - 1
        head = lax.slice_in_dim(cells, 0, width, axis=dim)
        tail = lax.slice_in_dim(cells, cells.shape[dim] - width, cells.shape[dim], axis=dim)
        cells = jnp.concatenate(
            [
                lax.ppermute(tail, axis, [(i, (i + 1) % count) for i in range(ends)]),
                cells,
                lax.ppermute(head, axis, [((i + 1) % count, i) for i in range(ends)]),
            ],
            axis=dim,
        )
    return cells


def halved(partial, axis, bit):
    count = lax.axis_size(axis)
    mine = (lax.axis_index(axis) >> bit) & 1
    keep = lax.dynamic_index_in_dim(partial, mine, 0, keepdims=False)
    send = lax.dynamic_index_in_dim(partial, 1 - mine, 0, keepdims=False)
    got = lax.ppermute(send.astype(jnp.bfloat16), axis, [(i, i ^ (1 << bit)) for i in range(count)])
    return keep + got.astype(jnp.float32)


def scattered_sum(summands):
    counts = [lax.axis_size(axis) for axis in ("blk", "tm", "fsdp")]
    bits = [count.bit_length() - 1 for count in counts]
    order = [("fsdp", bit) for bit in range(bits[2])]
    order += [("blk", bit) for bit in range(bits[0])]
    order += [("tm", bit) for bit in range(bits[1])]
    labels = [(axis, bit) for axis, many in zip(("blk", "tm", "fsdp"), bits) for bit in reversed(range(many))]
    partial = summands.reshape((2,) * len(labels) + (-1, 128))
    for axis, bit in order:
        place = labels.index((axis, bit))
        labels.pop(place)
        partial = halved(jnp.moveaxis(partial, place, 0), axis, bit)
    return partial.reshape(-1)


def rounded(values):
    return lax.optimization_barrier(values.astype(jnp.bfloat16)).astype(jnp.float32)


def attend_all(qkv_rows, grad_rows):
    frames, pixels, width = qkv_rows.shape
    channels = width // 3

    def split_heads(block):
        return block.reshape(frames, pixels, HEADS, channels // HEADS).astype(jnp.float32)

    queries = split_heads(qkv_rows[:, :, :channels])
    keys_all = split_heads(qkv_rows[:, :, channels : 2 * channels])
    values = split_heads(qkv_rows[:, :, 2 * channels :])
    grads = split_heads(grad_rows)
    scores = jnp.einsum("tpeh,upeh->petu", queries, keys_all) * 0.125
    causal = jnp.arange(frames)[:, None] >= jnp.arange(frames)[None, :]
    masked = jnp.where(causal, scores, -1e30)
    largest = jnp.max(masked, axis=-1, keepdims=True)
    totals = jnp.sum(jnp.exp(masked - largest), axis=-1, keepdims=True)
    log_total = largest + jnp.log(totals)
    weights = rounded(jnp.exp(masked - log_total))
    attended = jnp.einsum("petu,upeh->tpeh", weights, values)
    dprob = jnp.einsum("tpeh,upeh->petu", grads, values)
    delta = jnp.sum(weights * dprob, axis=-1, keepdims=True)
    dscore = rounded(weights * (dprob - delta) * 0.125)
    grad_query = jnp.einsum("petu,upeh->tpeh", dscore, keys_all)
    grad_key = jnp.einsum("petu,tpeh->upeh", dscore, queries)
    grad_value = jnp.einsum("petu,tpeh->upeh", weights, grads)
    joined = jnp.concatenate(
        [part.reshape(frames, pixels, channels) for part in (grad_query, grad_key, grad_value)],
        axis=-1,
    )
    return (
        attended.reshape(frames, pixels, channels).astype(jnp.bfloat16),
        joined.astype(jnp.bfloat16),
    )


def general_form(features, neighbours, conv_taps, norm_gain, qkv_weight, out_weight, cotangent):
    inputs = features[0, 0]
    upstream = cotangent[0, 0]
    pixels, channels = inputs.shape
    padded = with_halo(inputs, (("blk", 0),), HALO)
    first_pixel = lax.axis_index("blk") * pixels
    local_rows = neighbours - first_pixel + HALO
    inputs_f = inputs.astype(jnp.float32)
    spatial = conv_taps[0] * inputs_f
    for column in range(8):
        spatial = spatial + conv_taps[column + 1] * jnp.take(
            padded, local_rows[:, column], axis=0
        ).astype(jnp.float32)
    hidden_f = rounded(inputs_f + spatial)
    inverse = lax.rsqrt(jnp.mean(hidden_f * hidden_f, axis=-1, keepdims=True) + 1e-05)
    normed = (hidden_f * inverse * norm_gain).astype(jnp.bfloat16)
    full_qkv, full_out = (
        lax.all_gather(qkv_weight, "fsdp", axis=0, tiled=True),
        lax.all_gather(out_weight, "fsdp", axis=0, tiled=True),
    )
    att_grads = jnp.dot(upstream, full_out.T, preferred_element_type=jnp.float32).astype(
        jnp.bfloat16
    )
    swap_normed, swap_grads, swap_upstream = (
        lax.all_to_all(normed[None], "tm", split_axis=1, concat_axis=0, tiled=True),
        lax.all_to_all(att_grads[None], "tm", split_axis=1, concat_axis=0, tiled=True),
        lax.all_to_all(upstream[None], "tm", split_axis=1, concat_axis=0, tiled=True),
    )
    frames = swap_normed.shape[0]
    few_pixels = swap_normed.shape[1]
    flat_normed = swap_normed.reshape(-1, channels)
    qkv_rows = jnp.dot(flat_normed, full_qkv, preferred_element_type=jnp.float32).astype(
        jnp.bfloat16
    )
    qkv_rows = qkv_rows.reshape(frames, few_pixels, 3 * channels)
    attended_x, dqkv_x = attend_all(qkv_rows, swap_grads)
    grad_in = jnp.einsum(
        "pc,pd->cd",
        flat_normed,
        dqkv_x.reshape(-1, 3 * channels),
        preferred_element_type=jnp.float32,
    )
    grad_out = jnp.einsum(
        "pc,pd->cd",
        attended_x.reshape(-1, channels),
        swap_upstream.reshape(-1, channels),
        preferred_element_type=jnp.float32,
    )
    summands = jnp.concatenate([grad_in.reshape(-1), grad_out.reshape(-1)])
    return scattered_sum(summands)


def solution(mesh):
    sizes = mesh.shape

    def per_device(*arrays):
        pixels, channels = arrays[0].shape[-2:]
        devices = sizes["blk"] * sizes["tm"] * sizes["fsdp"]
        fits = (
            sizes["blk"] == 2
            and sizes["tm"] == sizes["fsdp"] == arrays[0].shape[0] * 4
            and devices == 4 * HEADS
            and pixels >= HALO
            and pixels % 32 == 0
            and channels == 64 * HEADS
        )
        if not fits:
            return general_form(*arrays)
        return split_form(*arrays)

    return jax.shard_map(
        per_device,
        mesh=mesh,
        in_specs=(
            P("fsdp", "tm", "blk", None),
            P("blk", None),
            P(),
            P(),
            P("fsdp", None),
            P("fsdp", None),
            P("fsdp", "tm", "blk", None),
        ),
        out_specs=P(("blk", "tm", "fsdp")),
        check_vma=False,
    )
```
